32 devices in a mesh: seq: 8 (over z, x), fsdp: 4 (over y, core).
Axes of the slice: x: 2, y: 2, z: 4, core: 2. Of those that a mesh axis runs over, the one named last changes fastest.
Arguments:
- tokens: bfloat16 [4096, 1024], P(('seq', 'fsdp')), may hold values from -6 to 6
- cotangent: bfloat16 [4096, 1024], P(('seq', 'fsdp')), may hold values from -6 to 6
- seq_lengths: int32 [4], replicated, may hold values from 1 to 2048, 4096 in all
- w_qkv: bfloat16 [1024, 3072], P(('seq', 'fsdp')), may hold values from -0.1875 to 0.1875
- w_attn_out: bfloat16 [1024, 1024], P(('seq', 'fsdp')), may hold values from -0.75 to 0.75
- w_in: bfloat16 [1024, 5248], P(('seq', 'fsdp')), may hold values from -0.1875 to 0.1875
- w_mlp_out: bfloat16 [1024, 2624], P(('seq', 'fsdp')), may hold values from -0.125 to 0.125
- gain_attn: bfloat16 [1024], P(('seq', 'fsdp')), may hold values from 0.5 to 1.5
- gain_mlp: bfloat16 [1024], P(('seq', 'fsdp')), may hold values from 0.5 to 1.5
Outputs:
- output: bfloat16 [4096, 1024], P(('seq', 'fsdp'))
- input_grad: float32 [4096, 1024], P(('seq', 'fsdp'))
- grad_w_qkv: float32 [1024, 3072], P(('seq', 'fsdp'))
- grad_w_attn_out: float32 [1024, 1024], P(('seq', 'fsdp'))
- grad_w_in: float32 [1024, 5248], P(('seq', 'fsdp'))
- grad_w_mlp_out: float32 [1024, 2624], P(('seq', 'fsdp'))
- grad_gain_attn: float32 [1024], P(('seq', 'fsdp'))
- grad_gain_mlp: float32 [1024], P(('seq', 'fsdp'))
The draws below stay inside these ranges and needn't reach their ends.
Inputs may be any that keep to these rules, and one draw needn't show every extreme that they name: `seq_lengths`: 4 lengths that add up to 4096; the longest is exactly 2048.
All inputs are finite; a program needn't handle non-finite values.
Results may differ from the reference program's by a relative error of at most 0.015.
Values may be sent and summed in bfloat16 or wider, within the bound.
No kernel may reach another device: no remote copies, remote signals or barrier semaphores. Data moves between devices by JAX's collectives and lax.ppermute only.
A program may use at most 256 MiB of HBM per device.

```python
import math
import jax
import jax.numpy as jnp
import numpy as np
from jax import lax

D = 1024
HEADS = 16
HDIM = 64
FF = 2624
HALF = 64
TOKENS = 4096
MAXLEN = 2048
SEQS = 4


def with_spikes(values, own_key, source, target, shards_of, factor):
    owner, partner = [(jnp.arange(values.shape[dim]) // (values.shape[dim] // shards_of)).reshape([-1 if axis == dim else 1 for axis in range(values.ndim)]) for dim in (source, target)]
    chosen = jax.random.permutation(own_key, shards_of)[partner]
    strong = (owner == chosen) | (owner == (partner + shards_of // 2) % shards_of)
    return jnp.where(strong, factor * values, values)


def block_scale(key, dims, shards, smallest, largest):
    def one(dim, shards_of):
        heights = jax.random.uniform(jax.random.fold_in(jax.random.fold_in(key, 6), dim), (shards_of,), jnp.float32, smallest / len(shards), largest / len(shards))
        return jnp.repeat(jnp.exp(heights), dims[dim] // shards_of).reshape((-1,) + (1,) * (len(dims) - dim - 1))

    loudness = one(*shards[0])
    for cut in shards[1:]:
        loudness = loudness * one(*cut)
    return loudness


def split_up(amount, total, reach, lean):
    loads = [(1 << 20) // math.isqrt(grade ** lean) + 1 for grade in range(2, amount + 1)]
    spare, counts = total - reach - (amount - 1), [1] * (amount - 1)
    while spare > 0:
        free = [i for i in range(amount - 1) if counts[i] < reach]
        whole, remaining = sum([loads[i] for i in free]), spare
        for i in free:
            more = min(reach - counts[i], max(1, remaining * loads[i] // whole), spare)
            counts[i] = counts[i] + more
            spare = spare - more
    return np.array([reach] + counts)


def ragged_sizes(rng, amount, total, reach, skew):
    if amount == 2:
        one = jax.random.randint(rng, (), max(1, total - reach), min(reach, total - 1) + 1)
        return jnp.stack([one, total - one])
    lengths = jnp.asarray(split_up(amount, total, reach, skew), jnp.int32)
    pairs = (amount - 1) // 2
    giver, sink = lengths[1:1 + 2 * pairs:2], lengths[2:2 + 2 * pairs:2]
    room = jnp.minimum(giver - 1, reach - sink)
    passed = jax.random.randint(jax.random.fold_in(rng, 1), (pairs,), 0, 1 << 20) % (room + 1)
    lengths = lengths.at[1:1 + 2 * pairs:2].set(giver - passed).at[2:2 + 2 * pairs:2].set(sink + passed)
    return lengths[jax.random.permutation(jax.random.fold_in(rng, 2), amount)]


def centred(key, shape, width, limit, cuts=(), held_as=jnp.bfloat16):
    values = width * jax.random.normal(key, shape, jnp.float32)
    if cuts:
        values = values * block_scale(key, shape, cuts, -0.22, 0.18)
    return jnp.clip(values, -limit, limit).astype(held_as)


def bell_draw_with(own_key, shape, deviation, reach, pieces, heavy, kind=jnp.bfloat16):
    entries = deviation * jax.random.normal(own_key, shape, jnp.float32)
    if pieces:
        entries = entries * block_scale(own_key, shape, pieces, -0.22, 0.18)
    return jnp.clip(with_spikes(entries, jax.random.fold_in(own_key, 3), *heavy), -reach, reach).astype(kind)


def setup_inputs(seed: int = 0) -> dict:
    splits = jax.random.split(jax.random.key(seed), 10)
    return {
        "tokens": centred(splits[0], (TOKENS, D), 1.0, 6.0, ((0, 32),)),
        "cotangent": bell_draw_with(splits[1], (TOKENS, D), 1.0, 6.0, ((0, 32),), (0, 1, 32, 2.75)),
        "seq_lengths": ragged_sizes(splits[2], SEQS, TOKENS, MAXLEN, 2).astype(jnp.int32),
        "w_qkv": centred(splits[3], (D, 3 * D), D ** -0.5, 0.1875, ((0, 32),)),
        "w_attn_out": centred(splits[4], (D, D), (D // 16) ** -0.5, 0.75, ((0, 32),)),
        "w_in": centred(splits[5], (D, 2 * FF), D ** -0.5, 0.1875, ((0, 32),)),
        "w_mlp_out": centred(splits[6], (D, FF), FF ** -0.5, 0.125, ((0, 32),)),
        "gain_attn": jnp.clip(1.0 + 0.1 * jax.random.normal(splits[7], (D,), jnp.float32), 0.5, 1.5).astype(jnp.bfloat16),
        "gain_mlp": jnp.clip(1.0 + 0.1 * jax.random.normal(splits[8], (D,), jnp.float32), 0.5, 1.5).astype(jnp.bfloat16),
    }


epsilon = 1e-05
highest = lax.Precision.HIGHEST

@jax.custom_vjp
def low(v):
    return lax.optimization_barrier(v.astype(jnp.bfloat16)).astype(jnp.float32)

@jax.custom_vjp
def low_back(v):
    return v

def low_keep(v):
    return (low(v), None)

def low_pass(kept, grad):
    return (grad,)

def back_keep(v):
    return (v, None)

def back_low(kept, grad):
    return (low(grad),)
low.defvjp(low_keep, low_pass)
low_back.defvjp(back_keep, back_low)

def normalize(values):
    average = lax.optimization_barrier(jnp.mean(values, axis=-1, keepdims=True))
    centered = values - average
    variance = lax.optimization_barrier(jnp.mean(centered * centered, axis=-1, keepdims=True))
    return centered * lax.rsqrt(variance + epsilon)

def rotate(flat, cosine, sine):
    split = flat.reshape(flat.shape[0], HEADS, HDIM)
    half_dim = HDIM // 2
    turned = jnp.concatenate([-split[..., half_dim:], split[..., :half_dim]], axis=-1)
    return (split * cosine[:, None, :] + turned * sine[:, None, :]).reshape(flat.shape[0], HEADS * HDIM)

def angles(position):
    freqs = 10000.0 ** (-(jnp.arange(HDIM // 2, dtype=jnp.float32) * 2.0) / HDIM)
    freqs = jnp.concatenate([freqs, freqs])
    turns = position.astype(jnp.float32)[:, None] * freqs[None, :]
    return (jnp.cos(turns), jnp.sin(turns))

def place(index, seq_lengths):
    seg_ends = jnp.cumsum(seq_lengths).astype(jnp.int32)
    seg_starts = (seg_ends - seq_lengths).astype(jnp.int32)
    segment = lax.optimization_barrier(jnp.sum((index[:, None] >= seg_ends[None, :]).astype(jnp.int32), axis=1)).astype(jnp.int32)
    seg_ids = jnp.arange(seq_lengths.shape[0], dtype=jnp.int32)
    begins = lax.optimization_barrier(jnp.sum(jnp.where(segment[:, None] == seg_ids[None, :], seg_starts[None, :], 0), axis=1)).astype(jnp.int32)
    return (segment, (index - begins).astype(jnp.int32))

def attend(query, keys, values, token_seg, key_seg, key_valid):
    row_count = query.shape[0]
    blocks = row_count // 512
    scale = HDIM ** (-0.5)
    q_blocks = query.reshape(blocks, 512, HEADS, HDIM)
    padded_k = jnp.pad(keys, ((HALF, HALF), (0, 0))).reshape(-1, HEADS, HDIM)
    padded_v = jnp.pad(values, ((HALF, HALF), (0, 0))).reshape(-1, HEADS, HDIM)
    span = 512 + 2 * HALF
    offset = jnp.arange(512, dtype=jnp.int32)[:, None] + HALF - jnp.arange(span, dtype=jnp.int32)[None, :]

    def one_block(inputs):
        block_id, q_block = inputs
        start_row = (block_id * 512).astype(jnp.int32)
        k_block = lax.dynamic_slice_in_dim(padded_k, start_row, span, 0)
        v_block = lax.dynamic_slice_in_dim(padded_v, start_row, span, 0)
        q_seg = lax.dynamic_slice_in_dim(token_seg, start_row, 512, 0)
        k_seg = lax.dynamic_slice_in_dim(key_seg, start_row, span, 0)
        k_valid = lax.dynamic_slice_in_dim(key_valid, start_row, span, 0)
        allowed = (q_seg[:, None] == k_seg[None, :]) & (jnp.abs(offset) <= HALF) & k_valid[None, :]
        scores = low_back(jnp.einsum('thd,shd->hts', q_block, k_block, precision=highest) * scale)
        scores = jnp.where(allowed[None], scores, -1e+30)
        peak_score = lax.optimization_barrier(jnp.max(scores, axis=-1, keepdims=True))
        exponent = jnp.exp(scores - peak_score)
        probability = exponent / lax.optimization_barrier(jnp.sum(exponent, axis=-1, keepdims=True))
        return jnp.einsum('hts,shd->thd', low(probability), v_block, precision=highest)
    results = lax.map(jax.checkpoint(one_block), (jnp.arange(blocks, dtype=jnp.int32), q_blocks))
    return results.reshape(row_count, HEADS * HDIM)

def layer(tokens, w_qkv, w_attn_out, w_in, w_mlp_out, gain_attn, gain_mlp, cosine, sine, token_seg, key_seg, key_valid):
    hidden = low(normalize(tokens) * gain_attn)
    packed = low_back(jnp.dot(hidden, w_qkv, precision=highest))
    query = low(rotate(packed[:, :D], cosine, sine))
    keys = low(rotate(packed[:, D:2 * D], cosine, sine))
    values = low(packed[:, 2 * D:])
    attended = low(low_back(attend(query, keys, values, token_seg, key_seg, key_valid)))
    middle = tokens + low_back(jnp.dot(attended, w_attn_out, precision=highest))
    lifted = low(normalize(middle) * gain_mlp)
    both = low_back(jnp.dot(lifted, w_in, precision=highest))
    mixed = low(jax.nn.gelu(both[:, :FF], approximate=False) * both[:, FF:])
    return middle + low_back(jnp.dot(mixed, w_mlp_out.T, precision=highest))

def reference(tokens, cotangent, seq_lengths, w_qkv, w_attn_out, w_in, w_mlp_out, gain_attn, gain_mlp):
    index = jnp.arange(TOKENS, dtype=jnp.int32)
    token_seg, position = place(index, seq_lengths)
    key_index = (jnp.arange(TOKENS + 2 * HALF, dtype=jnp.int32) - HALF).astype(jnp.int32)
    key_seg, unused = place(jnp.clip(key_index, 0, TOKENS - 1).astype(jnp.int32), seq_lengths)
    key_valid = (key_index >= 0) & (key_index < TOKENS)
    cosine, sine = angles(position)

    def forward(x_in, qkv_in, attn_in, lift_in, mlp_in, gain_one, gain_two):
        return layer(x_in, qkv_in, attn_in, lift_in, mlp_in, gain_one, gain_two, cosine, sine, token_seg, key_seg, key_valid)
    output, pull_back = jax.vjp(forward, tokens.astype(jnp.float32), w_qkv.astype(jnp.float32), w_attn_out.astype(jnp.float32), w_in.astype(jnp.float32), w_mlp_out.astype(jnp.float32), gain_attn.astype(jnp.float32), gain_mlp.astype(jnp.float32))
    grads = pull_back(cotangent.astype(jnp.float32))
    return (output.astype(jnp.bfloat16), grads[0], grads[1], grads[2], grads[3], grads[4], grads[5], grads[6])
```

```python
import jax
import jax.numpy as jnp
from jax import lax
from jax.experimental import pallas as pl
from jax.experimental.pallas import tpu as pltpu
from jax.sharding import Mesh, PartitionSpec as P

D = 1024
HEADS = 16
HDIM = 64
FF = 2624
HALF = 64
OWN_HEADS = HEADS // 2
OWN = OWN_HEADS * HDIM
OWN_FF = FF // 2

EPSILON = 1e-05
MASKED = -1e30
ALL = ("seq", "fy", "core")
CHIPS = ("seq", "fy")
BF16 = jnp.bfloat16
F32 = jnp.float32


def my_bit(step):
    axis, bit = step
    return (lax.axis_index(axis) >> bit) & 1


def dim_of(step):
    axis, bit = step
    seq_bits = lax.axis_size("seq").bit_length() - 1
    return seq_bits if axis == "fy" else seq_bits - 1 - bit


def relayed(step):
    return step == ("seq", 2) and lax.axis_size("seq") == 8


def swap(cells, step):
    axis, bit = step
    count = lax.axis_size(axis)
    return lax.ppermute(cells, axis, [(i, i ^ (1 << bit)) for i in range(count)])


MIDDLE = [(2, 4), (3, 5), (4, 2), (5, 3)]
OUTWARD = [(2, 0), (3, 1), (4, 6), (5, 7)]
INWARD = [(0, 2), (1, 3), (6, 4), (7, 5)]


def gather_step(cells, step):
    if relayed(step):
        crossed = lax.ppermute(cells, "seq", MIDDLE)
        handed = lax.ppermute(crossed, "seq", OUTWARD)
        inner = my_bit(("seq", 1)) != my_bit(("seq", 2))
        got = jnp.where(inner, crossed, handed)
    else:
        got = swap(cells, step)
    high = my_bit(step) == 1
    return jnp.concatenate(
        [jnp.where(high, got, cells), jnp.where(high, cells, got)], axis=dim_of(step)
    )


def gather_chips(shard, steps):
    dims = lax.axis_size("seq").bit_length()
    cells = shard.reshape((1,) * dims + shard.shape)
    for step in steps:
        cells = gather_step(cells, step)
    return cells.reshape((-1,) + shard.shape)


def scatter_chips(cells, steps):
    dims = lax.axis_size("seq").bit_length()
    cells = cells.reshape((2,) * dims + cells.shape[1:])
    for i, step in enumerate(steps):
        bit, dim = my_bit(step), dim_of(step)
        kept = lax.dynamic_slice_in_dim(cells, bit, 1, axis=dim).astype(F32)
        sent = lax.dynamic_slice_in_dim(cells, 1 - bit, 1, axis=dim)
        if relayed(step):
            sent = (sent.astype(F32) + lax.ppermute(sent, "seq", INWARD).astype(F32)).astype(BF16)
            got = lax.ppermute(sent, "seq", MIDDLE)
        else:
            got = swap(sent, step)
        cells = kept + got.astype(F32)
        if i < len(steps) - 1:
            cells = cells.astype(BF16)
    return cells.reshape(cells.shape[dims:])


def pair(cells, core, dim):
    other = lax.ppermute(cells, "core", [(0, 1), (1, 0)])
    first = core == 0
    return jnp.concatenate(
        [jnp.where(first, cells, other), jnp.where(first, other, cells)], axis=dim
    )


def core_swap(cells):
    return lax.ppermute(cells, "core", [(0, 1), (1, 0)])


def step_orders():
    bits = lax.axis_size("seq").bit_length() - 1
    z = [("seq", b) for b in range(1, bits)]
    x, y = [("seq", 0)], [("fy", 0)]
    return z + x + y, z + y + x


def gather_split(mine, theirs, core):
    one, two = step_orders()
    a, b = gather_chips(mine, one), gather_chips(theirs, two)
    first = core == 0
    both = jnp.stack([jnp.where(first, a, b), jnp.where(first, b, a)], axis=1)
    return both.reshape(-1, mine.shape[-1])


def scatter_split(grad, rows, core):
    one, two = step_orders()
    chips = grad.shape[0] // (2 * rows)
    cells = grad.reshape(chips, 2, rows, grad.shape[-1])
    mine = lax.dynamic_index_in_dim(cells, core, 1, keepdims=False)
    theirs = lax.dynamic_index_in_dim(cells, 1 - core, 1, keepdims=False)
    mine = scatter_chips(mine, one[::-1])
    theirs = scatter_chips(theirs, two[::-1])
    other = core_swap(theirs)
    return jnp.where(core == 0, mine, other), jnp.where(core == 0, other, mine)


def place(index, seq_lengths):
    count = seq_lengths.shape[0]
    ids = jnp.arange(count, dtype=jnp.int32)
    ends = jnp.sum(jnp.where(ids[None, :] <= ids[:, None], seq_lengths[None, :], 0), axis=1)
    starts = ends - seq_lengths
    segment = jnp.sum((index[:, None] >= ends[None, :]).astype(jnp.int32), axis=1)
    begins = jnp.sum(jnp.where(segment[:, None] == ids[None, :], starts[None, :], 0), axis=1)
    return segment, index - begins


def angles(position):
    freqs = 10000.0 ** (-(jnp.arange(HDIM // 2, dtype=F32) * 2.0) / HDIM)
    freqs = jnp.concatenate([freqs] * 4)
    turns = position.astype(F32)[:, None] * freqs[None, :]
    sign = jnp.where(jnp.arange(128) % HDIM < HDIM // 2, -1.0, 1.0)
    return jnp.cos(turns), jnp.sin(turns) * sign[None, :]


def normalize(values):
    average = jnp.mean(values, axis=-1, keepdims=True)
    centered = values - average
    variance = jnp.mean(centered * centered, axis=-1, keepdims=True)
    inverse = lax.rsqrt(variance + EPSILON)
    return centered * inverse, inverse


def norm_back(grad_hat, normed, inverse):
    return inverse * (
        grad_hat
        - jnp.mean(grad_hat, axis=-1, keepdims=True)
        - normed * jnp.mean(grad_hat * normed, axis=-1, keepdims=True)
    )


def geglu(gate_in, up_in):
    return jax.nn.gelu(gate_in, approximate=False) * up_in


def contract(left, right, dims, out=F32):
    return lax.dot_general(left, right, ((dims[0], dims[1]), ((), ())), preferred_element_type=out)


def rows_dot(left, right):
    return contract(left, right, ((0,), (0,)))


def cols_dot(left, right):
    return contract(left, right, ((1,), (1,)))


def half_swap(values):
    lane = lax.broadcasted_iota(jnp.int32, values.shape, 1)
    left = pltpu.roll(values, 128 - HDIM // 2, 1)
    right = pltpu.roll(values, HDIM // 2, 1)
    return jnp.where(lane % HDIM < HDIM // 2, left, right)


def bias_of(q_seg, k_seg, block):
    row = lax.broadcasted_iota(jnp.int32, (128, 256), 0)
    col = lax.broadcasted_iota(jnp.int32, (128, 256), 1)
    near = jnp.abs(row + HALF - col) <= HALF
    same = q_seg[pl.ds(block * 128, 128), :] == k_seg[:, pl.ds(block * 128, 256)]
    return jnp.where(near & same, 0.0, MASKED)


def softmax_of(scores):
    exponent = jnp.exp(scores - jnp.max(scores, axis=-1, keepdims=True))
    return exponent * (1.0 / jnp.sum(exponent, axis=-1, keepdims=True))


def attend_kernel(packed, cosine, sine, q_seg, k_seg, query, keys, values, attended, bias):
    rows = query.shape[0]
    blocks = rows // 128
    for b in range(blocks):
        bias[b] = bias_of(q_seg, k_seg, b)
    first = lax.broadcasted_iota(jnp.int32, (1, 128), 1) < HDIM
    for p in range(OWN_HEADS // 2):
        at = slice(p * 128, (p + 1) * 128)
        u = packed[HALF : HALF + rows, at]
        q_cos, q_sin = cosine[HALF : HALF + rows, :], sine[HALF : HALF + rows, :]
        query[:, at] = (u * q_cos + half_swap(u) * q_sin).astype(BF16)
        u = packed[:, OWN + p * 128 : OWN + (p + 1) * 128]
        keys[:, at] = (u * cosine[...] + half_swap(u) * sine[...]).astype(BF16)
        values[:, at] = packed[:, 2 * OWN + p * 128 : 2 * OWN + (p + 1) * 128].astype(BF16)
        for b in range(blocks):
            q = query[b * 128 : (b + 1) * 128, at]
            k = keys[b * 128 : b * 128 + 256, at]
            v = values[b * 128 : b * 128 + 256, at]
            outs = []
            for side in (first, ~first):
                q_one = jnp.where(side, q, jnp.zeros_like(q))
                scores = contract(q_one, k, ((1,), (1,))) * (HDIM**-0.5) + bias[b]
                prob = softmax_of(scores).astype(BF16)
                outs.append(contract(prob, v, ((1,), (0,))))
            attended[b * 128 : (b + 1) * 128, at] = jnp.where(first, outs[0], outs[1]).astype(BF16)


def attend_back_kernel(
    query, keys, values, grad, cosine, sine, q_seg, k_seg, grad_q, grad_k, grad_v, bias
):
    rows = query.shape[0]
    blocks = rows // 128
    scale = HDIM**-0.5
    for b in range(blocks):
        bias[b] = bias_of(q_seg, k_seg, b)
    first = lax.broadcasted_iota(jnp.int32, (1, 128), 1) < HDIM
    grad_k[...] = jnp.zeros_like(grad_k)
    grad_v[...] = jnp.zeros_like(grad_v)
    for p in range(OWN_HEADS // 2):
        at = slice(p * 128, (p + 1) * 128)
        for b in range(blocks):
            here, span = slice(b * 128, (b + 1) * 128), slice(b * 128, b * 128 + 256)
            q, go = query[here, at], grad[here, at]
            k, v = keys[span, at], values[span, at]
            d_q = jnp.zeros((128, 128), F32)
            d_k = jnp.zeros((256, 128), F32)
            d_v = jnp.zeros((256, 128), F32)
            for side in (first, ~first):
                q_one = jnp.where(side, q, jnp.zeros_like(q))
                k_one = jnp.where(side, k, jnp.zeros_like(k))
                go_one = jnp.where(side, go, jnp.zeros_like(go))
                scores = contract(q_one, k, ((1,), (1,))) * scale + bias[b]
                prob = softmax_of(scores)
                grad_prob = contract(go_one, v, ((1,), (1,)))
                inner = jnp.sum(grad_prob * prob, axis=-1, keepdims=True)
                grad_scores = (prob * (grad_prob - inner)).astype(BF16)
                d_q = d_q + contract(grad_scores, k_one, ((1,), (0,)))
                d_k = d_k + contract(grad_scores, q_one, ((0,), (0,)))
                d_v = d_v + contract(prob.astype(BF16), go_one, ((0,), (0,)))
            d_q = d_q * scale
            at_q = slice(HALF + b * 128, HALF + (b + 1) * 128)
            turned = d_q * cosine[at_q, :] - half_swap(d_q) * sine[at_q, :]
            grad_q[here, at] = turned.astype(BF16)
            grad_k[span, at] += d_k * scale
            grad_v[span, at] += d_v
        d_k = grad_k[:, at]
        grad_k[:, at] = d_k * cosine[...] - half_swap(d_k) * sine[...]


VMEM_LIMIT = 48 * 1024 * 1024


def call_kernel(kernel, outs, blocks, flops, args):
    moved = sum(a.size * a.dtype.itemsize for a in args) + sum(
        o.size * o.dtype.itemsize for o in outs
    )
    return pl.pallas_call(
        kernel,
        out_shape=outs,
        in_specs=[pl.BlockSpec(memory_space=pltpu.VMEM)] * len(args),
        out_specs=[pl.BlockSpec(memory_space=pltpu.VMEM)] * len(outs),
        scratch_shapes=[pltpu.VMEM((blocks, 128, 256), F32)],
        compiler_params=pltpu.CompilerParams(vmem_limit_bytes=VMEM_LIMIT),
        cost_estimate=pl.CostEstimate(flops=flops, bytes_accessed=moved, transcendentals=0),
    )(*args)


def like(shape, dtype):
    return jax.ShapeDtypeStruct(shape, dtype)


def on_device(
    tokens, cotangent, seq_lengths, w_qkv, w_attn_out, w_in, w_mlp_out, gain_attn, gain_mlp
):
    share = tokens.shape[0]
    rows = 2 * share
    core = lax.axis_index("core")
    chip = lax.axis_index(CHIPS)
    chips = lax.axis_size(CHIPS)
    total = chips * rows
    shard = w_qkv.shape[0]
    first = core == 0

    gain_a = gain_attn.astype(F32)[:, None]
    gain_m = gain_mlp.astype(F32)[:, None]
    qkv_cells = (w_qkv.astype(F32) * gain_a).astype(BF16).reshape(shard, 3, 2, OWN)
    in_cells = (w_in.astype(F32) * gain_m).astype(BF16).reshape(shard, 2, 2, OWN_FF)
    mlp_cells = w_mlp_out.reshape(shard, 1, 2, OWN_FF)

    def full(cells):
        one = cells[:, :, 0].reshape(shard, -1)
        two = cells[:, :, 1].reshape(shard, -1)
        mine, sent = jnp.where(first, one, two), jnp.where(first, two, one)
        return gather_split(mine, core_swap(sent), core)

    qkv_full = full(qkv_cells)
    one, two = step_orders()
    half = D // 2
    left = gather_chips(w_attn_out[:, :half], one)
    right = gather_chips(w_attn_out[:, half:], two)
    attn_cells = jnp.concatenate([left, right], axis=-1)
    here = lax.dynamic_slice_in_dim(attn_cells, core * (chips // 2), chips // 2, 0)
    there = lax.dynamic_slice_in_dim(attn_cells, (1 - core) * (chips // 2), chips // 2, 0)
    back = core_swap(there)
    attn_full = jnp.stack(
        [jnp.where(first, here, back), jnp.where(first, back, here)], axis=1
    ).reshape(OWN, D)
    mlp_full = full(mlp_cells)
    in_full = full(in_cells)

    ours = pair(tokens, core, 0)
    cot = pair(cotangent, core, 0)
    ahead = [(i, i + 1) for i in range(chips - 1)]
    behind = [(i + 1, i) for i in range(chips - 1)]
    before = lax.ppermute(ours[rows - HALF :], CHIPS, ahead)
    after = lax.ppermute(ours[:HALF], CHIPS, behind)
    wide = jnp.concatenate([before, ours, after], axis=0)
    index = chip * rows - HALF + jnp.arange(rows + 2 * HALF, dtype=jnp.int32)
    segment, position = place(jnp.clip(index, 0, total - 1), seq_lengths)
    segment = jnp.where((index >= 0) & (index < total), segment, -1)
    q_seg = segment[HALF : HALF + rows][:, None]
    k_seg = segment[None, :]
    cosine, sine = angles(position)

    wide_normed, wide_inverse = normalize(wide.astype(F32))
    hidden = wide_normed.astype(BF16)
    packed = jnp.dot(hidden, qkv_full, preferred_element_type=F32)
    blocks = rows // 128
    flops = blocks * OWN_HEADS * 128 * 256 * 128 * 4
    query, keys, values, attended = call_kernel(
        attend_kernel,
        [
            like((rows, OWN), BF16),
            like((rows + 2 * HALF, OWN), BF16),
            like((rows + 2 * HALF, OWN), BF16),
            like((rows, OWN), BF16),
        ],
        blocks,
        flops,
        (packed, cosine, sine, q_seg, k_seg),
    )
    part = jnp.dot(attended, attn_full, preferred_element_type=F32)
    middle = ours.astype(F32) + (part + core_swap(part))
    normed_mid, inverse_mid = normalize(middle)
    lifted = normed_mid.astype(BF16)
    both = jnp.dot(lifted, in_full, preferred_element_type=F32)
    gate, up = both[:, :OWN_FF], both[:, OWN_FF:]
    mixed = geglu(gate, up).astype(BF16)

    grad_mixed = jnp.dot(cot, mlp_full, preferred_element_type=F32)
    unused, gelu_back = jax.vjp(geglu, gate, up)
    grad_gate, grad_up = gelu_back(grad_mixed)
    grad_both = jnp.concatenate([grad_gate, grad_up], axis=1).astype(BF16)
    grad_mlp_w = rows_dot(cot, mixed).astype(BF16)
    grad_in_w = rows_dot(lifted, grad_both).astype(BF16)
    mlp_low, mlp_high = scatter_split(grad_mlp_w, shard, core)
    in_low, in_high = scatter_split(grad_in_w, shard, core)

    part_lifted = cols_dot(grad_both, in_full)
    grad_hat = part_lifted + core_swap(part_lifted)
    grad_middle = cot.astype(F32) + norm_back(grad_hat, normed_mid, inverse_mid)
    grad_attn = grad_middle.astype(BF16)
    grad_attended = cols_dot(grad_attn, attn_full).astype(BF16)

    grad_q, grad_k, grad_v = call_kernel(
        attend_back_kernel,
        [
            like((rows, OWN), BF16),
            like((rows + 2 * HALF, OWN), F32),
            like((rows + 2 * HALF, OWN), F32),
        ],
        blocks,
        flops * 3,
        (query, keys, values, grad_attended, cosine, sine, q_seg, k_seg),
    )
    grad_kv = jnp.concatenate([grad_k, grad_v], axis=1)
    low_edge = lax.ppermute(grad_kv[:HALF].astype(BF16), CHIPS, behind)
    high_edge = lax.ppermute(grad_kv[HALF + rows :].astype(BF16), CHIPS, ahead)
    middle_kv = grad_kv[HALF : HALF + rows]
    gap = jnp.zeros((rows - 2 * HALF, 2 * OWN), F32)
    edges = jnp.concatenate([high_edge.astype(F32), gap, low_edge.astype(F32)], axis=0)
    grad_packed = jnp.concatenate([grad_q, (middle_kv + edges).astype(BF16)], axis=1)

    grad_attn_w = rows_dot(attended, grad_attn).astype(BF16)
    grad_attn_w = grad_attn_w.reshape(chips // 2, 2, shard, D)
    kept = lax.dynamic_index_in_dim(grad_attn_w, core, 1, keepdims=False)
    given = core_swap(lax.dynamic_index_in_dim(grad_attn_w, 1 - core, 1, keepdims=False))
    attn_rows = jnp.concatenate(
        [jnp.where(first, kept, given), jnp.where(first, given, kept)], axis=0
    )
    grad_attn_out = jnp.concatenate(
        [
            scatter_chips(attn_rows[..., :half], one[::-1]),
            scatter_chips(attn_rows[..., half:], two[::-1]),
        ],
        axis=-1,
    )

    own_hidden = hidden[HALF : HALF + rows]
    grad_qkv_w = rows_dot(own_hidden, grad_packed).astype(BF16)
    qkv_low, qkv_high = scatter_split(grad_qkv_w, shard, core)

    def own_rows(values):
        return lax.dynamic_slice_in_dim(values, core * share, share, 0)

    def other_rows(values):
        return lax.dynamic_slice_in_dim(values, (1 - core) * share, share, 0)

    part_hidden = cols_dot(grad_packed, qkv_full)
    grad_hidden = own_rows(part_hidden) + core_swap(other_rows(part_hidden))
    own_normed = own_rows(wide_normed[HALF : HALF + rows])
    own_inverse = own_rows(wide_inverse[HALF : HALF + rows])
    input_grad = own_rows(grad_middle) + norm_back(grad_hidden, own_normed, own_inverse)

    part_out = cols_dot(mixed, mlp_full)
    output = own_rows(middle) + (own_rows(part_out) + core_swap(other_rows(part_out)))

    def joined(low, high, parts):
        size = low.shape[1] // parts
        cuts = [slice(i * size, (i + 1) * size) for i in range(parts)]
        return jnp.concatenate([half_of[:, c] for c in cuts for half_of in (low, high)], axis=1)

    raw_qkv = joined(qkv_low, qkv_high, 3)
    raw_in = joined(in_low, in_high, 2)
    grad_gain_attn = jnp.sum(raw_qkv * w_qkv.astype(F32), axis=1)
    grad_gain_mlp = jnp.sum(raw_in * w_in.astype(F32), axis=1)
    return (
        output.astype(BF16),
        input_grad,
        raw_qkv * gain_a,
        grad_attn_out,
        raw_in * gain_m,
        joined(mlp_low, mlp_high, 1),
        grad_gain_attn,
        grad_gain_mlp,
    )


def solution(mesh):
    split = Mesh(mesh.devices.reshape(mesh.shape["seq"], -1, 2), ALL)
    two, one = P(ALL, None), P(ALL)
    return jax.shard_map(
        on_device,
        mesh=split,
        in_specs=(two, two, P(), two, two, two, two, one, one),
        out_specs=(two, two, two, two, two, two, one, one),
        check_vma=False,
    )
```

```python
import jax
import jax.numpy as jnp
from jax import lax
from jax.experimental import pallas as pl
from jax.experimental.pallas import tpu as pltpu
from jax.sharding import Mesh, PartitionSpec as P

D = 1024
HEADS = 16
HDIM = 64
FF = 2624
HALF = 64
GROUP = 4
OWN_HEADS = HEADS // GROUP
OWN = OWN_HEADS * HDIM
OWN_FF = FF // GROUP

EPSILON = 1e-05
MASKED = -1e30
ALL = ("seq", "fy", "core")
BF16 = jnp.bfloat16
F32 = jnp.float32


def flat_pairs(change):
    count = lax.axis_size(ALL)
    return [(i, change(i)) for i in range(count)]


def send_seq(cells, flip):
    return lax.ppermute(cells, ALL, flat_pairs(lambda i: i ^ (flip * GROUP)))


def trade(cells, axis, dim):
    me = lax.axis_index(axis)
    kept = lax.dynamic_slice_in_dim(cells, me, 1, axis=dim)
    sent = lax.dynamic_slice_in_dim(cells, 1 - me, 1, axis=dim)
    got = lax.ppermute(sent, axis, [(0, 1), (1, 0)])
    low = me == 0
    return jnp.concatenate([jnp.where(low, kept, got), jnp.where(low, got, kept)], axis=dim)


def join(cells, axis, dim):
    me = lax.axis_index(axis)
    got = lax.ppermute(cells, axis, [(0, 1), (1, 0)])
    low = me == 0
    return jnp.stack([jnp.where(low, cells, got), jnp.where(low, got, cells)], axis=dim)


def reduce_pair(cells, axis, dim):
    me = lax.axis_index(axis)
    kept = lax.dynamic_index_in_dim(cells, me, dim, keepdims=False)
    sent = lax.dynamic_index_in_dim(cells, 1 - me, dim, keepdims=False).astype(BF16)
    got = lax.ppermute(sent, axis, [(0, 1), (1, 0)])
    return kept.astype(F32) + got.astype(F32)


def group_rows(cells):
    both = join(join(cells, "fy", 0), "core", 1)
    return both.reshape((-1,) + cells.shape[1:])


def group_sum(part, rows):
    cells = part.reshape(2, 2, rows, part.shape[-1])
    return reduce_pair(reduce_pair(cells, "core", 1), "fy", 0)


def depth_of():
    return lax.axis_size("seq") // 2


def z_stage(cells):
    z, x = depth_of(), lax.axis_index("seq") & 1
    me = lax.axis_index("seq") >> 1
    if z == 4:
        got = [cells] + [send_seq(cells, 2 * d) for d in range(1, 4)]
        odd, up = (me & 1) == 1, (me >> 1) == 1
        pairs = [
            (jnp.where(odd, got[i + 1], got[i]), jnp.where(odd, got[i], got[i + 1])) for i in (0, 2)
        ]
        return jnp.stack(
            [jnp.where(up, pairs[1][i], pairs[0][i]) for i in (0, 1)]
            + [jnp.where(up, pairs[0][i], pairs[1][i]) for i in (0, 1)]
        )
    cells = cells[None]
    flip = 1
    while flip < z:
        got = send_seq(cells, 2 * flip)
        high = (me & flip) != 0
        cells = jnp.concatenate([jnp.where(high, got, cells), jnp.where(high, cells, got)])
        flip *= 2
    return cells


def x_stage(cells):
    got = send_seq(cells, 1)
    high = (lax.axis_index("seq") & 1) == 1
    return jnp.stack([jnp.where(high, got, cells), jnp.where(high, cells, got)], axis=1)


def x_sum(cells):
    me = lax.axis_index("seq") & 1
    kept = lax.dynamic_index_in_dim(cells, me, 1, keepdims=False)
    got = send_seq(lax.dynamic_index_in_dim(cells, 1 - me, 1, keepdims=False), 1)
    return (kept.astype(F32) + got.astype(F32)).astype(BF16)


def z_sum(cells):
    z, me = depth_of(), lax.axis_index("seq") >> 1
    if z == 4:
        total = lax.dynamic_index_in_dim(cells, me, 0, keepdims=False).astype(F32)
        for d in range(1, 4):
            sent = lax.dynamic_index_in_dim(cells, me ^ d, 0, keepdims=False)
            total = total + send_seq(sent, 2 * d).astype(F32)
        return total
    flip = z // 2
    while flip:
        high = ((me & flip) != 0).astype(jnp.int32)
        kept = lax.dynamic_slice_in_dim(cells, high * flip, flip, 0)
        sent = lax.dynamic_slice_in_dim(cells, (1 - high) * flip, flip, 0)
        cells = kept.astype(F32) + send_seq(sent.astype(BF16), 2 * flip).astype(F32)
        flip //= 2
    return cells[0]


def place(index, seq_lengths):
    count = seq_lengths.shape[0]
    ids = jnp.arange(count, dtype=jnp.int32)
    ends = jnp.sum(jnp.where(ids[None, :] <= ids[:, None], seq_lengths[None, :], 0), axis=1)
    starts = ends - seq_lengths
    segment = jnp.sum((index[:, None] >= ends[None, :]).astype(jnp.int32), axis=1)
    begins = jnp.sum(jnp.where(segment[:, None] == ids[None, :], starts[None, :], 0), axis=1)
    return segment, index - begins


def angles(position):
    freqs = 10000.0 ** (-(jnp.arange(HDIM // 2, dtype=F32) * 2.0) / HDIM)
    freqs = jnp.concatenate([freqs] * 4)
    turns = position.astype(F32)[:, None] * freqs[None, :]
    sign = jnp.where(jnp.arange(128) % HDIM < HDIM // 2, -1.0, 1.0)
    return jnp.cos(turns), jnp.sin(turns) * sign[None, :]


def normalize(values):
    average = jnp.mean(values, axis=-1, keepdims=True)
    centered = values - average
    variance = jnp.mean(centered * centered, axis=-1, keepdims=True)
    inverse = lax.rsqrt(variance + EPSILON)
    return centered * inverse, inverse


def norm_back(grad_hat, normed, inverse):
    return inverse * (
        grad_hat
        - jnp.mean(grad_hat, axis=-1, keepdims=True)
        - normed * jnp.mean(grad_hat * normed, axis=-1, keepdims=True)
    )


def geglu(gate_in, up_in):
    return jax.nn.gelu(gate_in, approximate=False) * up_in


def contract(left, right, dims, out=F32):
    return lax.dot_general(left, right, ((dims[0], dims[1]), ((), ())), preferred_element_type=out)


def rows_dot(left, right):
    return contract(left, right, ((0,), (0,)))


def cols_dot(left, right):
    return contract(left, right, ((1,), (1,)))


def half_swap(values):
    lane = lax.broadcasted_iota(jnp.int32, values.shape, 1)
    left = pltpu.roll(values, 128 - HDIM // 2, 1)
    right = pltpu.roll(values, HDIM // 2, 1)
    return jnp.where(lane % HDIM < HDIM // 2, left, right)


def bias_of(q_seg, k_seg, block):
    row = lax.broadcasted_iota(jnp.int32, (128, 256), 0)
    col = lax.broadcasted_iota(jnp.int32, (128, 256), 1)
    near = jnp.abs(row + HALF - col) <= HALF
    same = q_seg[pl.ds(block * 128, 128), :] == k_seg[:, pl.ds(block * 128, 256)]
    return jnp.where(near & same, 0.0, MASKED)


def softmax_of(scores):
    exponent = jnp.exp(scores - jnp.max(scores, axis=-1, keepdims=True))
    return exponent * (1.0 / jnp.sum(exponent, axis=-1, keepdims=True))


def attend_kernel(packed, cosine, sine, q_seg, k_seg, query, keys, values, attended, bias):
    rows = query.shape[0]
    blocks = rows // 128
    for b in range(blocks):
        bias[b] = bias_of(q_seg, k_seg, b)
    first = lax.broadcasted_iota(jnp.int32, (1, 128), 1) < HDIM
    for p in range(OWN_HEADS // 2):
        at = slice(p * 128, (p + 1) * 128)
        u = packed[HALF : HALF + rows, at]
        q_cos, q_sin = cosine[HALF : HALF + rows, :], sine[HALF : HALF + rows, :]
        query[:, at] = (u * q_cos + half_swap(u) * q_sin).astype(BF16)
        u = packed[:, OWN + p * 128 : OWN + (p + 1) * 128]
        keys[:, at] = (u * cosine[...] + half_swap(u) * sine[...]).astype(BF16)
        values[:, at] = packed[:, 2 * OWN + p * 128 : 2 * OWN + (p + 1) * 128].astype(BF16)
        for b in range(blocks):
            q = query[b * 128 : (b + 1) * 128, at]
            k = keys[b * 128 : b * 128 + 256, at]
            v = values[b * 128 : b * 128 + 256, at]
            outs = []
            for side in (first, ~first):
                q_one = jnp.where(side, q, jnp.zeros_like(q))
                scores = contract(q_one, k, ((1,), (1,))) * (HDIM**-0.5) + bias[b]
                prob = softmax_of(scores).astype(BF16)
                outs.append(contract(prob, v, ((1,), (0,))))
            attended[b * 128 : (b + 1) * 128, at] = jnp.where(first, outs[0], outs[1]).astype(BF16)


def attend_back_kernel(
    query, keys, values, grad, cosine, sine, q_seg, k_seg, grad_q, grad_k, grad_v, bias
):
    rows = query.shape[0]
    blocks = rows // 128
    scale = HDIM**-0.5
    for b in range(blocks):
        bias[b] = bias_of(q_seg, k_seg, b)
    first = lax.broadcasted_iota(jnp.int32, (1, 128), 1) < HDIM
    grad_k[...] = jnp.zeros_like(grad_k)
    grad_v[...] = jnp.zeros_like(grad_v)
    for p in range(OWN_HEADS // 2):
        at = slice(p * 128, (p + 1) * 128)
        for b in range(blocks):
            here, span = slice(b * 128, (b + 1) * 128), slice(b * 128, b * 128 + 256)
            q, go = query[here, at], grad[here, at]
            k, v = keys[span, at], values[span, at]
            d_q = jnp.zeros((128, 128), F32)
            d_k = jnp.zeros((256, 128), F32)
            d_v = jnp.zeros((256, 128), F32)
            for side in (first, ~first):
                q_one = jnp.where(side, q, jnp.zeros_like(q))
                k_one = jnp.where(side, k, jnp.zeros_like(k))
                go_one = jnp.where(side, go, jnp.zeros_like(go))
                scores = contract(q_one, k, ((1,), (1,))) * scale + bias[b]
                prob = softmax_of(scores)
                grad_prob = contract(go_one, v, ((1,), (1,)))
                inner = jnp.sum(grad_prob * prob, axis=-1, keepdims=True)
                grad_scores = (prob * (grad_prob - inner)).astype(BF16)
                d_q = d_q + contract(grad_scores, k_one, ((1,), (0,)))
                d_k = d_k + contract(grad_scores, q_one, ((0,), (0,)))
                d_v = d_v + contract(prob.astype(BF16), go_one, ((0,), (0,)))
            d_q = d_q * scale
            at_q = slice(HALF + b * 128, HALF + (b + 1) * 128)
            turned = d_q * cosine[at_q, :] - half_swap(d_q) * sine[at_q, :]
            grad_q[here, at] = turned.astype(BF16)
            grad_k[span, at] += d_k * scale
            grad_v[span, at] += d_v
        d_k = grad_k[:, at]
        grad_k[:, at] = d_k * cosine[...] - half_swap(d_k) * sine[...]


VMEM_LIMIT = 48 * 1024 * 1024


def call_kernel(kernel, outs, blocks, flops, args):
    moved = sum(a.size * a.dtype.itemsize for a in args) + sum(
        o.size * o.dtype.itemsize for o in outs
    )
    return pl.pallas_call(
        kernel,
        out_shape=outs,
        in_specs=[pl.BlockSpec(memory_space=pltpu.VMEM)] * len(args),
        out_specs=[pl.BlockSpec(memory_space=pltpu.VMEM)] * len(outs),
        scratch_shapes=[pltpu.VMEM((blocks, 128, 256), F32)],
        compiler_params=pltpu.CompilerParams(vmem_limit_bytes=VMEM_LIMIT),
        cost_estimate=pl.CostEstimate(flops=flops, bytes_accessed=moved, transcendentals=0),
    )(*args)


def like(shape, dtype):
    return jax.ShapeDtypeStruct(shape, dtype)


def on_device(
    tokens, cotangent, seq_lengths, w_qkv, w_attn_out, w_in, w_mlp_out, gain_attn, gain_mlp
):
    share = tokens.shape[0]
    rows = GROUP * share
    seq, seqs = lax.axis_index("seq"), lax.axis_size("seq")
    total = seqs * rows
    shard = w_qkv.shape[0]
    tie = lax.optimization_barrier

    gain_a = gain_attn.astype(F32)[:, None]
    gain_m = gain_mlp.astype(F32)[:, None]

    def columns(w, parts, width):
        cells = w.reshape(shard, parts, 2, 2, width).transpose(2, 3, 0, 1, 4)
        return cells.reshape(2, 2, shard, parts * width)

    def regroup(cells):
        return trade(trade(cells, "fy", 0), "core", 1).reshape(GROUP * shard, -1)

    ours = tokens.astype(F32)
    normed, inverse = normalize(ours)
    hidden = group_rows(normed.astype(BF16))

    qkv = regroup(columns((w_qkv.astype(F32) * gain_a).astype(BF16), 3, OWN))
    attn = z_stage(w_attn_out)
    rest = regroup(
        jnp.concatenate(
            [
                columns(w_mlp_out, 1, OWN_FF),
                columns((w_in.astype(F32) * gain_m).astype(BF16), 2, OWN_FF),
            ],
            axis=-1,
        )
    )
    mlp, gate_w, up_w = (rest[:, i * OWN_FF : (i + 1) * OWN_FF] for i in range(3))
    qkv, attn, mlp, gate_w, up_w, hidden = tie((qkv, attn, mlp, gate_w, up_w, hidden))

    ahead = [(i, i + 1) for i in range(seqs - 1)]
    behind = [(i + 1, i) for i in range(seqs - 1)]
    before = lax.ppermute(hidden[rows - HALF :], "seq", ahead)
    after = lax.ppermute(hidden[:HALF], "seq", behind)
    qkv, attn = z_stage(qkv), x_stage(attn)
    qkv, attn, before, after, mlp = tie((qkv, attn, before, after, mlp))
    qkv, mlp = x_stage(qkv), z_stage(mlp)
    attn = trade(attn.reshape(2, 2, seqs // 4, shard, D), "fy", 0)
    attn = trade(attn, "core", 1)
    attn_full = attn.transpose(2, 0, 1, 3, 4).reshape(OWN, D)
    cot = group_rows(cotangent)
    qkv, mlp, gate_w, cot, attn_full = tie((qkv, mlp, gate_w, cot, attn_full))
    qkv_full = qkv.reshape(D, 3 * OWN)
    mlp, gate_w = x_stage(mlp), z_stage(gate_w)

    wide = jnp.concatenate([before, hidden, after], axis=0)
    index = seq * rows - HALF + jnp.arange(rows + 2 * HALF, dtype=jnp.int32)
    segment, position = place(jnp.clip(index, 0, total - 1), seq_lengths)
    segment = jnp.where((index >= 0) & (index < total), segment, -1)
    q_seg = segment[HALF : HALF + rows][:, None]
    k_seg = segment[None, :]
    cosine, sine = angles(position)

    packed = jnp.dot(wide, qkv_full, preferred_element_type=F32)
    blocks = rows // 128
    flops = blocks * OWN_HEADS * 128 * 256 * 128 * 4
    query, keys, values, attended = call_kernel(
        attend_kernel,
        [
            like((rows, OWN), BF16),
            like((rows + 2 * HALF, OWN), BF16),
            like((rows + 2 * HALF, OWN), BF16),
            like((rows, OWN), BF16),
        ],
        blocks,
        flops,
        (packed, cosine, sine, q_seg, k_seg),
    )
    part = jnp.dot(attended, attn_full, preferred_element_type=F32)
    middle = ours + group_sum(part, share)
    mlp, gate_w, up_w, middle = tie((mlp, gate_w, up_w, middle))
    gate_w, up_w = x_stage(gate_w), z_stage(up_w)
    normed_mid, inverse_mid = normalize(middle)
    lifted = group_rows(normed_mid.astype(BF16))
    mlp_full = mlp.reshape(D, OWN_FF)
    grad_mixed = jnp.dot(cot, mlp_full, preferred_element_type=F32)
    gate_w, up_w, lifted, grad_mixed = tie((gate_w, up_w, lifted, grad_mixed))
    up_full = x_stage(up_w).reshape(D, OWN_FF)
    gate_full = gate_w.reshape(D, OWN_FF)
    gate = jnp.dot(lifted, gate_full, preferred_element_type=F32)
    up_full, gate = tie((up_full, gate))
    up = jnp.dot(lifted, up_full, preferred_element_type=F32)
    mixed = geglu(gate, up).astype(BF16)

    unused, gelu_back = jax.vjp(geglu, gate, up)
    grad_gate, grad_up = gelu_back(grad_mixed)
    grad_gate, grad_up = grad_gate.astype(BF16), grad_up.astype(BF16)

    def stacked(grad):
        return grad.astype(BF16).reshape(seqs // 2, 2, -1, grad.shape[-1])

    mlp_g = stacked(rows_dot(cot, mixed))
    mixed, grad_gate, grad_up, mlp_g = tie((mixed, grad_gate, grad_up, mlp_g))
    mlp_g = x_sum(mlp_g)
    part_lifted = cols_dot(grad_gate, gate_full) + cols_dot(grad_up, up_full)
    gate_g = stacked(rows_dot(lifted, grad_gate))
    up_g = stacked(rows_dot(lifted, grad_up))
    grad_hat = group_sum(part_lifted, share)
    mlp_g, gate_g, up_g, grad_hat = tie((mlp_g, gate_g, up_g, grad_hat))
    mlp_g, gate_g = z_sum(mlp_g), x_sum(gate_g)
    grad_middle = cotangent.astype(F32) + norm_back(grad_hat, normed_mid, inverse_mid)
    grad_attn = group_rows(grad_middle.astype(BF16))
    grad_attended = cols_dot(grad_attn, attn_full).astype(BF16)
    attn_g = rows_dot(attended, grad_attn).astype(BF16)
    grad_q, grad_k, grad_v = call_kernel(
        attend_back_kernel,
        [
            like((rows, OWN), BF16),
            like((rows + 2 * HALF, OWN), F32),
            like((rows + 2 * HALF, OWN), F32),
        ],
        blocks,
        flops * 3,
        (query, keys, values, grad_attended, cosine, sine, q_seg, k_seg),
    )
    grad_kv = jnp.concatenate([grad_k, grad_v], axis=1)
    mlp_g, gate_g, up_g, grad_kv, grad_q, attn_g = tie((mlp_g, gate_g, up_g, grad_kv, grad_q, attn_g))
    low_edge = lax.ppermute(grad_kv[:HALF].astype(BF16), "seq", behind)
    high_edge = lax.ppermute(grad_kv[HALF + rows :].astype(BF16), "seq", ahead)
    gate_g, up_g = z_sum(gate_g), x_sum(up_g)
    attn_g = attn_g.reshape(seqs // 4, 2, 2, shard, D).transpose(1, 2, 0, 3, 4)
    attn_g = trade(trade(attn_g, "core", 1), "fy", 0).reshape(seqs // 2, 2, shard, D)
    middle_kv = grad_kv[HALF : HALF + rows]
    gap = jnp.zeros((rows - 2 * HALF, 2 * OWN), F32)
    edges = jnp.concatenate([high_edge.astype(F32), gap, low_edge.astype(F32)], axis=0)
    grad_packed = jnp.concatenate([grad_q, (middle_kv + edges).astype(BF16)], axis=1)
    qkv_g = stacked(rows_dot(hidden, grad_packed))
    gate_g, up_g, attn_g, qkv_g, grad_packed = tie((gate_g, up_g, attn_g, qkv_g, grad_packed))
    up_g, attn_g, qkv_g = z_sum(up_g), x_sum(attn_g), x_sum(qkv_g)
    part_hidden = cols_dot(grad_packed, qkv_full)
    grad_hidden = group_sum(part_hidden, share)
    part_out = cols_dot(mixed, mlp_full)
    output = middle + group_sum(part_out, share)

    def regroup_back(cells):
        cells = cells.astype(BF16).reshape(2, 2, shard, -1)
        return trade(trade(cells, "fy", 0), "core", 1)

    def back_columns(cells, parts, width):
        cells = cells.reshape(2, 2, shard, parts, width).transpose(2, 3, 0, 1, 4)
        return cells.reshape(shard, parts * 2 * 2 * width).astype(F32)

    up_g, attn_g, qkv_g, mlp_g, gate_g, grad_hidden, output = tie(
        (up_g, attn_g, qkv_g, mlp_g, gate_g, grad_hidden, output)
    )
    grad_qkv, grad_attn_out = z_sum(qkv_g), z_sum(attn_g)
    rest_g = regroup_back(jnp.concatenate([mlp_g, gate_g, up_g], axis=-1))
    raw_mlp = back_columns(rest_g[..., :OWN_FF], 1, OWN_FF)
    raw_in = back_columns(rest_g[..., OWN_FF:], 2, OWN_FF)
    raw_qkv = back_columns(regroup_back(grad_qkv), 3, OWN)
    input_grad = grad_middle + norm_back(grad_hidden, normed, inverse)
    grad_gain_attn = jnp.sum(raw_qkv * w_qkv.astype(F32), axis=1)
    grad_gain_mlp = jnp.sum(raw_in * w_in.astype(F32), axis=1)
    return (
        output.astype(BF16),
        input_grad,
        raw_qkv * gain_a,
        grad_attn_out,
        raw_in * gain_m,
        raw_mlp,
        grad_gain_attn,
        grad_gain_mlp,
    )


def solution(mesh):
    split = Mesh(mesh.devices.reshape(mesh.shape["seq"], -1, 2), ALL)
    two, one = P(ALL, None), P(ALL)
    return jax.shard_map(
        on_device,
        mesh=split,
        in_specs=(two, two, P(), two, two, two, two, one, one),
        out_specs=(two, two, two, two, two, two, one, one),
        check_vma=False,
    )
```

```python
import jax
import jax.numpy as jnp
from jax import lax
from jax.experimental import pallas as pl
from jax.experimental.pallas import tpu as pltpu
from jax.sharding import Mesh, PartitionSpec as P

D = 1024
HEADS = 16
HDIM = 64
FF = 2624
HALF = 64
GROUP = 4
OWN_HEADS = HEADS // GROUP
OWN = OWN_HEADS * HDIM
OWN_FF = FF // GROUP

EPSILON = 1e-05
MASKED = -1e30
ALL = ("seq", "fy", "core")
BF16 = jnp.bfloat16
F32 = jnp.float32


def flat_pairs(change):
    count = lax.axis_size(ALL)
    return [(i, change(i)) for i in range(count)]


def send_seq(cells, flip):
    return lax.ppermute(cells, ALL, flat_pairs(lambda i: i ^ (flip * GROUP)))


def trade(cells, axis, dim):
    me = lax.axis_index(axis)
    kept = lax.dynamic_slice_in_dim(cells, me, 1, axis=dim)
    sent = lax.dynamic_slice_in_dim(cells, 1 - me, 1, axis=dim)
    got = lax.ppermute(sent, axis, [(0, 1), (1, 0)])
    low = me == 0
    return jnp.concatenate([jnp.where(low, kept, got), jnp.where(low, got, kept)], axis=dim)


def join(cells, axis, dim):
    me = lax.axis_index(axis)
    got = lax.ppermute(cells, axis, [(0, 1), (1, 0)])
    low = me == 0
    return jnp.stack([jnp.where(low, cells, got), jnp.where(low, got, cells)], axis=dim)


def reduce_pair(cells, axis, dim):
    me = lax.axis_index(axis)
    kept = lax.dynamic_index_in_dim(cells, me, dim, keepdims=False)
    sent = lax.dynamic_index_in_dim(cells, 1 - me, dim, keepdims=False).astype(BF16)
    got = lax.ppermute(sent, axis, [(0, 1), (1, 0)])
    return kept.astype(F32) + got.astype(F32)


def group_rows(cells):
    both = join(join(cells, "fy", 0), "core", 1)
    return both.reshape((-1,) + cells.shape[1:])


def group_sum(part, rows):
    cells = part.reshape(2, 2, rows, part.shape[-1])
    return reduce_pair(reduce_pair(cells, "core", 1), "fy", 0)


def depth_of():
    return lax.axis_size("seq") // 2


def z_send(cells):
    if depth_of() == 4:
        return [cells] + [send_seq(cells, 2 * d) for d in range(1, 4)]
    return [cells]


def z_order(got):
    z, me = depth_of(), lax.axis_index("seq") >> 1
    if z == 4:
        odd, up = (me & 1) == 1, (me >> 1) == 1
        pairs = [
            (jnp.where(odd, got[i + 1], got[i]), jnp.where(odd, got[i], got[i + 1])) for i in (0, 2)
        ]
        return jnp.stack(
            [jnp.where(up, pairs[1][i], pairs[0][i]) for i in (0, 1)]
            + [jnp.where(up, pairs[0][i], pairs[1][i]) for i in (0, 1)]
        )
    cells = got[0][None]
    flip = 1
    while flip < z:
        other = send_seq(cells, 2 * flip)
        high = (me & flip) != 0
        cells = jnp.concatenate([jnp.where(high, other, cells), jnp.where(high, cells, other)])
        flip *= 2
    return cells


def x_order(cells, got):
    high = (lax.axis_index("seq") & 1) == 1
    blocks = []
    for i in range(cells.shape[0]):
        blocks += [jnp.where(high, got[i], cells[i]), jnp.where(high, cells[i], got[i])]
    return blocks


def x_split(blocks):
    high = (lax.axis_index("seq") & 1) == 1
    pairs = list(zip(blocks[::2], blocks[1::2]))
    kept = jnp.stack([jnp.where(high, b, a) for a, b in pairs])
    sent = jnp.stack([jnp.where(high, a, b) for a, b in pairs])
    return kept, sent


def lane_blocks(grad):
    count = lax.axis_size("seq")
    size = grad.shape[1] // count
    return [grad[:, i * size : (i + 1) * size] for i in range(count)]


def x_sum(kept, got):
    return (kept.astype(F32) + got.astype(F32)).astype(BF16)


def z_spread(cells):
    z, me = depth_of(), lax.axis_index("seq") >> 1
    if z == 4:
        blocks = [lax.dynamic_index_in_dim(cells, me ^ d, 0, keepdims=False) for d in range(4)]
        return [blocks[0]] + [send_seq(blocks[d], 2 * d) for d in range(1, 4)]
    flip = z // 2
    while flip:
        high = ((me & flip) != 0).astype(jnp.int32)
        kept = lax.dynamic_slice_in_dim(cells, high * flip, flip, 0)
        sent = lax.dynamic_slice_in_dim(cells, (1 - high) * flip, flip, 0)
        cells = kept.astype(F32) + send_seq(sent.astype(BF16), 2 * flip).astype(F32)
        flip //= 2
    return [cells[0]]


def z_total(got):
    return sum(cells.astype(F32) for cells in got)


def place(index, seq_lengths):
    count = seq_lengths.shape[0]
    ids = jnp.arange(count, dtype=jnp.int32)
    ends = jnp.sum(jnp.where(ids[None, :] <= ids[:, None], seq_lengths[None, :], 0), axis=1)
    starts = ends - seq_lengths
    segment = jnp.sum((index[:, None] >= ends[None, :]).astype(jnp.int32), axis=1)
    begins = jnp.sum(jnp.where(segment[:, None] == ids[None, :], starts[None, :], 0), axis=1)
    return segment, index - begins


def angles(position):
    freqs = 10000.0 ** (-(jnp.arange(HDIM // 2, dtype=F32) * 2.0) / HDIM)
    freqs = jnp.concatenate([freqs] * 4)
    turns = position.astype(F32)[:, None] * freqs[None, :]
    sign = jnp.where(jnp.arange(128) % HDIM < HDIM // 2, -1.0, 1.0)
    return jnp.cos(turns), jnp.sin(turns) * sign[None, :]


def normalize(values):
    average = jnp.mean(values, axis=-1, keepdims=True)
    centered = values - average
    variance = jnp.mean(centered * centered, axis=-1, keepdims=True)
    inverse = lax.rsqrt(variance + EPSILON)
    return centered * inverse, inverse


def norm_back(grad_hat, normed, inverse):
    return inverse * (
        grad_hat
        - jnp.mean(grad_hat, axis=-1, keepdims=True)
        - normed * jnp.mean(grad_hat * normed, axis=-1, keepdims=True)
    )


def geglu(gate_in, up_in):
    return jax.nn.gelu(gate_in, approximate=False) * up_in


def contract(left, right, dims, out=F32):
    return lax.dot_general(left, right, ((dims[0], dims[1]), ((), ())), preferred_element_type=out)


def rows_dot(left, right):
    return contract(left, right, ((0,), (0,)))


def cols_dot(left, right):
    return contract(left, right, ((1,), (1,)))


def half_swap(values):
    lane = lax.broadcasted_iota(jnp.int32, values.shape, 1)
    left = pltpu.roll(values, 128 - HDIM // 2, 1)
    right = pltpu.roll(values, HDIM // 2, 1)
    return jnp.where(lane % HDIM < HDIM // 2, left, right)


def bias_of(q_seg, k_seg, block):
    row = lax.broadcasted_iota(jnp.int32, (128, 256), 0)
    col = lax.broadcasted_iota(jnp.int32, (128, 256), 1)
    near = jnp.abs(row + HALF - col) <= HALF
    same = q_seg[pl.ds(block * 128, 128), :] == k_seg[:, pl.ds(block * 128, 256)]
    return jnp.where(near & same, 0.0, MASKED)


def softmax_of(scores):
    exponent = jnp.exp(scores - jnp.max(scores, axis=-1, keepdims=True))
    return exponent * (1.0 / jnp.sum(exponent, axis=-1, keepdims=True))


def attend_kernel(packed, cosine, sine, q_seg, k_seg, query, keys, values, attended, bias):
    rows = query.shape[0]
    blocks = rows // 128
    for b in range(blocks):
        bias[b] = bias_of(q_seg, k_seg, b)
    first = lax.broadcasted_iota(jnp.int32, (1, 128), 1) < HDIM
    for p in range(OWN_HEADS // 2):
        at = slice(p * 128, (p + 1) * 128)
        u = packed[HALF : HALF + rows, at]
        q_cos, q_sin = cosine[HALF : HALF + rows, :], sine[HALF : HALF + rows, :]
        query[:, at] = (u * q_cos + half_swap(u) * q_sin).astype(BF16)
        u = packed[:, OWN + p * 128 : OWN + (p + 1) * 128]
        keys[:, at] = (u * cosine[...] + half_swap(u) * sine[...]).astype(BF16)
        values[:, at] = packed[:, 2 * OWN + p * 128 : 2 * OWN + (p + 1) * 128].astype(BF16)
        for b in range(blocks):
            q = query[b * 128 : (b + 1) * 128, at]
            k = keys[b * 128 : b * 128 + 256, at]
            v = values[b * 128 : b * 128 + 256, at]
            outs = []
            for side in (first, ~first):
                q_one = jnp.where(side, q, jnp.zeros_like(q))
                scores = contract(q_one, k, ((1,), (1,))) * (HDIM**-0.5) + bias[b]
                prob = softmax_of(scores).astype(BF16)
                outs.append(contract(prob, v, ((1,), (0,))))
            attended[b * 128 : (b + 1) * 128, at] = jnp.where(first, outs[0], outs[1]).astype(BF16)


def attend_back_kernel(
    query, keys, values, grad, cosine, sine, q_seg, k_seg, grad_q, grad_k, grad_v, bias
):
    rows = query.shape[0]
    blocks = rows // 128
    scale = HDIM**-0.5
    for b in range(blocks):
        bias[b] = bias_of(q_seg, k_seg, b)
    first = lax.broadcasted_iota(jnp.int32, (1, 128), 1) < HDIM
    grad_k[...] = jnp.zeros_like(grad_k)
    grad_v[...] = jnp.zeros_like(grad_v)
    for p in range(OWN_HEADS // 2):
        at = slice(p * 128, (p + 1) * 128)
        for b in range(blocks):
            here, span = slice(b * 128, (b + 1) * 128), slice(b * 128, b * 128 + 256)
            q, go = query[here, at], grad[here, at]
            k, v = keys[span, at], values[span, at]
            d_q = jnp.zeros((128, 128), F32)
            d_k = jnp.zeros((256, 128), F32)
            d_v = jnp.zeros((256, 128), F32)
            for side in (first, ~first):
                q_one = jnp.where(side, q, jnp.zeros_like(q))
                k_one = jnp.where(side, k, jnp.zeros_like(k))
                go_one = jnp.where(side, go, jnp.zeros_like(go))
                scores = contract(q_one, k, ((1,), (1,))) * scale + bias[b]
                prob = softmax_of(scores)
                grad_prob = contract(go_one, v, ((1,), (1,)))
                inner = jnp.sum(grad_prob * prob, axis=-1, keepdims=True)
                grad_scores = (prob * (grad_prob - inner)).astype(BF16)
                d_q = d_q + contract(grad_scores, k_one, ((1,), (0,)))
                d_k = d_k + contract(grad_scores, q_one, ((0,), (0,)))
                d_v = d_v + contract(prob.astype(BF16), go_one, ((0,), (0,)))
            d_q = d_q * scale
            at_q = slice(HALF + b * 128, HALF + (b + 1) * 128)
            turned = d_q * cosine[at_q, :] - half_swap(d_q) * sine[at_q, :]
            grad_q[here, at] = turned.astype(BF16)
            grad_k[span, at] += d_k * scale
            grad_v[span, at] += d_v
        d_k = grad_k[:, at]
        grad_k[:, at] = d_k * cosine[...] - half_swap(d_k) * sine[...]


VMEM_LIMIT = 48 * 1024 * 1024


def call_kernel(kernel, outs, blocks, flops, args):
    moved = sum(a.size * a.dtype.itemsize for a in args) + sum(
        o.size * o.dtype.itemsize for o in outs
    )
    return pl.pallas_call(
        kernel,
        out_shape=outs,
        in_specs=[pl.BlockSpec(memory_space=pltpu.VMEM)] * len(args),
        out_specs=[pl.BlockSpec(memory_space=pltpu.VMEM)] * len(outs),
        scratch_shapes=[pltpu.VMEM((blocks, 128, 256), F32)],
        compiler_params=pltpu.CompilerParams(vmem_limit_bytes=VMEM_LIMIT),
        cost_estimate=pl.CostEstimate(flops=flops, bytes_accessed=moved, transcendentals=0),
    )(*args)


def like(shape, dtype):
    return jax.ShapeDtypeStruct(shape, dtype)


def on_device(
    tokens, cotangent, seq_lengths, w_qkv, w_attn_out, w_in, w_mlp_out, gain_attn, gain_mlp
):
    share = tokens.shape[0]
    rows = GROUP * share
    seq, seqs = lax.axis_index("seq"), lax.axis_size("seq")
    total = seqs * rows
    shard = w_qkv.shape[0]
    tie = lax.optimization_barrier

    gain_a = gain_attn.astype(F32)[:, None]
    gain_m = gain_mlp.astype(F32)[:, None]

    def columns(w, parts, width):
        cells = w.reshape(shard, parts, 2, 2, width).transpose(2, 3, 0, 1, 4)
        return cells.reshape(2, 2, shard, parts * width)

    def regroup(cells):
        cells = trade(trade(cells, "fy", 0), "core", 1)
        return cells.reshape(GROUP * shard, -1).T

    def whole(cells, got):
        return jnp.concatenate(x_order(cells, got), axis=-1)

    attn_got = z_send(w_attn_out)
    qkv_got = z_send(regroup(columns((w_qkv.astype(F32) * gain_a).astype(BF16), 3, OWN)))
    rest = regroup(
        jnp.concatenate(
            [
                columns(w_mlp_out, 1, OWN_FF),
                columns((w_in.astype(F32) * gain_m).astype(BF16), 2, OWN_FF),
            ],
            axis=-1,
        )
    )
    mlp_got, gate_got, up_got = (
        z_send(rest[i * OWN_FF : (i + 1) * OWN_FF]) for i in range(3)
    )
    ours = tokens.astype(F32)
    normed, inverse = normalize(ours)
    hidden = group_rows(normed.astype(BF16))
    cot = group_rows(cotangent)

    attn_z = z_order(attn_got)
    attn_x = send_seq(attn_z, 1)
    qkv_got, attn_z = tie((qkv_got, attn_z))
    qkv_z = z_order(qkv_got)
    qkv_x = send_seq(qkv_z, 1)
    hidden, qkv_z = tie((hidden, qkv_z))
    ahead = [(i, i + 1) for i in range(seqs - 1)]
    behind = [(i + 1, i) for i in range(seqs - 1)]
    before = lax.ppermute(hidden[rows - HALF :], "seq", ahead)
    after = lax.ppermute(hidden[:HALF], "seq", behind)
    attn = jnp.stack(x_order(attn_z, attn_x))
    attn = trade(attn.reshape(2, 2, seqs // 4, shard, D), "fy", 0)
    attn = trade(attn, "core", 1)
    attn_full = attn.transpose(2, 0, 1, 3, 4).reshape(OWN, D)
    mlp_got, qkv_z = tie((mlp_got, qkv_z))
    mlp_z = z_order(mlp_got)
    mlp_x = send_seq(mlp_z, 1)
    qkv_x, mlp_z, attn_full = tie((qkv_x, mlp_z, attn_full))
    qkv_full = whole(qkv_z, qkv_x)

    wide = jnp.concatenate([before, hidden, after], axis=0)
    index = seq * rows - HALF + jnp.arange(rows + 2 * HALF, dtype=jnp.int32)
    segment, position = place(jnp.clip(index, 0, total - 1), seq_lengths)
    segment = jnp.where((index >= 0) & (index < total), segment, -1)
    q_seg = segment[HALF : HALF + rows][:, None]
    k_seg = segment[None, :]
    cosine, sine = angles(position)

    packed = cols_dot(wide, qkv_full)
    blocks = rows // 128
    flops = blocks * OWN_HEADS * 128 * 256 * 128 * 4
    query, keys, values, attended = call_kernel(
        attend_kernel,
        [
            like((rows, OWN), BF16),
            like((rows + 2 * HALF, OWN), BF16),
            like((rows + 2 * HALF, OWN), BF16),
            like((rows, OWN), BF16),
        ],
        blocks,
        flops,
        (packed, cosine, sine, q_seg, k_seg),
    )
    part = jnp.dot(attended, attn_full, preferred_element_type=F32)
    middle = ours + group_sum(part, share)
    gate_got, part = tie((gate_got, part))
    gate_z = z_order(gate_got)
    gate_x = send_seq(gate_z, 1)
    gate_z, middle = tie((gate_z, middle))
    normed_mid, inverse_mid = normalize(middle)
    lifted = group_rows(normed_mid.astype(BF16))
    mlp_x, gate_z = tie((mlp_x, gate_z))
    mlp_full = whole(mlp_z, mlp_x)
    grad_mixed = cols_dot(cot, mlp_full)
    up_got, grad_mixed, lifted = tie((up_got, grad_mixed, lifted))
    up_z = z_order(up_got)
    up_x = send_seq(up_z, 1)
    gate_x, up_z = tie((gate_x, up_z))
    gate_full = whole(gate_z, gate_x)
    gate = cols_dot(lifted, gate_full)
    up_x, gate = tie((up_x, gate))
    up_full = whole(up_z, up_x)
    up = cols_dot(lifted, up_full)
    mixed = geglu(gate, up).astype(BF16)

    unused, gelu_back = jax.vjp(geglu, gate, up)
    grad_gate, grad_up = gelu_back(grad_mixed)
    grad_gate, grad_up = grad_gate.astype(BF16), grad_up.astype(BF16)

    def grad_split(left, right):
        return x_split(lane_blocks(rows_dot(left, right).astype(BF16)))

    mlp_kept, mlp_sent = grad_split(mixed, cot)
    mlp_x = send_seq(mlp_sent, 1)
    mlp_sent, grad_gate, grad_up = tie((mlp_sent, grad_gate, grad_up))
    part_lifted = jnp.dot(grad_gate, gate_full, preferred_element_type=F32) + jnp.dot(
        grad_up, up_full, preferred_element_type=F32
    )
    half_hat = reduce_pair(part_lifted.reshape(2, 2, share, D), "core", 1)
    part_lifted, grad_gate, grad_up = tie((part_lifted, grad_gate, grad_up))
    gate_kept, gate_sent = grad_split(grad_gate, lifted)
    gate_x = send_seq(gate_sent, 1)
    half_hat, gate_sent = tie((half_hat, gate_sent))
    grad_hat = reduce_pair(half_hat, "fy", 0)
    up_kept, up_sent = grad_split(grad_up, lifted)
    up_x = send_seq(up_sent, 1)
    grad_hat, up_sent = tie((grad_hat, up_sent))
    grad_middle = cotangent.astype(F32) + norm_back(grad_hat, normed_mid, inverse_mid)
    grad_attn = group_rows(grad_middle.astype(BF16))
    grad_attended = cols_dot(grad_attn, attn_full).astype(BF16)
    grad_q, grad_k, grad_v = call_kernel(
        attend_back_kernel,
        [
            like((rows, OWN), BF16),
            like((rows + 2 * HALF, OWN), F32),
            like((rows + 2 * HALF, OWN), F32),
        ],
        blocks,
        flops * 3,
        (query, keys, values, grad_attended, cosine, sine, q_seg, k_seg),
    )
    grad_kv = jnp.concatenate([grad_k, grad_v], axis=1)
    low_sent = grad_kv[:HALF].astype(BF16)
    high_sent = grad_kv[HALF + rows :].astype(BF16)
    low_edge = lax.ppermute(low_sent, "seq", behind)
    high_edge = lax.ppermute(high_sent, "seq", ahead)
    mlp_x, gate_x, low_sent, attended = tie((mlp_x, gate_x, low_sent, attended))
    mlp_got = z_spread(x_sum(mlp_kept, mlp_x))
    attn_g = rows_dot(attended, grad_attn).astype(BF16)
    attn_g = attn_g.reshape(seqs // 4, 2, 2, shard, D).transpose(1, 2, 0, 3, 4)
    attn_g = trade(trade(attn_g, "core", 1), "fy", 0).reshape(seqs, shard, D)
    low_edge, high_edge, mlp_got = tie((low_edge, high_edge, mlp_got))
    middle_kv = grad_kv[HALF : HALF + rows]
    gap = jnp.zeros((rows - 2 * HALF, 2 * OWN), F32)
    edges = jnp.concatenate([high_edge.astype(F32), gap, low_edge.astype(F32)], axis=0)
    grad_packed = jnp.concatenate([grad_q, (middle_kv + edges).astype(BF16)], axis=1)
    qkv_kept, qkv_sent = grad_split(grad_packed, hidden)
    qkv_x = send_seq(qkv_sent, 1)
    gate_x, qkv_sent = tie((gate_x, qkv_sent))
    gate_got = z_spread(x_sum(gate_kept, gate_x))
    attn_kept, attn_sent = x_split([attn_g[i] for i in range(seqs)])
    attn_x = send_seq(attn_sent, 1)
    up_x, gate_got, attn_sent = tie((up_x, gate_got, attn_sent))
    up_got = z_spread(x_sum(up_kept, up_x))
    part_hidden = jnp.dot(grad_packed, qkv_full, preferred_element_type=F32)
    grad_hidden = group_sum(part_hidden, share)
    part_out = jnp.dot(mixed, mlp_full, preferred_element_type=F32)
    output = middle + group_sum(part_out, share)
    qkv_x, up_got, grad_hidden, output = tie((qkv_x, up_got, grad_hidden, output))
    qkv_got = z_spread(x_sum(qkv_kept, qkv_x))
    attn_x, qkv_got = tie((attn_x, qkv_got))
    grad_attn_out = z_total(z_spread(x_sum(attn_kept, attn_x)))
    mlp_g, gate_g, up_g = z_total(mlp_got), z_total(gate_got), z_total(up_got)
    grad_qkv = z_total(qkv_got)

    def regroup_back(cells):
        cells = cells.T.astype(BF16).reshape(2, 2, shard, -1)
        return trade(trade(cells, "fy", 0), "core", 1)

    def back_columns(cells, parts, width):
        cells = cells.reshape(2, 2, shard, parts, width).transpose(2, 3, 0, 1, 4)
        return cells.reshape(shard, parts * 2 * 2 * width).astype(F32)

    rest_g = regroup_back(jnp.concatenate([mlp_g, gate_g, up_g], axis=0))
    raw_mlp = back_columns(rest_g[..., :OWN_FF], 1, OWN_FF)
    raw_in = back_columns(rest_g[..., OWN_FF:], 2, OWN_FF)
    raw_qkv = back_columns(regroup_back(grad_qkv), 3, OWN)
    input_grad = grad_middle + norm_back(grad_hidden, normed, inverse)
    grad_gain_attn = jnp.sum(raw_qkv * w_qkv.astype(F32), axis=1)
    grad_gain_mlp = jnp.sum(raw_in * w_in.astype(F32), axis=1)
    return (
        output.astype(BF16),
        input_grad,
        raw_qkv * gain_a,
        grad_attn_out,
        raw_in * gain_m,
        raw_mlp,
        grad_gain_attn,
        grad_gain_mlp,
    )


def solution(mesh):
    split = Mesh(mesh.devices.reshape(mesh.shape["seq"], -1, 2), ALL)
    two, one = P(ALL, None), P(ALL)
    return jax.shard_map(
        on_device,
        mesh=split,
        in_specs=(two, two, P(), two, two, two, two, one, one),
        out_specs=(two, two, two, two, two, two, one, one),
        check_vma=False,
    )
```

```python
import jax
import jax.numpy as jnp
from jax import lax
from jax.experimental import pallas as pl
from jax.experimental.pallas import tpu as pltpu
from jax.sharding import Mesh, PartitionSpec as P

D = 1024
HEADS = 16
HDIM = 64
FF = 2624
HALF = 64
GROUP = 4
OWN_HEADS = HEADS // GROUP
OWN = OWN_HEADS * HDIM
OWN_FF = FF // GROUP
WIDE = 2048
VMEM_LIMIT = 48 * 1024 * 1024

EPSILON = 1e-05
MASKED = -1e30
ALL = ("seq", "fy", "core")
BF16 = jnp.bfloat16
F32 = jnp.float32


def flat_pairs(change):
    count = lax.axis_size(ALL)
    return [(i, change(i)) for i in range(count)]


def send_seq(cells, flip):
    return lax.ppermute(cells, ALL, flat_pairs(lambda i: i ^ (flip * GROUP)))


def trade(cells, axis, dim):
    me = lax.axis_index(axis)
    kept = lax.dynamic_slice_in_dim(cells, me, 1, axis=dim)
    sent = lax.dynamic_slice_in_dim(cells, 1 - me, 1, axis=dim)
    got = lax.ppermute(sent, axis, [(0, 1), (1, 0)])
    low = me == 0
    return jnp.concatenate([jnp.where(low, kept, got), jnp.where(low, got, kept)], axis=dim)


def join(cells, axis, dim):
    me = lax.axis_index(axis)
    got = lax.ppermute(cells, axis, [(0, 1), (1, 0)])
    low = me == 0
    return jnp.stack([jnp.where(low, cells, got), jnp.where(low, got, cells)], axis=dim)


def reduce_pair(cells, axis, dim):
    me = lax.axis_index(axis)
    kept = lax.dynamic_index_in_dim(cells, me, dim, keepdims=False)
    sent = lax.dynamic_index_in_dim(cells, 1 - me, dim, keepdims=False).astype(BF16)
    got = lax.ppermute(sent, axis, [(0, 1), (1, 0)])
    return kept.astype(F32) + got.astype(F32)


def group_rows(cells):
    both = join(join(cells, "fy", 0), "core", 1)
    return both.reshape((-1,) + cells.shape[1:])


def group_sum(part, rows):
    cells = part.reshape(2, 2, rows, part.shape[-1])
    return reduce_pair(reduce_pair(cells, "core", 1), "fy", 0)


def depth_of():
    return lax.axis_size("seq") // 2


def direct():
    return lax.axis_size("seq") == 8


def place_of_device():
    seq = lax.axis_index("seq")
    return jnp.stack([seq >> 1, seq & 1]).astype(jnp.int32)


def z_gather(cells):
    if direct():
        return jnp.stack([cells] + [send_seq(cells, 2 * d) for d in range(1, 4)])
    cells, me = cells[None], lax.axis_index("seq") >> 1
    flip = 1
    while flip < depth_of():
        other = send_seq(cells, 2 * flip)
        high = (me & flip) != 0
        cells = jnp.concatenate([jnp.where(high, other, cells), jnp.where(high, cells, other)])
        flip *= 2
    return cells


def x_sum(kept, got):
    return (kept.astype(F32) + got.astype(F32)).astype(BF16)


def z_spread(cells):
    if direct():
        return [cells[0]] + [send_seq(cells[d], 2 * d) for d in range(1, 4)]
    flip, me = depth_of() // 2, lax.axis_index("seq") >> 1
    while flip:
        high = ((me & flip) != 0).astype(jnp.int32)
        kept = lax.dynamic_slice_in_dim(cells, high * flip, flip, 0)
        sent = lax.dynamic_slice_in_dim(cells, (1 - high) * flip, flip, 0)
        cells = kept.astype(F32) + send_seq(sent.astype(BF16), 2 * flip).astype(F32)
        flip //= 2
    return [cells[0]]


def total_of(got):
    return sum(cells.astype(F32) for cells in got)


def local_kernel(kernel, outs, args, scratch=()):
    spaces = [
        pltpu.SMEM if a.dtype == jnp.int32 and a.size == 2 else pltpu.VMEM for a in args
    ]
    moved = sum(a.size * a.dtype.itemsize for a in args)
    return pl.pallas_call(
        kernel,
        out_shape=outs,
        in_specs=[pl.BlockSpec(memory_space=s) for s in spaces],
        out_specs=[pl.BlockSpec(memory_space=pltpu.VMEM)] * len(outs),
        scratch_shapes=list(scratch),
        compiler_params=pltpu.CompilerParams(vmem_limit_bytes=VMEM_LIMIT),
        cost_estimate=pl.CostEstimate(flops=0, bytes_accessed=moved, transcendentals=0),
    )(*args)


def lane_assemble_kernel(cells, got, where, full):
    for d in range(4):
        z = where[0] ^ d
        mine = pl.multiple_of((2 * z + where[1]) * 128, 128)
        theirs = pl.multiple_of((2 * z + 1 - where[1]) * 128, 128)
        full[:, pl.ds(mine, 128)] = cells[d]
        full[:, pl.ds(theirs, 128)] = got[d]


def lane_split_kernel(full, where, kept, sent):
    for d in range(4):
        z = where[0] ^ d
        mine = pl.multiple_of((2 * z + where[1]) * 128, 128)
        theirs = pl.multiple_of((2 * z + 1 - where[1]) * 128, 128)
        kept[d] = full[:, pl.ds(mine, 128)]
        sent[d] = full[:, pl.ds(theirs, 128)]


def row_assemble_kernel(cells, got, where, full):
    for d in range(4):
        z = where[0] ^ d
        full[2 * z + where[1]] = cells[d]
        full[2 * z + 1 - where[1]] = got[d]


def row_split_kernel(full, where, kept, sent):
    for d in range(4):
        z = where[0] ^ d
        kept[d] = full[2 * z + where[1]]
        sent[d] = full[2 * z + 1 - where[1]]


def turn_kernel(cells, *outs):
    turned = cells[...].astype(F32).T.astype(BF16)
    at = 0
    for out in outs:
        out[...] = turned[at : at + out.shape[0]]
        at += out.shape[0]


def turn_back_kernel(*refs):
    *parts, out, full = refs
    at = 0
    full[...] = jnp.zeros_like(full)
    for i in range(0, len(parts), 4):
        total = parts[i][...].astype(F32)
        for j in range(1, 4):
            total = total + parts[i + j][...].astype(F32)
        full[at : at + total.shape[0], :] = total
        at += total.shape[0]
    out[...] = full[...].T.astype(out.dtype)


def x_blocks(cells, got):
    high = (lax.axis_index("seq") & 1) == 1
    blocks = []
    for i in range(cells.shape[0]):
        blocks += [jnp.where(high, got[i], cells[i]), jnp.where(high, cells[i], got[i])]
    return blocks


def x_parts(blocks):
    high = (lax.axis_index("seq") & 1) == 1
    pairs = list(zip(blocks[::2], blocks[1::2]))
    kept = jnp.stack([jnp.where(high, b, a) for a, b in pairs])
    sent = jnp.stack([jnp.where(high, a, b) for a, b in pairs])
    return kept, sent


def assemble(cells, got):
    if direct():
        shape = like((cells.shape[1], D), BF16)
        return local_kernel(lane_assemble_kernel, [shape], (cells, got, place_of_device()))[0]
    return jnp.concatenate(x_blocks(cells, got), axis=-1)


def split(grad):
    count = lax.axis_size("seq")
    size = D // count
    if direct():
        shape = like((4, grad.shape[0], size), BF16)
        return local_kernel(lane_split_kernel, [shape, shape], (grad, place_of_device()))
    return x_parts([grad[:, i * size : (i + 1) * size] for i in range(count)])


def assemble_rows(cells, got):
    if direct():
        shape = like((8,) + cells.shape[1:], BF16)
        return local_kernel(row_assemble_kernel, [shape], (cells, got, place_of_device()))[0]
    return jnp.stack(x_blocks(cells, got))


def split_rows(cells):
    if direct():
        shape = like((4,) + cells.shape[1:], BF16)
        return local_kernel(row_split_kernel, [shape, shape], (cells, place_of_device()))
    return x_parts([cells[i] for i in range(cells.shape[0])])


def turn(cells, sizes):
    if direct():
        return local_kernel(turn_kernel, [like((n, cells.shape[0]), BF16) for n in sizes], (cells,))
    turned, outs, at = cells.T, [], 0
    for n in sizes:
        outs.append(turned[at : at + n])
        at += n
    return outs


def turn_back(chunks, width):
    if direct():
        lanes = chunks[0][0].shape[1]
        return local_kernel(
            turn_back_kernel,
            [like((lanes, width), BF16)],
            tuple(c for chunk in chunks for c in chunk),
            [pltpu.VMEM((width, lanes), F32)],
        )[0]
    turned = jnp.concatenate([total_of(c) for c in chunks], axis=0).T.astype(BF16)
    return jnp.pad(turned, ((0, 0), (0, width - turned.shape[1])))


def place(index, seq_lengths):
    count = seq_lengths.shape[0]
    ids = jnp.arange(count, dtype=jnp.int32)
    ends = jnp.sum(jnp.where(ids[None, :] <= ids[:, None], seq_lengths[None, :], 0), axis=1)
    starts = ends - seq_lengths
    segment = jnp.sum((index[:, None] >= ends[None, :]).astype(jnp.int32), axis=1)
    begins = jnp.sum(jnp.where(segment[:, None] == ids[None, :], starts[None, :], 0), axis=1)
    return segment, index - begins


def angles(position):
    freqs = 10000.0 ** (-(jnp.arange(HDIM // 2, dtype=F32) * 2.0) / HDIM)
    freqs = jnp.concatenate([freqs] * 4)
    turns = position.astype(F32)[:, None] * freqs[None, :]
    sign = jnp.where(jnp.arange(128) % HDIM < HDIM // 2, -1.0, 1.0)
    return jnp.cos(turns), jnp.sin(turns) * sign[None, :]


def normalize(values):
    average = jnp.mean(values, axis=-1, keepdims=True)
    centered = values - average
    variance = jnp.mean(centered * centered, axis=-1, keepdims=True)
    inverse = lax.rsqrt(variance + EPSILON)
    return centered * inverse, inverse


def norm_back(grad_hat, normed, inverse):
    return inverse * (
        grad_hat
        - jnp.mean(grad_hat, axis=-1, keepdims=True)
        - normed * jnp.mean(grad_hat * normed, axis=-1, keepdims=True)
    )


def geglu(gate_in, up_in):
    return jax.nn.gelu(gate_in, approximate=False) * up_in


def contract(left, right, dims, out=F32):
    return lax.dot_general(left, right, ((dims[0], dims[1]), ((), ())), preferred_element_type=out)


def rows_dot(left, right):
    return contract(left, right, ((0,), (0,)))


def cols_dot(left, right):
    return contract(left, right, ((1,), (1,)))


def half_swap(values):
    lane = lax.broadcasted_iota(jnp.int32, values.shape, 1)
    left = pltpu.roll(values, 128 - HDIM // 2, 1)
    right = pltpu.roll(values, HDIM // 2, 1)
    return jnp.where(lane % HDIM < HDIM // 2, left, right)


def bias_of(q_seg, k_seg, block):
    row = lax.broadcasted_iota(jnp.int32, (128, 256), 0)
    col = lax.broadcasted_iota(jnp.int32, (128, 256), 1)
    near = jnp.abs(row + HALF - col) <= HALF
    same = q_seg[pl.ds(block * 128, 128), :] == k_seg[:, pl.ds(block * 128, 256)]
    return jnp.where(near & same, 0.0, MASKED)


def softmax_of(scores):
    exponent = jnp.exp(scores - jnp.max(scores, axis=-1, keepdims=True))
    return exponent * (1.0 / jnp.sum(exponent, axis=-1, keepdims=True))


def attend_kernel(packed, cosine, sine, q_seg, k_seg, query, keys, values, attended, bias):
    rows = query.shape[0]
    blocks = rows // 128
    for b in range(blocks):
        bias[b] = bias_of(q_seg, k_seg, b)
    first = lax.broadcasted_iota(jnp.int32, (1, 128), 1) < HDIM
    for p in range(OWN_HEADS // 2):
        at = slice(p * 128, (p + 1) * 128)
        u = packed[HALF : HALF + rows, at]
        q_cos, q_sin = cosine[HALF : HALF + rows, :], sine[HALF : HALF + rows, :]
        query[:, at] = (u * q_cos + half_swap(u) * q_sin).astype(BF16)
        u = packed[:, OWN + p * 128 : OWN + (p + 1) * 128]
        keys[:, at] = (u * cosine[...] + half_swap(u) * sine[...]).astype(BF16)
        values[:, at] = packed[:, 2 * OWN + p * 128 : 2 * OWN + (p + 1) * 128].astype(BF16)
        for b in range(blocks):
            q = query[b * 128 : (b + 1) * 128, at]
            k = keys[b * 128 : b * 128 + 256, at]
            v = values[b * 128 : b * 128 + 256, at]
            outs = []
            for side in (first, ~first):
                q_one = jnp.where(side, q, jnp.zeros_like(q))
                scores = contract(q_one, k, ((1,), (1,))) * (HDIM**-0.5) + bias[b]
                prob = softmax_of(scores).astype(BF16)
                outs.append(contract(prob, v, ((1,), (0,))))
            attended[b * 128 : (b + 1) * 128, at] = jnp.where(first, outs[0], outs[1]).astype(BF16)


def attend_back_kernel(
    query, keys, values, grad, cosine, sine, q_seg, k_seg, grad_q, grad_k, grad_v, bias
):
    rows = query.shape[0]
    blocks = rows // 128
    scale = HDIM**-0.5
    for b in range(blocks):
        bias[b] = bias_of(q_seg, k_seg, b)
    first = lax.broadcasted_iota(jnp.int32, (1, 128), 1) < HDIM
    grad_k[...] = jnp.zeros_like(grad_k)
    grad_v[...] = jnp.zeros_like(grad_v)
    for p in range(OWN_HEADS // 2):
        at = slice(p * 128, (p + 1) * 128)
        for b in range(blocks):
            here, span = slice(b * 128, (b + 1) * 128), slice(b * 128, b * 128 + 256)
            q, go = query[here, at], grad[here, at]
            k, v = keys[span, at], values[span, at]
            d_q = jnp.zeros((128, 128), F32)
            d_k = jnp.zeros((256, 128), F32)
            d_v = jnp.zeros((256, 128), F32)
            for side in (first, ~first):
                q_one = jnp.where(side, q, jnp.zeros_like(q))
                k_one = jnp.where(side, k, jnp.zeros_like(k))
                go_one = jnp.where(side, go, jnp.zeros_like(go))
                scores = contract(q_one, k, ((1,), (1,))) * scale + bias[b]
                prob = softmax_of(scores)
                grad_prob = contract(go_one, v, ((1,), (1,)))
                inner = jnp.sum(grad_prob * prob, axis=-1, keepdims=True)
                grad_scores = (prob * (grad_prob - inner)).astype(BF16)
                d_q = d_q + contract(grad_scores, k_one, ((1,), (0,)))
                d_k = d_k + contract(grad_scores, q_one, ((0,), (0,)))
                d_v = d_v + contract(prob.astype(BF16), go_one, ((0,), (0,)))
            d_q = d_q * scale
            at_q = slice(HALF + b * 128, HALF + (b + 1) * 128)
            turned = d_q * cosine[at_q, :] - half_swap(d_q) * sine[at_q, :]
            grad_q[here, at] = turned.astype(BF16)
            grad_k[span, at] += d_k * scale
            grad_v[span, at] += d_v
        d_k = grad_k[:, at]
        grad_k[:, at] = d_k * cosine[...] - half_swap(d_k) * sine[...]


def call_kernel(kernel, outs, blocks, flops, args):
    moved = sum(a.size * a.dtype.itemsize for a in args) + sum(
        o.size * o.dtype.itemsize for o in outs
    )
    return pl.pallas_call(
        kernel,
        out_shape=outs,
        in_specs=[pl.BlockSpec(memory_space=pltpu.VMEM)] * len(args),
        out_specs=[pl.BlockSpec(memory_space=pltpu.VMEM)] * len(outs),
        scratch_shapes=[pltpu.VMEM((blocks, 128, 256), F32)],
        compiler_params=pltpu.CompilerParams(vmem_limit_bytes=VMEM_LIMIT),
        cost_estimate=pl.CostEstimate(flops=flops, bytes_accessed=moved, transcendentals=0),
    )(*args)


def like(shape, dtype):
    return jax.ShapeDtypeStruct(shape, dtype)


def on_device(
    tokens, cotangent, seq_lengths, w_qkv, w_attn_out, w_in, w_mlp_out, gain_attn, gain_mlp
):
    share = tokens.shape[0]
    rows = GROUP * share
    seq, seqs = lax.axis_index("seq"), lax.axis_size("seq")
    total = seqs * rows
    shard = w_qkv.shape[0]
    tie = lax.optimization_barrier

    gain_a = gain_attn.astype(F32)[:, None]
    gain_m = gain_mlp.astype(F32)[:, None]

    def columns(w, parts, width):
        cells = w.reshape(shard, parts, 2, 2, width).transpose(2, 3, 0, 1, 4)
        return cells.reshape(2, 2, shard, parts * width)

    def regroup(cells):
        cells = trade(trade(cells, "fy", 0), "core", 1)
        return cells.reshape(GROUP * shard, -1)

    attn_z = z_gather(w_attn_out)
    qkv = regroup(columns((w_qkv.astype(F32) * gain_a).astype(BF16), 3, OWN))
    (qkv,) = turn(qkv, (3 * OWN,))
    rest = jnp.concatenate(
        [
            columns(w_mlp_out, 1, OWN_FF),
            columns((w_in.astype(F32) * gain_m).astype(BF16), 2, OWN_FF),
            jnp.zeros((2, 2, shard, WIDE - 3 * OWN_FF), BF16),
        ],
        axis=-1,
    )
    ours = tokens.astype(F32)
    normed, inverse = normalize(ours)
    attn_z, qkv, rest, normed = tie((attn_z, qkv, rest, normed))
    qkv_z = z_gather(qkv)
    attn_x = send_seq(attn_z, 1)
    hidden = group_rows(normed.astype(BF16))
    mlp, gate, up = turn(regroup(rest), (OWN_FF,) * 3)
    qkv_z, attn_x, hidden, mlp, gate, up = tie((qkv_z, attn_x, hidden, mlp, gate, up))
    mlp_z = z_gather(mlp)
    qkv_x = send_seq(qkv_z, 1)
    ahead = [(i, i + 1) for i in range(seqs - 1)]
    behind = [(i + 1, i) for i in range(seqs - 1)]
    before = lax.ppermute(hidden[rows - HALF :], "seq", ahead)
    after = lax.ppermute(hidden[:HALF], "seq", behind)
    attn = assemble_rows(attn_z, attn_x).reshape(2, 2, seqs // 4, shard, D)
    attn = trade(trade(attn, "fy", 0), "core", 1)
    attn_full = attn.transpose(2, 0, 1, 3, 4).reshape(OWN, D)
    mlp_z, qkv_x, before, after, attn_full, gate = tie((mlp_z, qkv_x, before, after, attn_full, gate))
    gate_z = z_gather(gate)
    mlp_x = send_seq(mlp_z, 1)
    qkv_full = assemble(qkv_z, qkv_x)
    wide = jnp.concatenate([before, hidden, after], axis=0)
    index = seq * rows - HALF + jnp.arange(rows + 2 * HALF, dtype=jnp.int32)
    segment, position = place(jnp.clip(index, 0, total - 1), seq_lengths)
    segment = jnp.where((index >= 0) & (index < total), segment, -1)
    q_seg = segment[HALF : HALF + rows][:, None]
    k_seg = segment[None, :]
    cosine, sine = angles(position)
    packed = cols_dot(wide, qkv_full)
    blocks = rows // 128
    flops = blocks * OWN_HEADS * 128 * 256 * 128 * 4
    query, keys, values, attended = call_kernel(
        attend_kernel,
        [
            like((rows, OWN), BF16),
            like((rows + 2 * HALF, OWN), BF16),
            like((rows + 2 * HALF, OWN), BF16),
            like((rows, OWN), BF16),
        ],
        blocks,
        flops,
        (packed, cosine, sine, q_seg, k_seg),
    )
    part = jnp.dot(attended, attn_full, preferred_element_type=F32)
    middle = ours + group_sum(part, share)
    gate_z, mlp_x, middle, up = tie((gate_z, mlp_x, middle, up))
    up_z = z_gather(up)
    gate_x = send_seq(gate_z, 1)
    normed_mid, inverse_mid = normalize(middle)
    lifted = group_rows(normed_mid.astype(BF16))
    cot = group_rows(cotangent)
    mlp_full = assemble(mlp_z, mlp_x)
    grad_mixed = cols_dot(cot, mlp_full)
    up_z, gate_x, lifted, grad_mixed = tie((up_z, gate_x, lifted, grad_mixed))
    up_x = send_seq(up_z, 1)
    gate_full = assemble(gate_z, gate_x)
    gate = cols_dot(lifted, gate_full)
    up_x, gate = tie((up_x, gate))
    up_full = assemble(up_z, up_x)
    up = cols_dot(lifted, up_full)
    mixed = geglu(gate, up).astype(BF16)

    unused, gelu_back = jax.vjp(geglu, gate, up)
    grad_gate, grad_up = gelu_back(grad_mixed)
    grad_gate, grad_up = grad_gate.astype(BF16), grad_up.astype(BF16)
    mlp_kept, mlp_sent = split(rows_dot(mixed, cot).astype(BF16))
    mlp_kept, mlp_sent, grad_gate, grad_up = tie((mlp_kept, mlp_sent, grad_gate, grad_up))
    mlp_x = send_seq(mlp_sent, 1)
    part_lifted = jnp.dot(grad_gate, gate_full, preferred_element_type=F32) + jnp.dot(
        grad_up, up_full, preferred_element_type=F32
    )
    grad_hat = group_sum(part_lifted, share)
    gate_kept, gate_sent = split(rows_dot(grad_gate, lifted).astype(BF16))
    mlp_x, gate_sent, grad_hat = tie((mlp_x, gate_sent, grad_hat))
    mlp_got = z_spread(x_sum(mlp_kept, mlp_x))
    gate_x = send_seq(gate_sent, 1)
    grad_middle = cotangent.astype(F32) + norm_back(grad_hat, normed_mid, inverse_mid)
    grad_attn = group_rows(grad_middle.astype(BF16))
    up_kept, up_sent = split(rows_dot(grad_up, lifted).astype(BF16))
    grad_attended = cols_dot(grad_attn, attn_full).astype(BF16)
    grad_q, grad_k, grad_v = call_kernel(
        attend_back_kernel,
        [
            like((rows, OWN), BF16),
            like((rows + 2 * HALF, OWN), F32),
            like((rows + 2 * HALF, OWN), F32),
        ],
        blocks,
        flops * 3,
        (query, keys, values, grad_attended, cosine, sine, q_seg, k_seg),
    )
    grad_kv = jnp.concatenate([grad_k, grad_v], axis=1)
    mlp_got, gate_x, up_sent, grad_kv, attended = tie((mlp_got, gate_x, up_sent, grad_kv, attended))
    low_edge = lax.ppermute(grad_kv[:HALF].astype(BF16), "seq", behind)
    high_edge = lax.ppermute(grad_kv[HALF + rows :].astype(BF16), "seq", ahead)
    gate_got = z_spread(x_sum(gate_kept, gate_x))
    up_x = send_seq(up_sent, 1)
    attn_g = rows_dot(attended, grad_attn).astype(BF16)
    attn_g = attn_g.reshape(seqs // 4, 2, 2, shard, D).transpose(1, 2, 0, 3, 4)
    attn_g = trade(trade(attn_g, "core", 1), "fy", 0).reshape(seqs, shard, D)
    attn_kept, attn_sent = split_rows(attn_g)
    middle_kv = grad_kv[HALF : HALF + rows]
    gap = jnp.zeros((rows - 2 * HALF, 2 * OWN), F32)
    edges = jnp.concatenate([high_edge.astype(F32), gap, low_edge.astype(F32)], axis=0)
    grad_packed = jnp.concatenate([grad_q, (middle_kv + edges).astype(BF16)], axis=1)
    qkv_kept, qkv_sent = split(rows_dot(grad_packed, hidden).astype(BF16))
    gate_got, up_x, attn_sent, qkv_sent, mixed = tie((gate_got, up_x, attn_sent, qkv_sent, mixed))
    up_got = z_spread(x_sum(up_kept, up_x))
    qkv_x = send_seq(qkv_sent, 1)
    attn_x = send_seq(attn_sent, 1)
    part_hidden = jnp.dot(grad_packed, qkv_full, preferred_element_type=F32)
    grad_hidden = group_sum(part_hidden, share)
    part_out = jnp.dot(mixed, mlp_full, preferred_element_type=F32)
    output = middle + group_sum(part_out, share)
    up_got, qkv_x, attn_x, grad_hidden, output = tie((up_got, qkv_x, attn_x, grad_hidden, output))
    qkv_got = z_spread(x_sum(qkv_kept, qkv_x))
    grad_attn_out = total_of(z_spread(x_sum(attn_kept, attn_x)))

    def regroup_back(cells):
        cells = cells.reshape(2, 2, shard, -1)
        return trade(trade(cells, "fy", 0), "core", 1)

    def back_columns(cells, parts, width):
        cells = cells.reshape(2, 2, shard, parts, width).transpose(2, 3, 0, 1, 4)
        return cells.reshape(shard, parts * 2 * 2 * width).astype(F32)

    rest_g = regroup_back(turn_back([mlp_got, gate_got, up_got], WIDE))
    raw_mlp = back_columns(rest_g[..., :OWN_FF], 1, OWN_FF)
    raw_in = back_columns(rest_g[..., OWN_FF : 3 * OWN_FF], 2, OWN_FF)
    raw_qkv = back_columns(regroup_back(turn_back([qkv_got], 3 * OWN)), 3, OWN)
    input_grad = grad_middle + norm_back(grad_hidden, normed, inverse)
    grad_gain_attn = jnp.sum(raw_qkv * w_qkv.astype(F32), axis=1)
    grad_gain_mlp = jnp.sum(raw_in * w_in.astype(F32), axis=1)
    return (
        output.astype(BF16),
        input_grad,
        raw_qkv * gain_a,
        grad_attn_out,
        raw_in * gain_m,
        raw_mlp,
        grad_gain_attn,
        grad_gain_mlp,
    )


def solution(mesh):
    split = Mesh(mesh.devices.reshape(mesh.shape["seq"], -1, 2), ALL)
    two, one = P(ALL, None), P(ALL)
    return jax.shard_map(
        on_device,
        mesh=split,
        in_specs=(two, two, P(), two, two, two, two, one, one),
        out_specs=(two, two, two, two, two, two, one, one),
        check_vma=False,
    )
```

```python
import jax
import jax.numpy as jnp
from jax import lax
from jax.experimental import pallas as pl
from jax.experimental.pallas import tpu as pltpu
from jax.sharding import Mesh, PartitionSpec as P

D = 1024
HEADS = 16
HDIM = 64
FF = 2624
HALF = 64
GROUP = 4
OWN_HEADS = HEADS // GROUP
OWN = OWN_HEADS * HDIM
OWN_FF = FF // GROUP
WIDE = 2048
VMEM_LIMIT = 48 * 1024 * 1024

EPSILON = 1e-05
MASKED = -1e30
ALL = ("seq", "fy", "core")
BF16 = jnp.bfloat16
F32 = jnp.float32


def flat_pairs(change):
    count = lax.axis_size(ALL)
    return [(i, change(i)) for i in range(count)]


def send_seq(cells, flip):
    return lax.ppermute(cells, ALL, flat_pairs(lambda i: i ^ (flip * GROUP)))


def trade(cells, axis, dim):
    me = lax.axis_index(axis)
    kept = lax.dynamic_slice_in_dim(cells, me, 1, axis=dim)
    sent = lax.dynamic_slice_in_dim(cells, 1 - me, 1, axis=dim)
    got = lax.ppermute(sent, axis, [(0, 1), (1, 0)])
    low = me == 0
    return jnp.concatenate([jnp.where(low, kept, got), jnp.where(low, got, kept)], axis=dim)


def join(cells, axis, dim):
    me = lax.axis_index(axis)
    got = lax.ppermute(cells, axis, [(0, 1), (1, 0)])
    low = me == 0
    return jnp.stack([jnp.where(low, cells, got), jnp.where(low, got, cells)], axis=dim)


def reduce_pair(cells, axis, dim):
    me = lax.axis_index(axis)
    kept = lax.dynamic_index_in_dim(cells, me, dim, keepdims=False)
    sent = lax.dynamic_index_in_dim(cells, 1 - me, dim, keepdims=False).astype(BF16)
    got = lax.ppermute(sent, axis, [(0, 1), (1, 0)])
    return kept.astype(F32) + got.astype(F32)


def core_rows(cells):
    return join(cells, "core", 1).reshape((-1,) + cells.shape[2:])


def group_rows(cells):
    return core_rows(join(cells, "fy", 0))


def group_sum(part, rows):
    cells = part.reshape(2, 2, rows, part.shape[-1])
    return reduce_pair(reduce_pair(cells, "core", 1), "fy", 0)


def depth_of():
    return lax.axis_size("seq") // 2


def direct():
    return lax.axis_size("seq") == 8


def place_of_device():
    seq = lax.axis_index("seq")
    return jnp.stack([seq >> 1, seq & 1]).astype(jnp.int32)


def z_gather(cells):
    if direct():
        return jnp.stack([cells] + [send_seq(cells, 2 * d) for d in range(1, 4)])
    cells, me = cells[None], lax.axis_index("seq") >> 1
    flip = 1
    while flip < depth_of():
        other = send_seq(cells, 2 * flip)
        high = (me & flip) != 0
        cells = jnp.concatenate([jnp.where(high, other, cells), jnp.where(high, cells, other)])
        flip *= 2
    return cells


def x_sum(kept, got):
    return (kept.astype(F32) + got.astype(F32)).astype(BF16)


def z_spread(cells):
    if direct():
        return [cells[0]] + [send_seq(cells[d], 2 * d) for d in range(1, 4)]
    flip, me = depth_of() // 2, lax.axis_index("seq") >> 1
    while flip:
        high = ((me & flip) != 0).astype(jnp.int32)
        kept = lax.dynamic_slice_in_dim(cells, high * flip, flip, 0)
        sent = lax.dynamic_slice_in_dim(cells, (1 - high) * flip, flip, 0)
        cells = kept.astype(F32) + send_seq(sent.astype(BF16), 2 * flip).astype(F32)
        flip //= 2
    return [cells[0]]


def total_of(got):
    return sum(cells.astype(F32) for cells in got)


def local_kernel(kernel, outs, args, scratch=()):
    spaces = [
        pltpu.SMEM if a.dtype == jnp.int32 and a.size == 2 else pltpu.VMEM for a in args
    ]
    moved = sum(a.size * a.dtype.itemsize for a in args)
    return pl.pallas_call(
        kernel,
        out_shape=outs,
        in_specs=[pl.BlockSpec(memory_space=s) for s in spaces],
        out_specs=[pl.BlockSpec(memory_space=pltpu.VMEM)] * len(outs),
        scratch_shapes=list(scratch),
        compiler_params=pltpu.CompilerParams(vmem_limit_bytes=VMEM_LIMIT),
        cost_estimate=pl.CostEstimate(flops=0, bytes_accessed=moved, transcendentals=0),
    )(*args)


def lane_assemble_kernel(cells, got, where, full):
    for d in range(4):
        z = where[0] ^ d
        mine = pl.multiple_of((2 * z + where[1]) * 128, 128)
        theirs = pl.multiple_of((2 * z + 1 - where[1]) * 128, 128)
        full[:, pl.ds(mine, 128)] = cells[d]
        full[:, pl.ds(theirs, 128)] = got[d]


def lane_split_kernel(full, where, kept, sent):
    for d in range(4):
        z = where[0] ^ d
        mine = pl.multiple_of((2 * z + where[1]) * 128, 128)
        theirs = pl.multiple_of((2 * z + 1 - where[1]) * 128, 128)
        kept[d] = full[:, pl.ds(mine, 128)]
        sent[d] = full[:, pl.ds(theirs, 128)]


def row_assemble_kernel(cells, got, where, full):
    for d in range(4):
        z = where[0] ^ d
        full[2 * z + where[1]] = cells[d]
        full[2 * z + 1 - where[1]] = got[d]


def row_split_kernel(full, where, kept, sent):
    for d in range(4):
        z = where[0] ^ d
        kept[d] = full[2 * z + where[1]]
        sent[d] = full[2 * z + 1 - where[1]]


def turn_kernel(cells, *outs):
    turned = cells[...].astype(F32).T.astype(BF16)
    at = 0
    for out in outs:
        out[...] = turned[at : at + out.shape[0]]
        at += out.shape[0]


def turn_back_kernel(*refs):
    *parts, out, full = refs
    at = 0
    full[...] = jnp.zeros_like(full)
    for i in range(0, len(parts), 4):
        total = parts[i][...].astype(F32)
        for j in range(1, 4):
            total = total + parts[i + j][...].astype(F32)
        full[at : at + total.shape[0], :] = total
        at += total.shape[0]
    out[...] = full[...].T.astype(out.dtype)


def x_blocks(cells, got):
    high = (lax.axis_index("seq") & 1) == 1
    blocks = []
    for i in range(cells.shape[0]):
        blocks += [jnp.where(high, got[i], cells[i]), jnp.where(high, cells[i], got[i])]
    return blocks


def x_parts(blocks):
    high = (lax.axis_index("seq") & 1) == 1
    pairs = list(zip(blocks[::2], blocks[1::2]))
    kept = jnp.stack([jnp.where(high, b, a) for a, b in pairs])
    sent = jnp.stack([jnp.where(high, a, b) for a, b in pairs])
    return kept, sent


def assemble(cells, got):
    if direct():
        shape = like((cells.shape[1], D), BF16)
        return local_kernel(lane_assemble_kernel, [shape], (cells, got, place_of_device()))[0]
    return jnp.concatenate(x_blocks(cells, got), axis=-1)


def split(grad):
    count = lax.axis_size("seq")
    size = D // count
    if direct():
        shape = like((4, grad.shape[0], size), BF16)
        return local_kernel(lane_split_kernel, [shape, shape], (grad, place_of_device()))
    return x_parts([grad[:, i * size : (i + 1) * size] for i in range(count)])


def assemble_rows(cells, got):
    if direct():
        shape = like((8,) + cells.shape[1:], BF16)
        return local_kernel(row_assemble_kernel, [shape], (cells, got, place_of_device()))[0]
    return jnp.stack(x_blocks(cells, got))


def split_rows(cells):
    if direct():
        shape = like((4,) + cells.shape[1:], BF16)
        return local_kernel(row_split_kernel, [shape, shape], (cells, place_of_device()))
    return x_parts([cells[i] for i in range(cells.shape[0])])


def turn(cells, sizes):
    if direct():
        return local_kernel(turn_kernel, [like((n, cells.shape[0]), BF16) for n in sizes], (cells,))
    turned, outs, at = cells.T, [], 0
    for n in sizes:
        outs.append(turned[at : at + n])
        at += n
    return outs


def turn_back(chunks, width):
    if direct():
        lanes = chunks[0][0].shape[1]
        return local_kernel(
            turn_back_kernel,
            [like((lanes, width), BF16)],
            tuple(c for chunk in chunks for c in chunk),
            [pltpu.VMEM((width, lanes), F32)],
        )[0]
    turned = jnp.concatenate([total_of(c) for c in chunks], axis=0).T.astype(BF16)
    return jnp.pad(turned, ((0, 0), (0, width - turned.shape[1])))


def place(index, seq_lengths):
    count = seq_lengths.shape[0]
    ids = jnp.arange(count, dtype=jnp.int32)
    ends = jnp.sum(jnp.where(ids[None, :] <= ids[:, None], seq_lengths[None, :], 0), axis=1)
    starts = ends - seq_lengths
    segment = jnp.sum((index[:, None] >= ends[None, :]).astype(jnp.int32), axis=1)
    begins = jnp.sum(jnp.where(segment[:, None] == ids[None, :], starts[None, :], 0), axis=1)
    return segment, index - begins


def angles(position):
    freqs = 10000.0 ** (-(jnp.arange(HDIM // 2, dtype=F32) * 2.0) / HDIM)
    freqs = jnp.concatenate([freqs] * 4)
    turns = position.astype(F32)[:, None] * freqs[None, :]
    sign = jnp.where(jnp.arange(128) % HDIM < HDIM // 2, -1.0, 1.0)
    return jnp.cos(turns), jnp.sin(turns) * sign[None, :]


def normalize(values):
    average = jnp.mean(values, axis=-1, keepdims=True)
    centered = values - average
    variance = jnp.mean(centered * centered, axis=-1, keepdims=True)
    inverse = lax.rsqrt(variance + EPSILON)
    return centered * inverse, inverse


def norm_back(grad_hat, normed, inverse):
    return inverse * (
        grad_hat
        - jnp.mean(grad_hat, axis=-1, keepdims=True)
        - normed * jnp.mean(grad_hat * normed, axis=-1, keepdims=True)
    )


def geglu(gate_in, up_in):
    return jax.nn.gelu(gate_in, approximate=False) * up_in


def contract(left, right, dims, out=F32):
    return lax.dot_general(left, right, ((dims[0], dims[1]), ((), ())), preferred_element_type=out)


def rows_dot(left, right):
    return contract(left, right, ((0,), (0,)))


def cols_dot(left, right):
    return contract(left, right, ((1,), (1,)))


def half_swap(values):
    lane = lax.broadcasted_iota(jnp.int32, values.shape, 1)
    left = pltpu.roll(values, 128 - HDIM // 2, 1)
    right = pltpu.roll(values, HDIM // 2, 1)
    return jnp.where(lane % HDIM < HDIM // 2, left, right)


def bias_of(q_seg, k_seg, block):
    row = lax.broadcasted_iota(jnp.int32, (128, 256), 0)
    col = lax.broadcasted_iota(jnp.int32, (128, 256), 1)
    near = jnp.abs(row + HALF - col) <= HALF
    same = q_seg[pl.ds(block * 128, 128), :] == k_seg[:, pl.ds(block * 128, 256)]
    return jnp.where(near & same, 0.0, MASKED)


def softmax_of(scores):
    exponent = jnp.exp(scores - jnp.max(scores, axis=-1, keepdims=True))
    return exponent * (1.0 / jnp.sum(exponent, axis=-1, keepdims=True))


def attend_kernel(packed, cosine, sine, q_seg, k_seg, query, keys, values, attended, bias):
    rows = query.shape[0]
    blocks = rows // 128
    for b in range(blocks):
        bias[b] = bias_of(q_seg, k_seg, b)
    first = lax.broadcasted_iota(jnp.int32, (1, 128), 1) < HDIM
    for p in range(OWN_HEADS // 2):
        at = slice(p * 128, (p + 1) * 128)
        u = packed[HALF : HALF + rows, at]
        q_cos, q_sin = cosine[HALF : HALF + rows, :], sine[HALF : HALF + rows, :]
        query[:, at] = (u * q_cos + half_swap(u) * q_sin).astype(BF16)
        u = packed[:, OWN + p * 128 : OWN + (p + 1) * 128]
        keys[:, at] = (u * cosine[...] + half_swap(u) * sine[...]).astype(BF16)
        values[:, at] = packed[:, 2 * OWN + p * 128 : 2 * OWN + (p + 1) * 128].astype(BF16)
        for b in range(blocks):
            q = query[b * 128 : (b + 1) * 128, at]
            k = keys[b * 128 : b * 128 + 256, at]
            v = values[b * 128 : b * 128 + 256, at]
            outs = []
            for side in (first, ~first):
                q_one = jnp.where(side, q, jnp.zeros_like(q))
                scores = contract(q_one, k, ((1,), (1,))) * (HDIM**-0.5) + bias[b]
                prob = softmax_of(scores).astype(BF16)
                outs.append(contract(prob, v, ((1,), (0,))))
            attended[b * 128 : (b + 1) * 128, at] = jnp.where(first, outs[0], outs[1]).astype(BF16)


def attend_back_kernel(
    query, keys, values, grad, cosine, sine, q_seg, k_seg, grad_q, grad_k, grad_v, bias
):
    rows = query.shape[0]
    blocks = rows // 128
    scale = HDIM**-0.5
    for b in range(blocks):
        bias[b] = bias_of(q_seg, k_seg, b)
    first = lax.broadcasted_iota(jnp.int32, (1, 128), 1) < HDIM
    grad_k[...] = jnp.zeros_like(grad_k)
    grad_v[...] = jnp.zeros_like(grad_v)
    for p in range(OWN_HEADS // 2):
        at = slice(p * 128, (p + 1) * 128)
        for b in range(blocks):
            here, span = slice(b * 128, (b + 1) * 128), slice(b * 128, b * 128 + 256)
            q, go = query[here, at], grad[here, at]
            k, v = keys[span, at], values[span, at]
            d_q = jnp.zeros((128, 128), F32)
            d_k = jnp.zeros((256, 128), F32)
            d_v = jnp.zeros((256, 128), F32)
            for side in (first, ~first):
                q_one = jnp.where(side, q, jnp.zeros_like(q))
                k_one = jnp.where(side, k, jnp.zeros_like(k))
                go_one = jnp.where(side, go, jnp.zeros_like(go))
                scores = contract(q_one, k, ((1,), (1,))) * scale + bias[b]
                prob = softmax_of(scores)
                grad_prob = contract(go_one, v, ((1,), (1,)))
                inner = jnp.sum(grad_prob * prob, axis=-1, keepdims=True)
                grad_scores = (prob * (grad_prob - inner)).astype(BF16)
                d_q = d_q + contract(grad_scores, k_one, ((1,), (0,)))
                d_k = d_k + contract(grad_scores, q_one, ((0,), (0,)))
                d_v = d_v + contract(prob.astype(BF16), go_one, ((0,), (0,)))
            d_q = d_q * scale
            at_q = slice(HALF + b * 128, HALF + (b + 1) * 128)
            turned = d_q * cosine[at_q, :] - half_swap(d_q) * sine[at_q, :]
            grad_q[here, at] = turned.astype(BF16)
            grad_k[span, at] += d_k * scale
            grad_v[span, at] += d_v
        d_k = grad_k[:, at]
        grad_k[:, at] = d_k * cosine[...] - half_swap(d_k) * sine[...]


def call_kernel(kernel, outs, blocks, flops, args):
    moved = sum(a.size * a.dtype.itemsize for a in args) + sum(
        o.size * o.dtype.itemsize for o in outs
    )
    return pl.pallas_call(
        kernel,
        out_shape=outs,
        in_specs=[pl.BlockSpec(memory_space=pltpu.VMEM)] * len(args),
        out_specs=[pl.BlockSpec(memory_space=pltpu.VMEM)] * len(outs),
        scratch_shapes=[pltpu.VMEM((blocks, 128, 256), F32)],
        compiler_params=pltpu.CompilerParams(vmem_limit_bytes=VMEM_LIMIT),
        cost_estimate=pl.CostEstimate(flops=flops, bytes_accessed=moved, transcendentals=0),
    )(*args)


def like(shape, dtype):
    return jax.ShapeDtypeStruct(shape, dtype)


def on_device(
    tokens, cotangent, seq_lengths, w_qkv, w_attn_out, w_in, w_mlp_out, gain_attn, gain_mlp
):
    share = tokens.shape[0]
    rows = GROUP * share
    seq, seqs = lax.axis_index("seq"), lax.axis_size("seq")
    total = seqs * rows
    shard = w_qkv.shape[0]
    tie = lax.optimization_barrier

    gain_a = gain_attn.astype(F32)[:, None]
    gain_m = gain_mlp.astype(F32)[:, None]

    def columns(w, parts, width):
        cells = w.reshape(shard, parts, 2, 2, width).transpose(2, 3, 0, 1, 4)
        return cells.reshape(2, 2, shard, parts * width)

    def regroup(cells):
        cells = trade(trade(cells, "fy", 0), "core", 1)
        return cells.reshape(GROUP * shard, -1)

    attn_z = z_gather(w_attn_out)
    qkv = regroup(columns((w_qkv.astype(F32) * gain_a).astype(BF16), 3, OWN))
    (qkv,) = turn(qkv, (3 * OWN,))
    rest = jnp.concatenate(
        [
            columns(w_mlp_out, 1, OWN_FF),
            columns((w_in.astype(F32) * gain_m).astype(BF16), 2, OWN_FF),
            jnp.zeros((2, 2, shard, WIDE - 3 * OWN_FF), BF16),
        ],
        axis=-1,
    )
    ours = tokens.astype(F32)
    normed, inverse = normalize(ours)
    hidden = normed.astype(BF16)
    devices = lax.axis_size(ALL)
    ahead = [(i, i + 1) for i in range(GROUP - 1, devices - 1, GROUP)]
    behind = [(i + 1, i) for i in range(GROUP - 1, devices - 1, GROUP)]
    edge = lax.ppermute(hidden[share - HALF :], ALL, ahead)
    edge = edge + lax.ppermute(hidden[:HALF], ALL, behind)
    attn_z, qkv, rest, hidden, edge = tie((attn_z, qkv, rest, hidden, edge))
    qkv_z = z_gather(qkv)
    attn_x = send_seq(attn_z, 1)
    hidden = group_rows(jnp.concatenate([hidden, edge], axis=0)).reshape(GROUP, share + HALF, D)
    before, after = hidden[0, share:], hidden[GROUP - 1, share:]
    hidden = hidden[:, :share].reshape(rows, D)
    mlp, gate, up = turn(regroup(rest), (OWN_FF,) * 3)
    wide = jnp.concatenate([before, hidden, after], axis=0)
    qkv_z, attn_x, wide, mlp, gate, up = tie((qkv_z, attn_x, wide, mlp, gate, up))
    hidden = wide[HALF : HALF + rows]
    mlp_z = z_gather(mlp)
    qkv_x = send_seq(qkv_z, 1)
    cot = group_rows(cotangent)
    attn = assemble_rows(attn_z, attn_x).reshape(2, 2, seqs // 4, shard, D)
    attn = trade(trade(attn, "fy", 0), "core", 1)
    attn_full = attn.transpose(2, 0, 1, 3, 4).reshape(OWN, D)
    mlp_z, qkv_x, attn_full, gate, cot = tie((mlp_z, qkv_x, attn_full, gate, cot))
    gate_z = z_gather(gate)
    mlp_x = send_seq(mlp_z, 1)
    qkv_full = assemble(qkv_z, qkv_x)
    index = seq * rows - HALF + jnp.arange(rows + 2 * HALF, dtype=jnp.int32)
    segment, position = place(jnp.clip(index, 0, total - 1), seq_lengths)
    segment = jnp.where((index >= 0) & (index < total), segment, -1)
    q_seg = segment[HALF : HALF + rows][:, None]
    k_seg = segment[None, :]
    cosine, sine = angles(position)
    packed = cols_dot(wide, qkv_full)
    blocks = rows // 128
    flops = blocks * OWN_HEADS * 128 * 256 * 128 * 4
    query, keys, values, attended = call_kernel(
        attend_kernel,
        [
            like((rows, OWN), BF16),
            like((rows + 2 * HALF, OWN), BF16),
            like((rows + 2 * HALF, OWN), BF16),
            like((rows, OWN), BF16),
        ],
        blocks,
        flops,
        (packed, cosine, sine, q_seg, k_seg),
    )
    part = jnp.dot(attended, attn_full, preferred_element_type=F32)
    gate_z, mlp_x, part, up = tie((gate_z, mlp_x, part, up))
    up_z = z_gather(up)
    gate_x = send_seq(gate_z, 1)
    middle = ours + group_sum(part, share)
    mlp_full = assemble(mlp_z, mlp_x)
    grad_mixed = cols_dot(cot, mlp_full)
    up_z, gate_x, middle, grad_mixed = tie((up_z, gate_x, middle, grad_mixed))
    up_x = send_seq(up_z, 1)
    normed_mid, inverse_mid = normalize(middle)
    lifted = join(normed_mid.astype(BF16), "fy", 0)
    gate_full = assemble(gate_z, gate_x)
    up_x, lifted, gate_full = tie((up_x, lifted, gate_full))
    lifted = core_rows(lifted)
    gate = cols_dot(lifted, gate_full)
    up_full = assemble(up_z, up_x)
    up = cols_dot(lifted, up_full)
    mixed = geglu(gate, up).astype(BF16)

    unused, gelu_back = jax.vjp(geglu, gate, up)
    grad_gate, grad_up = gelu_back(grad_mixed)
    grad_gate, grad_up = grad_gate.astype(BF16), grad_up.astype(BF16)
    mlp_kept, mlp_sent = split(rows_dot(mixed, cot).astype(BF16))
    mlp_kept, mlp_sent, grad_gate, grad_up = tie((mlp_kept, mlp_sent, grad_gate, grad_up))
    mlp_x = send_seq(mlp_sent, 1)
    part_lifted = jnp.dot(grad_gate, gate_full, preferred_element_type=F32) + jnp.dot(
        grad_up, up_full, preferred_element_type=F32
    )
    grad_hat = group_sum(part_lifted, share)
    gate_kept, gate_sent = split(rows_dot(grad_gate, lifted).astype(BF16))
    up_kept, up_sent = split(rows_dot(grad_up, lifted).astype(BF16))
    mlp_x, gate_sent, up_sent, grad_hat = tie((mlp_x, gate_sent, up_sent, grad_hat))
    mlp_got = z_spread(x_sum(mlp_kept, mlp_x))
    gate_x = send_seq(gate_sent, 1)
    grad_middle = cotangent.astype(F32) + norm_back(grad_hat, normed_mid, inverse_mid)
    grad_attn = join(grad_middle.astype(BF16), "fy", 0)
    mlp_got, gate_x, grad_attn, grad_up, attended = tie((mlp_got, gate_x, grad_attn, grad_up, attended))
    gate_got = z_spread(x_sum(gate_kept, gate_x))
    up_x = send_seq(up_sent, 1)
    grad_attn = core_rows(grad_attn)
    grad_attended = cols_dot(grad_attn, attn_full).astype(BF16)
    grad_q, grad_k, grad_v = call_kernel(
        attend_back_kernel,
        [
            like((rows, OWN), BF16),
            like((rows + 2 * HALF, OWN), F32),
            like((rows + 2 * HALF, OWN), F32),
        ],
        blocks,
        flops * 3,
        (query, keys, values, grad_attended, cosine, sine, q_seg, k_seg),
    )
    grad_kv = jnp.concatenate([grad_k, grad_v], axis=1)
    attn_g = rows_dot(attended, grad_attn).astype(BF16)
    attn_g = attn_g.reshape(seqs // 4, 2, 2, shard, D).transpose(1, 2, 0, 3, 4)
    part_out = jnp.dot(mixed, mlp_full, preferred_element_type=F32)
    gate_got, up_x, grad_kv, attn_g, part_out = tie((gate_got, up_x, grad_kv, attn_g, part_out))
    up_got = z_spread(x_sum(up_kept, up_x))
    ahead = [(i, i + 1) for i in range(seqs - 1)]
    behind = [(i + 1, i) for i in range(seqs - 1)]
    low_edge = lax.ppermute(grad_kv[:HALF].astype(BF16), "seq", behind)
    high_edge = lax.ppermute(grad_kv[HALF + rows :].astype(BF16), "seq", ahead)
    attn_g = trade(trade(attn_g, "core", 1), "fy", 0).reshape(seqs, shard, D)
    attn_kept, attn_sent = split_rows(attn_g)
    middle_kv = grad_kv[HALF : HALF + rows]
    gap = jnp.zeros((rows - 2 * HALF, 2 * OWN), F32)
    edges = jnp.concatenate([high_edge.astype(F32), gap, low_edge.astype(F32)], axis=0)
    grad_packed = jnp.concatenate([grad_q, (middle_kv + edges).astype(BF16)], axis=1)
    qkv_kept, qkv_sent = split(rows_dot(grad_packed, hidden).astype(BF16))
    attn_sent, qkv_sent, grad_packed = tie((attn_sent, qkv_sent, grad_packed))
    qkv_x = send_seq(qkv_sent, 1)
    attn_x = send_seq(attn_sent, 1)
    part_hidden = jnp.dot(grad_packed, qkv_full, preferred_element_type=F32)
    parts = jnp.stack([part_hidden, part_out]).reshape(2, 2, 2, share, D)
    parts = reduce_pair(parts, "core", 2)
    up_got, qkv_x, attn_x, parts = tie((up_got, qkv_x, attn_x, parts))
    qkv_got = z_spread(x_sum(qkv_kept, qkv_x))
    grad_attn_out = total_of(z_spread(x_sum(attn_kept, attn_x)))
    grad_hidden, sum_out = reduce_pair(parts, "fy", 1)
    output = middle + sum_out

    def regroup_back(cells):
        cells = cells.reshape(2, 2, shard, -1)
        return trade(trade(cells, "fy", 0), "core", 1)

    def back_columns(cells, parts, width):
        cells = cells.reshape(2, 2, shard, parts, width).transpose(2, 3, 0, 1, 4)
        return cells.reshape(shard, parts * 2 * 2 * width).astype(F32)

    rest_g = regroup_back(turn_back([mlp_got, gate_got, up_got], WIDE))
    raw_mlp = back_columns(rest_g[..., :OWN_FF], 1, OWN_FF)
    raw_in = back_columns(rest_g[..., OWN_FF : 3 * OWN_FF], 2, OWN_FF)
    output, rest_g, raw_in, raw_mlp, qkv_got = tie((output, rest_g, raw_in, raw_mlp, qkv_got))
    raw_qkv = back_columns(regroup_back(turn_back([qkv_got], 3 * OWN)), 3, OWN)
    input_grad = grad_middle + norm_back(grad_hidden, normed, inverse)
    grad_gain_attn = jnp.sum(raw_qkv * w_qkv.astype(F32), axis=1)
    grad_gain_mlp = jnp.sum(raw_in * w_in.astype(F32), axis=1)
    return (
        output.astype(BF16),
        input_grad,
        raw_qkv * gain_a,
        grad_attn_out,
        raw_in * gain_m,
        raw_mlp,
        grad_gain_attn,
        grad_gain_mlp,
    )


def solution(mesh):
    split = Mesh(mesh.devices.reshape(mesh.shape["seq"], -1, 2), ALL)
    two, one = P(ALL, None), P(ALL)
    return jax.shard_map(
        on_device,
        mesh=split,
        in_specs=(two, two, P(), two, two, two, two, one, one),
        out_specs=(two, two, two, two, two, two, one, one),
        check_vma=False,
    )
```

```python
import jax
import jax.numpy as jnp
from jax import lax
from jax.experimental import pallas as pl
from jax.experimental.pallas import tpu as pltpu
from jax.sharding import Mesh, PartitionSpec as P

D = 1024
HEADS = 16
HDIM = 64
FF = 2624
HALF = 64
GROUP = 4
OWN_HEADS = HEADS // GROUP
OWN = OWN_HEADS * HDIM
OWN_FF = FF // GROUP
WIDE = 2048
VMEM_LIMIT = 48 * 1024 * 1024

EPSILON = 1e-05
MASKED = -1e30
ALL = ("seq", "fy", "core")
BF16 = jnp.bfloat16
F32 = jnp.float32


def flat_pairs(change):
    count = lax.axis_size(ALL)
    return [(i, change(i)) for i in range(count)]


def send_seq(cells, flip):
    return lax.ppermute(cells, ALL, flat_pairs(lambda i: i ^ (flip * GROUP)))


def trade(cells, axis, dim):
    me = lax.axis_index(axis)
    kept = lax.dynamic_slice_in_dim(cells, me, 1, axis=dim)
    sent = lax.dynamic_slice_in_dim(cells, 1 - me, 1, axis=dim)
    got = lax.ppermute(sent, axis, [(0, 1), (1, 0)])
    low = me == 0
    return jnp.concatenate([jnp.where(low, kept, got), jnp.where(low, got, kept)], axis=dim)


def join(cells, axis, dim):
    me = lax.axis_index(axis)
    got = lax.ppermute(cells, axis, [(0, 1), (1, 0)])
    low = me == 0
    return jnp.stack([jnp.where(low, cells, got), jnp.where(low, got, cells)], axis=dim)


def reduce_pair(cells, axis, dim):
    me = lax.axis_index(axis)
    kept = lax.dynamic_index_in_dim(cells, me, dim, keepdims=False)
    sent = lax.dynamic_index_in_dim(cells, 1 - me, dim, keepdims=False).astype(BF16)
    got = lax.ppermute(sent, axis, [(0, 1), (1, 0)])
    return kept.astype(F32) + got.astype(F32)


def core_rows(cells):
    return join(cells, "core", 1).reshape((-1,) + cells.shape[2:])


def group_rows(cells):
    return core_rows(join(cells, "fy", 0))


def group_sum(part, rows):
    cells = part.reshape(2, 2, rows, part.shape[-1])
    return reduce_pair(reduce_pair(cells, "core", 1), "fy", 0)


def depth_of():
    return lax.axis_size("seq") // 2


def direct():
    return lax.axis_size("seq") == 8


def place_of_device():
    seq = lax.axis_index("seq")
    return jnp.stack([seq >> 1, seq & 1]).astype(jnp.int32)


def z_gather(cells):
    if direct():
        return jnp.stack([cells] + [send_seq(cells, 2 * d) for d in range(1, 4)])
    cells, me = cells[None], lax.axis_index("seq") >> 1
    flip = 1
    while flip < depth_of():
        other = send_seq(cells, 2 * flip)
        high = (me & flip) != 0
        cells = jnp.concatenate([jnp.where(high, other, cells), jnp.where(high, cells, other)])
        flip *= 2
    return cells


def x_sum(kept, got):
    return (kept.astype(F32) + got.astype(F32)).astype(BF16)


def z_spread(cells):
    if direct():
        return [cells[0]] + [send_seq(cells[d], 2 * d) for d in range(1, 4)]
    flip, me = depth_of() // 2, lax.axis_index("seq") >> 1
    while flip:
        high = ((me & flip) != 0).astype(jnp.int32)
        kept = lax.dynamic_slice_in_dim(cells, high * flip, flip, 0)
        sent = lax.dynamic_slice_in_dim(cells, (1 - high) * flip, flip, 0)
        cells = kept.astype(F32) + send_seq(sent.astype(BF16), 2 * flip).astype(F32)
        flip //= 2
    return [cells[0]]


def total_of(got):
    return sum(cells.astype(F32) for cells in got)


def local_kernel(kernel, outs, args, scratch=()):
    spaces = [
        pltpu.SMEM if a.dtype == jnp.int32 and a.size == 2 else pltpu.VMEM for a in args
    ]
    moved = sum(a.size * a.dtype.itemsize for a in args)
    return pl.pallas_call(
        kernel,
        out_shape=outs,
        in_specs=[pl.BlockSpec(memory_space=s) for s in spaces],
        out_specs=[pl.BlockSpec(memory_space=pltpu.VMEM)] * len(outs),
        scratch_shapes=list(scratch),
        compiler_params=pltpu.CompilerParams(vmem_limit_bytes=VMEM_LIMIT),
        cost_estimate=pl.CostEstimate(flops=0, bytes_accessed=moved, transcendentals=0),
    )(*args)


def lane_assemble_kernel(cells, got, where, full):
    for d in range(4):
        z = where[0] ^ d
        mine = pl.multiple_of((2 * z + where[1]) * 128, 128)
        theirs = pl.multiple_of((2 * z + 1 - where[1]) * 128, 128)
        full[:, pl.ds(mine, 128)] = cells[d]
        full[:, pl.ds(theirs, 128)] = got[d]


def lane_split_kernel(full, where, kept, sent):
    for d in range(4):
        z = where[0] ^ d
        mine = pl.multiple_of((2 * z + where[1]) * 128, 128)
        theirs = pl.multiple_of((2 * z + 1 - where[1]) * 128, 128)
        kept[d] = full[:, pl.ds(mine, 128)]
        sent[d] = full[:, pl.ds(theirs, 128)]


def row_assemble_kernel(cells, got, where, full):
    for d in range(4):
        z = where[0] ^ d
        full[2 * z + where[1]] = cells[d]
        full[2 * z + 1 - where[1]] = got[d]


def row_split_kernel(full, where, kept, sent):
    for d in range(4):
        z = where[0] ^ d
        kept[d] = full[2 * z + where[1]]
        sent[d] = full[2 * z + 1 - where[1]]


def turn_kernel(cells, *outs):
    turned = cells[...].astype(F32).T.astype(BF16)
    at = 0
    for out in outs:
        out[...] = turned[at : at + out.shape[0]]
        at += out.shape[0]


def turn_back_kernel(*refs):
    *parts, out, full = refs
    at = 0
    full[...] = jnp.zeros_like(full)
    for i in range(0, len(parts), 4):
        total = parts[i][...].astype(F32)
        for j in range(1, 4):
            total = total + parts[i + j][...].astype(F32)
        full[at : at + total.shape[0], :] = total
        at += total.shape[0]
    out[...] = full[...].T.astype(out.dtype)


def x_blocks(cells, got):
    high = (lax.axis_index("seq") & 1) == 1
    blocks = []
    for i in range(cells.shape[0]):
        blocks += [jnp.where(high, got[i], cells[i]), jnp.where(high, cells[i], got[i])]
    return blocks


def x_parts(blocks):
    high = (lax.axis_index("seq") & 1) == 1
    pairs = list(zip(blocks[::2], blocks[1::2]))
    kept = jnp.stack([jnp.where(high, b, a) for a, b in pairs])
    sent = jnp.stack([jnp.where(high, a, b) for a, b in pairs])
    return kept, sent


def assemble(cells, got):
    if direct():
        shape = like((cells.shape[1], D), BF16)
        return local_kernel(lane_assemble_kernel, [shape], (cells, got, place_of_device()))[0]
    return jnp.concatenate(x_blocks(cells, got), axis=-1)


def split(grad):
    count = lax.axis_size("seq")
    size = D // count
    if direct():
        shape = like((4, grad.shape[0], size), BF16)
        return local_kernel(lane_split_kernel, [shape, shape], (grad, place_of_device()))
    return x_parts([grad[:, i * size : (i + 1) * size] for i in range(count)])


def assemble_rows(cells, got):
    if direct():
        shape = like((8,) + cells.shape[1:], BF16)
        return local_kernel(row_assemble_kernel, [shape], (cells, got, place_of_device()))[0]
    return jnp.stack(x_blocks(cells, got))


def split_rows(cells):
    if direct():
        shape = like((4,) + cells.shape[1:], BF16)
        return local_kernel(row_split_kernel, [shape, shape], (cells, place_of_device()))
    return x_parts([cells[i] for i in range(cells.shape[0])])


def turn(cells, sizes):
    if direct():
        return local_kernel(turn_kernel, [like((n, cells.shape[0]), BF16) for n in sizes], (cells,))
    turned, outs, at = cells.T, [], 0
    for n in sizes:
        outs.append(turned[at : at + n])
        at += n
    return outs


def turn_back(chunks, width):
    if direct():
        lanes = chunks[0][0].shape[1]
        return local_kernel(
            turn_back_kernel,
            [like((lanes, width), BF16)],
            tuple(c for chunk in chunks for c in chunk),
            [pltpu.VMEM((width, lanes), F32)],
        )[0]
    turned = jnp.concatenate([total_of(c) for c in chunks], axis=0).T.astype(BF16)
    return jnp.pad(turned, ((0, 0), (0, width - turned.shape[1])))


def place(index, seq_lengths):
    count = seq_lengths.shape[0]
    ids = jnp.arange(count, dtype=jnp.int32)
    ends = jnp.sum(jnp.where(ids[None, :] <= ids[:, None], seq_lengths[None, :], 0), axis=1)
    starts = ends - seq_lengths
    segment = jnp.sum((index[:, None] >= ends[None, :]).astype(jnp.int32), axis=1)
    begins = jnp.sum(jnp.where(segment[:, None] == ids[None, :], starts[None, :], 0), axis=1)
    return segment, index - begins


def angles(position):
    freqs = 10000.0 ** (-(jnp.arange(HDIM // 2, dtype=F32) * 2.0) / HDIM)
    freqs = jnp.concatenate([freqs] * 4)
    turns = position.astype(F32)[:, None] * freqs[None, :]
    sign = jnp.where(jnp.arange(128) % HDIM < HDIM // 2, -1.0, 1.0)
    return jnp.cos(turns), jnp.sin(turns) * sign[None, :]


def normalize(values):
    average = jnp.mean(values, axis=-1, keepdims=True)
    centered = values - average
    variance = jnp.mean(centered * centered, axis=-1, keepdims=True)
    inverse = lax.rsqrt(variance + EPSILON)
    return centered * inverse, inverse


def norm_back(grad_hat, normed, inverse):
    return inverse * (
        grad_hat
        - jnp.mean(grad_hat, axis=-1, keepdims=True)
        - normed * jnp.mean(grad_hat * normed, axis=-1, keepdims=True)
    )


def geglu(gate_in, up_in):
    return jax.nn.gelu(gate_in, approximate=False) * up_in


def contract(left, right, dims, out=F32):
    return lax.dot_general(left, right, ((dims[0], dims[1]), ((), ())), preferred_element_type=out)


def rows_dot(left, right):
    return contract(left, right, ((0,), (0,)))


def cols_dot(left, right):
    return contract(left, right, ((1,), (1,)))


def half_swap(values):
    lane = lax.broadcasted_iota(jnp.int32, values.shape, 1)
    left = pltpu.roll(values, 128 - HDIM // 2, 1)
    right = pltpu.roll(values, HDIM // 2, 1)
    return jnp.where(lane % HDIM < HDIM // 2, left, right)


def bias_of(q_seg, k_seg, block):
    row = lax.broadcasted_iota(jnp.int32, (128, 256), 0)
    col = lax.broadcasted_iota(jnp.int32, (128, 256), 1)
    near = jnp.abs(row + HALF - col) <= HALF
    same = q_seg[pl.ds(block * 128, 128), :] == k_seg[:, pl.ds(block * 128, 256)]
    return jnp.where(near & same, 0.0, MASKED)


def softmax_of(scores):
    exponent = jnp.exp(scores - jnp.max(scores, axis=-1, keepdims=True))
    return exponent * (1.0 / jnp.sum(exponent, axis=-1, keepdims=True))


def attend_kernel(packed, cosine, sine, q_seg, k_seg, query, keys, values, attended, bias):
    rows = query.shape[0]
    blocks = rows // 128
    for b in range(blocks):
        bias[b] = bias_of(q_seg, k_seg, b)
    first = lax.broadcasted_iota(jnp.int32, (1, 128), 1) < HDIM
    for p in range(OWN_HEADS // 2):
        at = slice(p * 128, (p + 1) * 128)
        u = packed[HALF : HALF + rows, at]
        q_cos, q_sin = cosine[HALF : HALF + rows, :], sine[HALF : HALF + rows, :]
        query[:, at] = (u * q_cos + half_swap(u) * q_sin).astype(BF16)
        u = packed[:, OWN + p * 128 : OWN + (p + 1) * 128]
        keys[:, at] = (u * cosine[...] + half_swap(u) * sine[...]).astype(BF16)
        values[:, at] = packed[:, 2 * OWN + p * 128 : 2 * OWN + (p + 1) * 128].astype(BF16)
        for b in range(blocks):
            q = query[b * 128 : (b + 1) * 128, at]
            k = keys[b * 128 : b * 128 + 256, at]
            v = values[b * 128 : b * 128 + 256, at]
            outs = []
            for side in (first, ~first):
                q_one = jnp.where(side, q, jnp.zeros_like(q))
                scores = contract(q_one, k, ((1,), (1,))) * (HDIM**-0.5) + bias[b]
                prob = softmax_of(scores).astype(BF16)
                outs.append(contract(prob, v, ((1,), (0,))))
            attended[b * 128 : (b + 1) * 128, at] = jnp.where(first, outs[0], outs[1]).astype(BF16)


def attend_back_kernel(
    query, keys, values, grad, cosine, sine, q_seg, k_seg, grad_q, grad_k, grad_v, bias
):
    rows = query.shape[0]
    blocks = rows // 128
    scale = HDIM**-0.5
    for b in range(blocks):
        bias[b] = bias_of(q_seg, k_seg, b)
    first = lax.broadcasted_iota(jnp.int32, (1, 128), 1) < HDIM
    grad_k[...] = jnp.zeros_like(grad_k)
    grad_v[...] = jnp.zeros_like(grad_v)
    for p in range(OWN_HEADS // 2):
        at = slice(p * 128, (p + 1) * 128)
        for b in range(blocks):
            here, span = slice(b * 128, (b + 1) * 128), slice(b * 128, b * 128 + 256)
            q, go = query[here, at], grad[here, at]
            k, v = keys[span, at], values[span, at]
            d_q = jnp.zeros((128, 128), F32)
            d_k = jnp.zeros((256, 128), F32)
            d_v = jnp.zeros((256, 128), F32)
            for side in (first, ~first):
                q_one = jnp.where(side, q, jnp.zeros_like(q))
                k_one = jnp.where(side, k, jnp.zeros_like(k))
                go_one = jnp.where(side, go, jnp.zeros_like(go))
                scores = contract(q_one, k, ((1,), (1,))) * scale + bias[b]
                prob = softmax_of(scores)
                grad_prob = contract(go_one, v, ((1,), (1,)))
                inner = jnp.sum(grad_prob * prob, axis=-1, keepdims=True)
                grad_scores = (prob * (grad_prob - inner)).astype(BF16)
                d_q = d_q + contract(grad_scores, k_one, ((1,), (0,)))
                d_k = d_k + contract(grad_scores, q_one, ((0,), (0,)))
                d_v = d_v + contract(prob.astype(BF16), go_one, ((0,), (0,)))
            d_q = d_q * scale
            at_q = slice(HALF + b * 128, HALF + (b + 1) * 128)
            turned = d_q * cosine[at_q, :] - half_swap(d_q) * sine[at_q, :]
            grad_q[here, at] = turned.astype(BF16)
            grad_k[span, at] += d_k * scale
            grad_v[span, at] += d_v
        d_k = grad_k[:, at]
        grad_k[:, at] = d_k * cosine[...] - half_swap(d_k) * sine[...]


def call_kernel(kernel, outs, blocks, flops, args):
    moved = sum(a.size * a.dtype.itemsize for a in args) + sum(
        o.size * o.dtype.itemsize for o in outs
    )
    return pl.pallas_call(
        kernel,
        out_shape=outs,
        in_specs=[pl.BlockSpec(memory_space=pltpu.VMEM)] * len(args),
        out_specs=[pl.BlockSpec(memory_space=pltpu.VMEM)] * len(outs),
        scratch_shapes=[pltpu.VMEM((blocks, 128, 256), F32)],
        compiler_params=pltpu.CompilerParams(vmem_limit_bytes=VMEM_LIMIT),
        cost_estimate=pl.CostEstimate(flops=flops, bytes_accessed=moved, transcendentals=0),
    )(*args)


def like(shape, dtype):
    return jax.ShapeDtypeStruct(shape, dtype)


def on_device(
    tokens, cotangent, seq_lengths, w_qkv, w_attn_out, w_in, w_mlp_out, gain_attn, gain_mlp
):
    share = tokens.shape[0]
    rows = GROUP * share
    seq, seqs = lax.axis_index("seq"), lax.axis_size("seq")
    total = seqs * rows
    shard = w_qkv.shape[0]
    tie = lax.optimization_barrier

    def close(first, last):
        first = tie(first)
        return tie((first, last))


    gain_a = gain_attn.astype(F32)[:, None]
    gain_m = gain_mlp.astype(F32)[:, None]

    def columns(w, parts, width):
        cells = w.reshape(shard, parts, 2, 2, width).transpose(2, 3, 0, 1, 4)
        return cells.reshape(2, 2, shard, parts * width)

    devices = lax.axis_size(ALL)
    ahead = [(i, i + 1) for i in range(GROUP - 1, devices - 1, GROUP)]
    behind = [(i + 1, i) for i in range(GROUP - 1, devices - 1, GROUP)]
    edge = lax.ppermute(tokens[share - HALF :], ALL, ahead)
    edge = edge + lax.ppermute(tokens[:HALF], ALL, behind)
    attn_z = z_gather(w_attn_out)
    qkv = trade(columns((w_qkv.astype(F32) * gain_a).astype(BF16), 3, OWN), "fy", 0)
    qkv = trade(qkv, "core", 1).reshape(GROUP * shard, -1)
    (qkv,) = turn(qkv, (3 * OWN,))
    rest = jnp.concatenate(
        [
            columns(w_mlp_out, 1, OWN_FF),
            columns((w_in.astype(F32) * gain_m).astype(BF16), 2, OWN_FF),
            jnp.zeros((2, 2, shard, WIDE - 3 * OWN_FF), BF16),
        ],
        axis=-1,
    )
    rest = trade(rest, "fy", 0)
    attn_z, qkv, rest, edge, cotangent_in = tie((attn_z, qkv, rest, edge, cotangent))
    qkv_z = z_gather(qkv)
    attn_x = send_seq(attn_z, 1)
    ours = tokens.astype(F32)
    normed, inverse = normalize(ours)
    hidden = jnp.concatenate([normed, normalize(edge.astype(F32))[0]], axis=0).astype(BF16)
    hidden = group_rows(hidden).reshape(GROUP, share + HALF, D)
    before, after = hidden[0, share:], hidden[GROUP - 1, share:]
    hidden = hidden[:, :share].reshape(rows, D)
    mlp, gate, up = turn(trade(rest, "core", 1).reshape(GROUP * shard, -1), (OWN_FF,) * 3)
    wide = jnp.concatenate([before, hidden, after], axis=0)
    (attn_x, wide, mlp, gate, up), qkv_z = close((attn_x, wide, mlp, gate, up), qkv_z)
    hidden = wide[HALF : HALF + rows]
    mlp_z = z_gather(mlp)
    qkv_x = send_seq(qkv_z, 1)
    attn = assemble_rows(attn_z, attn_x).reshape(2, 2, seqs // 4, shard, D)
    attn_full = trade(trade(attn, "fy", 0), "core", 1)
    attn_full = attn_full.transpose(2, 0, 1, 3, 4).reshape(OWN, D)
    (qkv_x, attn_full, gate, cotangent_in), mlp_z = close(
        (qkv_x, attn_full, gate, cotangent_in), mlp_z
    )
    gate_z = z_gather(gate)
    mlp_x = send_seq(mlp_z, 1)
    qkv_full = assemble(qkv_z, qkv_x)
    index = seq * rows - HALF + jnp.arange(rows + 2 * HALF, dtype=jnp.int32)
    segment, position = place(jnp.clip(index, 0, total - 1), seq_lengths)
    segment = jnp.where((index >= 0) & (index < total), segment, -1)
    q_seg = segment[HALF : HALF + rows][:, None]
    k_seg = segment[None, :]
    cosine, sine = angles(position)
    packed = cols_dot(wide, qkv_full)
    blocks = rows // 128
    flops = blocks * OWN_HEADS * 128 * 256 * 128 * 4
    query, keys, values, attended = call_kernel(
        attend_kernel,
        [
            like((rows, OWN), BF16),
            like((rows + 2 * HALF, OWN), BF16),
            like((rows + 2 * HALF, OWN), BF16),
            like((rows, OWN), BF16),
        ],
        blocks,
        flops,
        (packed, cosine, sine, q_seg, k_seg),
    )
    part = jnp.dot(attended, attn_full, preferred_element_type=F32)
    cot = join(cotangent_in, "fy", 0)
    (mlp_x, part, up, cot), gate_z = close((mlp_x, part, up, cot), gate_z)
    up_z = z_gather(up)
    gate_x = send_seq(gate_z, 1)
    middle = ours + group_sum(part, share)
    mlp_full = assemble(mlp_z, mlp_x)
    (gate_x, middle, mlp_full), up_z = close((gate_x, middle, mlp_full), up_z)
    up_x = send_seq(up_z, 1)
    normed_mid, inverse_mid = normalize(middle)
    lifted = join(normed_mid.astype(BF16), "fy", 0)
    gate_full = assemble(gate_z, gate_x)
    up_x, lifted, gate_full = tie((up_x, lifted, gate_full))
    lifted, cot = core_rows(lifted), core_rows(cot)
    grad_mixed = cols_dot(cot, mlp_full)
    gate = cols_dot(lifted, gate_full)
    up_full = assemble(up_z, up_x)
    up = cols_dot(lifted, up_full)
    gate, up = tie((gate, up))
    mixed = geglu(gate, up).astype(BF16)

    unused, gelu_back = jax.vjp(geglu, gate, up)
    grad_gate, grad_up = gelu_back(grad_mixed)
    grad_gate, grad_up = grad_gate.astype(BF16), grad_up.astype(BF16)
    mlp_kept, mlp_sent = split(rows_dot(mixed, cot).astype(BF16))
    mlp_kept, mlp_sent, grad_gate, grad_up = tie((mlp_kept, mlp_sent, grad_gate, grad_up))
    mlp_x = send_seq(mlp_sent, 1)
    part_lifted = jnp.dot(grad_gate, gate_full, preferred_element_type=F32) + jnp.dot(
        grad_up, up_full, preferred_element_type=F32
    )
    grad_hat = group_sum(part_lifted, share)
    gate_kept, gate_sent = split(rows_dot(grad_gate, lifted).astype(BF16))
    up_kept, up_sent = split(rows_dot(grad_up, lifted).astype(BF16))
    mlp_x, gate_sent, up_sent, grad_hat = tie((mlp_x, gate_sent, up_sent, grad_hat))
    mlp_got = z_spread(x_sum(mlp_kept, mlp_x))
    gate_x = send_seq(gate_sent, 1)
    grad_middle = cotangent.astype(F32) + norm_back(grad_hat, normed_mid, inverse_mid)
    grad_attn = join(grad_middle.astype(BF16), "fy", 0)
    (gate_x, grad_attn, attended), mlp_got = close((gate_x, grad_attn, attended), mlp_got)
    gate_got = z_spread(x_sum(gate_kept, gate_x))
    up_x = send_seq(up_sent, 1)
    grad_attn = core_rows(grad_attn)
    grad_attended = cols_dot(grad_attn, attn_full).astype(BF16)
    grad_q, grad_k, grad_v = call_kernel(
        attend_back_kernel,
        [
            like((rows, OWN), BF16),
            like((rows + 2 * HALF, OWN), F32),
            like((rows + 2 * HALF, OWN), F32),
        ],
        blocks,
        flops * 3,
        (query, keys, values, grad_attended, cosine, sine, q_seg, k_seg),
    )
    grad_kv = jnp.concatenate([grad_k, grad_v], axis=1)
    attn_g = rows_dot(attended, grad_attn).astype(BF16)
    attn_g = attn_g.reshape(seqs // 4, 2, 2, shard, D).transpose(1, 2, 0, 3, 4)
    attn_g = trade(attn_g, "core", 1)
    part_out = jnp.dot(mixed, mlp_full, preferred_element_type=F32)
    (up_x, grad_kv, attn_g, part_out), gate_got = close((up_x, grad_kv, attn_g, part_out), gate_got)
    up_got = z_spread(x_sum(up_kept, up_x))
    ahead = [(i, i + 1) for i in range(seqs - 1)]
    behind = [(i + 1, i) for i in range(seqs - 1)]
    low_edge = lax.ppermute(grad_kv[:HALF].astype(BF16), "seq", behind)
    high_edge = lax.ppermute(grad_kv[HALF + rows :].astype(BF16), "seq", ahead)
    attn_g = trade(attn_g, "fy", 0).reshape(seqs, shard, D)
    middle_kv = grad_kv[HALF : HALF + rows]
    gap = jnp.zeros((rows - 2 * HALF, 2 * OWN), F32)
    edges = jnp.concatenate([high_edge.astype(F32), gap, low_edge.astype(F32)], axis=0)
    grad_packed = jnp.concatenate([grad_q, (middle_kv + edges).astype(BF16)], axis=1)
    qkv_kept, qkv_sent = split(rows_dot(grad_packed, hidden).astype(BF16))
    (attn_g, qkv_sent, grad_packed), up_got = close((attn_g, qkv_sent, grad_packed), up_got)
    qkv_x = send_seq(qkv_sent, 1)
    rest_g = turn_back([mlp_got, gate_got, up_got], WIDE).reshape(2, 2, shard, -1)
    rest_g = trade(rest_g, "fy", 0)
    attn_kept, attn_sent = split_rows(attn_g)
    part_hidden = jnp.dot(grad_packed, qkv_full, preferred_element_type=F32)
    parts = jnp.stack([part_hidden, part_out]).reshape(2, 2, 2, share, D)
    qkv_x, rest_g, parts, attn_sent = tie((qkv_x, rest_g, parts, attn_sent))
    qkv_got = z_spread(x_sum(qkv_kept, qkv_x))
    attn_x = send_seq(attn_sent, 1)

    def back_columns(cells, parts, width):
        cells = cells.reshape(2, 2, shard, parts, width).transpose(2, 3, 0, 1, 4)
        return cells.reshape(shard, parts * 2 * 2 * width).astype(F32)

    rest_g = trade(rest_g, "core", 1)
    raw_mlp = back_columns(rest_g[..., :OWN_FF], 1, OWN_FF)
    raw_in = back_columns(rest_g[..., OWN_FF : 3 * OWN_FF], 2, OWN_FF)
    grad_w_in = raw_in * gain_m
    grad_gain_mlp = jnp.sum(raw_in * w_in.astype(F32), axis=1)
    grad_hidden, sum_out = reduce_pair(reduce_pair(parts, "core", 2), "fy", 1)
    output = (middle + sum_out).astype(BF16)
    input_grad = grad_middle + norm_back(grad_hidden, normed, inverse)
    attn_x, qkv_got, output, input_grad, raw_mlp, grad_w_in, grad_gain_mlp = tie(
        (attn_x, qkv_got, output, input_grad, raw_mlp, grad_w_in, grad_gain_mlp)
    )
    attn_got = z_spread(x_sum(attn_kept, attn_x))
    raw_qkv = turn_back([qkv_got], 3 * OWN).reshape(2, 2, shard, -1)
    raw_qkv = back_columns(trade(trade(raw_qkv, "fy", 0), "core", 1), 3, OWN)
    grad_gain_attn = jnp.sum(raw_qkv * w_qkv.astype(F32), axis=1)
    grad_attn_out = total_of(attn_got)
    return (
        output,
        input_grad,
        raw_qkv * gain_a,
        grad_attn_out,
        grad_w_in,
        raw_mlp,
        grad_gain_attn,
        grad_gain_mlp,
    )


def solution(mesh):
    split = Mesh(mesh.devices.reshape(mesh.shape["seq"], -1, 2), ALL)
    two, one = P(ALL, None), P(ALL)
    return jax.shard_map(
        on_device,
        mesh=split,
        in_specs=(two, two, P(), two, two, two, two, one, one),
        out_specs=(two, two, two, two, two, two, one, one),
        check_vma=False,
    )
```

```python
import jax
import jax.numpy as jnp
from jax import lax
from jax.experimental import pallas as pl
from jax.experimental.pallas import tpu as pltpu
from jax.sharding import Mesh, PartitionSpec as P

D = 1024
HEADS = 16
HDIM = 64
FF = 2624
HALF = 64
GROUP = 4
OWN_HEADS = HEADS // GROUP
OWN = OWN_HEADS * HDIM
OWN_FF = FF // GROUP
WIDE = 2048
VMEM_LIMIT = 48 * 1024 * 1024

EPSILON = 1e-05
MASKED = -1e30
ALL = ("seq", "fy", "core")
BF16 = jnp.bfloat16
F32 = jnp.float32


def flat_pairs(change):
    count = lax.axis_size(ALL)
    return [(i, change(i)) for i in range(count)]


def send_seq(cells, flip):
    return lax.ppermute(cells, ALL, flat_pairs(lambda i: i ^ (flip * GROUP)))


def trade(cells, axis, dim):
    me = lax.axis_index(axis)
    kept = lax.dynamic_slice_in_dim(cells, me, 1, axis=dim)
    sent = lax.dynamic_slice_in_dim(cells, 1 - me, 1, axis=dim)
    got = lax.ppermute(sent, axis, [(0, 1), (1, 0)])
    low = me == 0
    return jnp.concatenate([jnp.where(low, kept, got), jnp.where(low, got, kept)], axis=dim)


def join(cells, axis, dim):
    me = lax.axis_index(axis)
    got = lax.ppermute(cells, axis, [(0, 1), (1, 0)])
    low = me == 0
    return jnp.stack([jnp.where(low, cells, got), jnp.where(low, got, cells)], axis=dim)


def reduce_pair(cells, axis, dim):
    me = lax.axis_index(axis)
    kept = lax.dynamic_index_in_dim(cells, me, dim, keepdims=False)
    sent = lax.dynamic_index_in_dim(cells, 1 - me, dim, keepdims=False).astype(BF16)
    got = lax.ppermute(sent, axis, [(0, 1), (1, 0)])
    return kept.astype(F32) + got.astype(F32)


def core_rows(cells):
    return join(cells, "core", 1).reshape((-1,) + cells.shape[2:])


def group_rows(cells):
    return core_rows(join(cells, "fy", 0))


def group_sum(part, rows):
    cells = part.reshape(2, 2, rows, part.shape[-1])
    return reduce_pair(reduce_pair(cells, "core", 1), "fy", 0)


def depth_of():
    return lax.axis_size("seq") // 2


def direct():
    return lax.axis_size("seq") == 8


def place_of_device():
    seq = lax.axis_index("seq")
    return jnp.stack([seq >> 1, seq & 1]).astype(jnp.int32)


def z_gather(cells):
    if direct():
        return jnp.stack([cells] + [send_seq(cells, 2 * d) for d in range(1, 4)])
    cells, me = cells[None], lax.axis_index("seq") >> 1
    flip = 1
    while flip < depth_of():
        other = send_seq(cells, 2 * flip)
        high = (me & flip) != 0
        cells = jnp.concatenate([jnp.where(high, other, cells), jnp.where(high, cells, other)])
        flip *= 2
    return cells


def x_sum(kept, got):
    return (kept.astype(F32) + got.astype(F32)).astype(BF16)


def z_spread(cells):
    if direct():
        return [cells[0]] + [send_seq(cells[d], 2 * d) for d in range(1, 4)]
    flip, me = depth_of() // 2, lax.axis_index("seq") >> 1
    while flip:
        high = ((me & flip) != 0).astype(jnp.int32)
        kept = lax.dynamic_slice_in_dim(cells, high * flip, flip, 0)
        sent = lax.dynamic_slice_in_dim(cells, (1 - high) * flip, flip, 0)
        cells = kept.astype(F32) + send_seq(sent.astype(BF16), 2 * flip).astype(F32)
        flip //= 2
    return [cells[0]]


def total_of(got):
    return sum(cells.astype(F32) for cells in got)


def local_kernel(kernel, outs, args, scratch=()):
    spaces = [
        pltpu.SMEM if a.dtype == jnp.int32 and a.size == 2 else pltpu.VMEM for a in args
    ]
    moved = sum(a.size * a.dtype.itemsize for a in args)
    return pl.pallas_call(
        kernel,
        out_shape=outs,
        in_specs=[pl.BlockSpec(memory_space=s) for s in spaces],
        out_specs=[pl.BlockSpec(memory_space=pltpu.VMEM)] * len(outs),
        scratch_shapes=list(scratch),
        compiler_params=pltpu.CompilerParams(vmem_limit_bytes=VMEM_LIMIT),
        cost_estimate=pl.CostEstimate(flops=0, bytes_accessed=moved, transcendentals=0),
    )(*args)


def lane_assemble_kernel(cells, got, where, full):
    for d in range(4):
        z = where[0] ^ d
        mine = pl.multiple_of((2 * z + where[1]) * 128, 128)
        theirs = pl.multiple_of((2 * z + 1 - where[1]) * 128, 128)
        full[:, pl.ds(mine, 128)] = cells[d]
        full[:, pl.ds(theirs, 128)] = got[d]


def lane_split_kernel(full, where, kept, sent):
    for d in range(4):
        z = where[0] ^ d
        mine = pl.multiple_of((2 * z + where[1]) * 128, 128)
        theirs = pl.multiple_of((2 * z + 1 - where[1]) * 128, 128)
        kept[d] = full[:, pl.ds(mine, 128)]
        sent[d] = full[:, pl.ds(theirs, 128)]


def row_assemble_kernel(cells, got, where, full):
    for d in range(4):
        z = where[0] ^ d
        full[2 * z + where[1]] = cells[d]
        full[2 * z + 1 - where[1]] = got[d]


def row_split_kernel(full, where, kept, sent):
    for d in range(4):
        z = where[0] ^ d
        kept[d] = full[2 * z + where[1]]
        sent[d] = full[2 * z + 1 - where[1]]


def turn_kernel(cells, *outs):
    turned = cells[...].astype(F32).T.astype(BF16)
    at = 0
    for out in outs:
        out[...] = turned[at : at + out.shape[0]]
        at += out.shape[0]


def turn_back_kernel(*refs):
    *parts, out, full = refs
    at = 0
    full[...] = jnp.zeros_like(full)
    for i in range(0, len(parts), 4):
        total = parts[i][...].astype(F32)
        for j in range(1, 4):
            total = total + parts[i + j][...].astype(F32)
        full[at : at + total.shape[0], :] = total
        at += total.shape[0]
    out[...] = full[...].T.astype(out.dtype)


def columns_kernel(qkv, mlp, both, gain_a, gain_m, out):
    for g in range(GROUP):
        parts = [
            (qkv[:, p * D + g * OWN : p * D + (g + 1) * OWN].astype(F32) * gain_a[...]).astype(BF16)
            for p in range(3)
        ]
        parts.append(mlp[:, g * OWN_FF : (g + 1) * OWN_FF])
        parts += [
            (both[:, p * FF + g * OWN_FF : p * FF + (g + 1) * OWN_FF].astype(F32) * gain_m[...]).astype(
                BF16
            )
            for p in range(2)
        ]
        parts.append(jnp.zeros((qkv.shape[0], WIDE - 3 * OWN_FF), BF16))
        out[g] = jnp.concatenate(parts, axis=1)


def back_ff_kernel(cells, weight, gain, grad_mlp, grad_in, grad_gain):
    total = jnp.zeros(grad_gain.shape, F32)
    for g in range(GROUP):
        block = cells[g].astype(F32)
        grad_mlp[:, g * OWN_FF : (g + 1) * OWN_FF] = block[:, :OWN_FF]
        for p in range(2):
            raw = block[:, (p + 1) * OWN_FF : (p + 2) * OWN_FF]
            at = slice(p * FF + g * OWN_FF, p * FF + (g + 1) * OWN_FF)
            total = total + jnp.sum(raw * weight[:, at].astype(F32), axis=1, keepdims=True)
            grad_in[:, at] = raw * gain[...]
    grad_gain[...] = total


def back_qkv_kernel(cells, weight, gain, grad, grad_gain):
    total = jnp.zeros(grad_gain.shape, F32)
    for g in range(GROUP):
        block = cells[g].astype(F32)
        for p in range(3):
            raw = block[:, p * OWN : (p + 1) * OWN]
            at = slice(p * D + g * OWN, p * D + (g + 1) * OWN)
            total = total + jnp.sum(raw * weight[:, at].astype(F32), axis=1, keepdims=True)
            grad[:, at] = raw * gain[...]
    grad_gain[...] = total


def columns_of(qkv, mlp, both, gain_a, gain_m):
    rows = qkv.shape[0]
    if direct():
        shape = like((GROUP, rows, 3 * OWN + WIDE), BF16)
        cells = local_kernel(columns_kernel, [shape], (qkv, mlp, both, gain_a, gain_m))[0]
        return cells.reshape(2, 2, rows, -1)

    def columns(w, parts, width):
        cells = w.reshape(rows, parts, 2, 2, width).transpose(2, 3, 0, 1, 4)
        return cells.reshape(2, 2, rows, parts * width)

    return jnp.concatenate(
        [
            columns((qkv.astype(F32) * gain_a).astype(BF16), 3, OWN),
            columns(mlp, 1, OWN_FF),
            columns((both.astype(F32) * gain_m).astype(BF16), 2, OWN_FF),
            jnp.zeros((2, 2, rows, WIDE - 3 * OWN_FF), BF16),
        ],
        axis=-1,
    )


def back_columns(cells, parts, width):
    rows = cells.shape[2]
    cells = cells.reshape(2, 2, rows, parts, width).transpose(2, 3, 0, 1, 4)
    return cells.reshape(rows, parts * GROUP * width).astype(F32)


def back_ff(cells, weight, gain):
    rows = weight.shape[0]
    if direct():
        outs = [like((rows, FF), F32), like((rows, 2 * FF), F32), like((rows, 1), F32)]
        return local_kernel(back_ff_kernel, outs, (cells.reshape(GROUP, rows, WIDE), weight, gain))
    raw = back_columns(cells[..., OWN_FF : 3 * OWN_FF], 2, OWN_FF)
    grad_gain = jnp.sum(raw * weight.astype(F32), axis=1, keepdims=True)
    return back_columns(cells[..., :OWN_FF], 1, OWN_FF), raw * gain, grad_gain


def back_qkv(cells, weight, gain):
    rows = weight.shape[0]
    if direct():
        outs = [like((rows, 3 * D), F32), like((rows, 1), F32)]
        return local_kernel(back_qkv_kernel, outs, (cells.reshape(GROUP, rows, -1), weight, gain))
    raw = back_columns(cells, 3, OWN)
    return raw * gain, jnp.sum(raw * weight.astype(F32), axis=1, keepdims=True)


def x_blocks(cells, got):
    high = (lax.axis_index("seq") & 1) == 1
    blocks = []
    for i in range(cells.shape[0]):
        blocks += [jnp.where(high, got[i], cells[i]), jnp.where(high, cells[i], got[i])]
    return blocks


def x_parts(blocks):
    high = (lax.axis_index("seq") & 1) == 1
    pairs = list(zip(blocks[::2], blocks[1::2]))
    kept = jnp.stack([jnp.where(high, b, a) for a, b in pairs])
    sent = jnp.stack([jnp.where(high, a, b) for a, b in pairs])
    return kept, sent


def assemble(cells, got):
    if direct():
        shape = like((cells.shape[1], D), BF16)
        return local_kernel(lane_assemble_kernel, [shape], (cells, got, place_of_device()))[0]
    return jnp.concatenate(x_blocks(cells, got), axis=-1)


def split(grad):
    count = lax.axis_size("seq")
    size = D // count
    if direct():
        shape = like((4, grad.shape[0], size), BF16)
        return local_kernel(lane_split_kernel, [shape, shape], (grad, place_of_device()))
    return x_parts([grad[:, i * size : (i + 1) * size] for i in range(count)])


def assemble_rows(cells, got):
    if direct():
        shape = like((8,) + cells.shape[1:], BF16)
        return local_kernel(row_assemble_kernel, [shape], (cells, got, place_of_device()))[0]
    return jnp.stack(x_blocks(cells, got))


def split_rows(cells):
    if direct():
        shape = like((4,) + cells.shape[1:], BF16)
        return local_kernel(row_split_kernel, [shape, shape], (cells, place_of_device()))
    return x_parts([cells[i] for i in range(cells.shape[0])])


def turn(cells, sizes):
    if direct():
        return local_kernel(turn_kernel, [like((n, cells.shape[0]), BF16) for n in sizes], (cells,))
    turned, outs, at = cells.T, [], 0
    for n in sizes:
        outs.append(turned[at : at + n])
        at += n
    return outs


def turn_back(chunks, width):
    if direct():
        lanes = chunks[0][0].shape[1]
        return local_kernel(
            turn_back_kernel,
            [like((lanes, width), BF16)],
            tuple(c for chunk in chunks for c in chunk),
            [pltpu.VMEM((width, lanes), F32)],
        )[0]
    turned = jnp.concatenate([total_of(c) for c in chunks], axis=0).T.astype(BF16)
    return jnp.pad(turned, ((0, 0), (0, width - turned.shape[1])))


def place(index, seq_lengths):
    count = seq_lengths.shape[0]
    ids = jnp.arange(count, dtype=jnp.int32)
    ends = jnp.sum(jnp.where(ids[None, :] <= ids[:, None], seq_lengths[None, :], 0), axis=1)
    starts = ends - seq_lengths
    segment = jnp.sum((index[:, None] >= ends[None, :]).astype(jnp.int32), axis=1)
    begins = jnp.sum(jnp.where(segment[:, None] == ids[None, :], starts[None, :], 0), axis=1)
    return segment, index - begins


def angles(position):
    freqs = 10000.0 ** (-(jnp.arange(HDIM // 2, dtype=F32) * 2.0) / HDIM)
    freqs = jnp.concatenate([freqs] * 4)
    turns = position.astype(F32)[:, None] * freqs[None, :]
    sign = jnp.where(jnp.arange(128) % HDIM < HDIM // 2, -1.0, 1.0)
    return jnp.cos(turns), jnp.sin(turns) * sign[None, :]


def normalize(values):
    average = jnp.mean(values, axis=-1, keepdims=True)
    centered = values - average
    variance = jnp.mean(centered * centered, axis=-1, keepdims=True)
    inverse = lax.rsqrt(variance + EPSILON)
    return centered * inverse, inverse


def norm_back(grad_hat, normed, inverse):
    return inverse * (
        grad_hat
        - jnp.mean(grad_hat, axis=-1, keepdims=True)
        - normed * jnp.mean(grad_hat * normed, axis=-1, keepdims=True)
    )


def geglu(gate_in, up_in):
    return jax.nn.gelu(gate_in, approximate=False) * up_in


def contract(left, right, dims, out=F32):
    return lax.dot_general(left, right, ((dims[0], dims[1]), ((), ())), preferred_element_type=out)


def rows_dot(left, right):
    return contract(left, right, ((0,), (0,)))


def cols_dot(left, right):
    return contract(left, right, ((1,), (1,)))


def half_swap(values):
    lane = lax.broadcasted_iota(jnp.int32, values.shape, 1)
    left = pltpu.roll(values, 128 - HDIM // 2, 1)
    right = pltpu.roll(values, HDIM // 2, 1)
    return jnp.where(lane % HDIM < HDIM // 2, left, right)


def bias_of(q_seg, k_seg, block):
    row = lax.broadcasted_iota(jnp.int32, (128, 256), 0)
    col = lax.broadcasted_iota(jnp.int32, (128, 256), 1)
    near = jnp.abs(row + HALF - col) <= HALF
    same = q_seg[pl.ds(block * 128, 128), :] == k_seg[:, pl.ds(block * 128, 256)]
    return jnp.where(near & same, 0.0, MASKED)


def softmax_of(scores):
    exponent = jnp.exp(scores - jnp.max(scores, axis=-1, keepdims=True))
    return exponent * (1.0 / jnp.sum(exponent, axis=-1, keepdims=True))


def attend_kernel(packed, cosine, sine, q_seg, k_seg, query, keys, values, attended, bias):
    rows = query.shape[0]
    blocks = rows // 128
    for b in range(blocks):
        bias[b] = bias_of(q_seg, k_seg, b)
    first = lax.broadcasted_iota(jnp.int32, (1, 128), 1) < HDIM
    for p in range(OWN_HEADS // 2):
        at = slice(p * 128, (p + 1) * 128)
        u = packed[HALF : HALF + rows, at]
        q_cos, q_sin = cosine[HALF : HALF + rows, :], sine[HALF : HALF + rows, :]
        query[:, at] = (u * q_cos + half_swap(u) * q_sin).astype(BF16)
        u = packed[:, OWN + p * 128 : OWN + (p + 1) * 128]
        keys[:, at] = (u * cosine[...] + half_swap(u) * sine[...]).astype(BF16)
        values[:, at] = packed[:, 2 * OWN + p * 128 : 2 * OWN + (p + 1) * 128].astype(BF16)
        for b in range(blocks):
            q = query[b * 128 : (b + 1) * 128, at]
            k = keys[b * 128 : b * 128 + 256, at]
            v = values[b * 128 : b * 128 + 256, at]
            outs = []
            for side in (first, ~first):
                q_one = jnp.where(side, q, jnp.zeros_like(q))
                scores = contract(q_one, k, ((1,), (1,))) * (HDIM**-0.5) + bias[b]
                prob = softmax_of(scores).astype(BF16)
                outs.append(contract(prob, v, ((1,), (0,))))
            attended[b * 128 : (b + 1) * 128, at] = jnp.where(first, outs[0], outs[1]).astype(BF16)


def attend_back_kernel(
    query, keys, values, grad, cosine, sine, q_seg, k_seg, grad_q, grad_k, grad_v, bias
):
    rows = query.shape[0]
    blocks = rows // 128
    scale = HDIM**-0.5
    for b in range(blocks):
        bias[b] = bias_of(q_seg, k_seg, b)
    first = lax.broadcasted_iota(jnp.int32, (1, 128), 1) < HDIM
    grad_k[...] = jnp.zeros_like(grad_k)
    grad_v[...] = jnp.zeros_like(grad_v)
    for p in range(OWN_HEADS // 2):
        at = slice(p * 128, (p + 1) * 128)
        for b in range(blocks):
            here, span = slice(b * 128, (b + 1) * 128), slice(b * 128, b * 128 + 256)
            q, go = query[here, at], grad[here, at]
            k, v = keys[span, at], values[span, at]
            d_q = jnp.zeros((128, 128), F32)
            d_k = jnp.zeros((256, 128), F32)
            d_v = jnp.zeros((256, 128), F32)
            for side in (first, ~first):
                q_one = jnp.where(side, q, jnp.zeros_like(q))
                k_one = jnp.where(side, k, jnp.zeros_like(k))
                go_one = jnp.where(side, go, jnp.zeros_like(go))
                scores = contract(q_one, k, ((1,), (1,))) * scale + bias[b]
                prob = softmax_of(scores)
                grad_prob = contract(go_one, v, ((1,), (1,)))
                inner = jnp.sum(grad_prob * prob, axis=-1, keepdims=True)
                grad_scores = (prob * (grad_prob - inner)).astype(BF16)
                d_q = d_q + contract(grad_scores, k_one, ((1,), (0,)))
                d_k = d_k + contract(grad_scores, q_one, ((0,), (0,)))
                d_v = d_v + contract(prob.astype(BF16), go_one, ((0,), (0,)))
            d_q = d_q * scale
            at_q = slice(HALF + b * 128, HALF + (b + 1) * 128)
            turned = d_q * cosine[at_q, :] - half_swap(d_q) * sine[at_q, :]
            grad_q[here, at] = turned.astype(BF16)
            grad_k[span, at] += d_k * scale
            grad_v[span, at] += d_v
        d_k = grad_k[:, at]
        grad_k[:, at] = d_k * cosine[...] - half_swap(d_k) * sine[...]


def call_kernel(kernel, outs, blocks, flops, args):
    moved = sum(a.size * a.dtype.itemsize for a in args) + sum(
        o.size * o.dtype.itemsize for o in outs
    )
    return pl.pallas_call(
        kernel,
        out_shape=outs,
        in_specs=[pl.BlockSpec(memory_space=pltpu.VMEM)] * len(args),
        out_specs=[pl.BlockSpec(memory_space=pltpu.VMEM)] * len(outs),
        scratch_shapes=[pltpu.VMEM((blocks, 128, 256), F32)],
        compiler_params=pltpu.CompilerParams(vmem_limit_bytes=VMEM_LIMIT),
        cost_estimate=pl.CostEstimate(flops=flops, bytes_accessed=moved, transcendentals=0),
    )(*args)


def like(shape, dtype):
    return jax.ShapeDtypeStruct(shape, dtype)


def on_device(
    tokens, cotangent, seq_lengths, w_qkv, w_attn_out, w_in, w_mlp_out, gain_attn, gain_mlp
):
    share = tokens.shape[0]
    rows = GROUP * share
    seq, seqs = lax.axis_index("seq"), lax.axis_size("seq")
    total = seqs * rows
    shard = w_qkv.shape[0]
    tie = lax.optimization_barrier

    def close(first, last):
        first = tie(first)
        return tie((first, last))


    gain_a = gain_attn.astype(F32)[:, None]
    gain_m = gain_mlp.astype(F32)[:, None]

    devices = lax.axis_size(ALL)
    ahead = [(i, i + 1) for i in range(GROUP - 1, devices - 1, GROUP)]
    behind = [(i + 1, i) for i in range(GROUP - 1, devices - 1, GROUP)]
    edge = lax.ppermute(tokens[share - HALF :], ALL, ahead)
    edge = edge + lax.ppermute(tokens[:HALF], ALL, behind)
    attn_z = z_gather(w_attn_out)
    cells = columns_of(w_qkv, w_mlp_out, w_in, gain_a, gain_m)
    cells = trade(trade(cells, "fy", 0), "core", 1).reshape(GROUP * shard, -1)
    qkv, mlp, gate, up = turn(cells, (3 * OWN, OWN_FF, OWN_FF, OWN_FF))
    attn_z, qkv, mlp, gate, up, edge, cotangent_in = tie(
        (attn_z, qkv, mlp, gate, up, edge, cotangent)
    )
    qkv_z = z_gather(qkv)
    attn_x = send_seq(attn_z, 1)
    ours = tokens.astype(F32)
    normed, inverse = normalize(ours)
    hidden = jnp.concatenate([normed, normalize(edge.astype(F32))[0]], axis=0).astype(BF16)
    hidden = join(hidden, "fy", 0)
    cot = join(cotangent_in, "fy", 0)
    (attn_x, hidden, cot, mlp, gate, up), qkv_z = close((attn_x, hidden, cot, mlp, gate, up), qkv_z)
    mlp_z = z_gather(mlp)
    qkv_x = send_seq(qkv_z, 1)
    attn = assemble_rows(attn_z, attn_x).reshape(2, 2, seqs // 4, shard, D)
    hidden = core_rows(hidden).reshape(GROUP, share + HALF, D)
    attn = trade(attn, "core", 1)
    (qkv_x, attn, hidden, gate), mlp_z = close((qkv_x, attn, hidden, gate), mlp_z)
    gate_z = z_gather(gate)
    mlp_x = send_seq(mlp_z, 1)
    attn = trade(attn, "fy", 0)
    before, after = hidden[0, share:], hidden[GROUP - 1, share:]
    hidden = hidden[:, :share].reshape(rows, D)
    wide = jnp.concatenate([before, hidden, after], axis=0)
    qkv_full = assemble(qkv_z, qkv_x)
    index = seq * rows - HALF + jnp.arange(rows + 2 * HALF, dtype=jnp.int32)
    segment, position = place(jnp.clip(index, 0, total - 1), seq_lengths)
    segment = jnp.where((index >= 0) & (index < total), segment, -1)
    q_seg = segment[HALF : HALF + rows][:, None]
    k_seg = segment[None, :]
    cosine, sine = angles(position)
    packed = cols_dot(wide, qkv_full)
    blocks = rows // 128
    flops = blocks * OWN_HEADS * 128 * 256 * 128 * 4
    query, keys, values, attended = call_kernel(
        attend_kernel,
        [
            like((rows, OWN), BF16),
            like((rows + 2 * HALF, OWN), BF16),
            like((rows + 2 * HALF, OWN), BF16),
            like((rows, OWN), BF16),
        ],
        blocks,
        flops,
        (packed, cosine, sine, q_seg, k_seg),
    )
    (mlp_x, attended, attn, up), gate_z = close((mlp_x, attended, attn, up), gate_z)
    up_z = z_gather(up)
    gate_x = send_seq(gate_z, 1)
    attn_full = attn.transpose(2, 0, 1, 3, 4).reshape(OWN, D)
    part = jnp.dot(attended, attn_full, preferred_element_type=F32)
    middle = ours + group_sum(part, share)
    mlp_full = assemble(mlp_z, mlp_x)
    (gate_x, middle, mlp_full), up_z = close((gate_x, middle, mlp_full), up_z)
    up_x = send_seq(up_z, 1)
    normed_mid, inverse_mid = normalize(middle)
    lifted = join(normed_mid.astype(BF16), "fy", 0)
    gate_full = assemble(gate_z, gate_x)
    up_x, lifted, gate_full = tie((up_x, lifted, gate_full))
    lifted, cot = core_rows(lifted), core_rows(cot)
    grad_mixed = cols_dot(cot, mlp_full)
    gate = cols_dot(lifted, gate_full)
    up_full = assemble(up_z, up_x)
    up = cols_dot(lifted, up_full)
    gate, up = tie((gate, up))
    mixed = geglu(gate, up).astype(BF16)

    unused, gelu_back = jax.vjp(geglu, gate, up)
    grad_gate, grad_up = gelu_back(grad_mixed)
    grad_gate, grad_up = grad_gate.astype(BF16), grad_up.astype(BF16)
    mlp_kept, mlp_sent = split(rows_dot(mixed, cot).astype(BF16))
    mlp_kept, mlp_sent, grad_gate, grad_up = tie((mlp_kept, mlp_sent, grad_gate, grad_up))
    mlp_x = send_seq(mlp_sent, 1)
    part_lifted = jnp.dot(grad_gate, gate_full, preferred_element_type=F32) + jnp.dot(
        grad_up, up_full, preferred_element_type=F32
    )
    half_hat = reduce_pair(part_lifted.reshape(2, 2, share, D), "core", 1)
    half_hat, grad_gate, grad_up = tie((half_hat, grad_gate, grad_up))
    grad_hat = reduce_pair(half_hat, "fy", 0)
    gate_kept, gate_sent = split(rows_dot(grad_gate, lifted).astype(BF16))
    up_kept, up_sent = split(rows_dot(grad_up, lifted).astype(BF16))
    mlp_x, gate_sent, up_sent, grad_hat = tie((mlp_x, gate_sent, up_sent, grad_hat))
    mlp_got = z_spread(x_sum(mlp_kept, mlp_x))
    gate_x = send_seq(gate_sent, 1)
    grad_middle = cotangent.astype(F32) + norm_back(grad_hat, normed_mid, inverse_mid)
    grad_attn = join(grad_middle.astype(BF16), "fy", 0)
    (gate_x, grad_attn, attended), mlp_got = close((gate_x, grad_attn, attended), mlp_got)
    gate_got = z_spread(x_sum(gate_kept, gate_x))
    up_x = send_seq(up_sent, 1)
    grad_attn = core_rows(grad_attn)
    grad_attended = cols_dot(grad_attn, attn_full).astype(BF16)
    grad_q, grad_k, grad_v = call_kernel(
        attend_back_kernel,
        [
            like((rows, OWN), BF16),
            like((rows + 2 * HALF, OWN), F32),
            like((rows + 2 * HALF, OWN), F32),
        ],
        blocks,
        flops * 3,
        (query, keys, values, grad_attended, cosine, sine, q_seg, k_seg),
    )
    grad_kv = jnp.concatenate([grad_k, grad_v], axis=1)
    attn_g = rows_dot(attended, grad_attn).astype(BF16)
    attn_g = attn_g.reshape(seqs // 4, 2, 2, shard, D).transpose(1, 2, 0, 3, 4)
    attn_g = trade(attn_g, "core", 1)
    part_out = jnp.dot(mixed, mlp_full, preferred_element_type=F32)
    (up_x, grad_kv, attn_g, part_out), gate_got = close((up_x, grad_kv, attn_g, part_out), gate_got)
    up_got = z_spread(x_sum(up_kept, up_x))
    ahead = [(i, i + 1) for i in range(seqs - 1)]
    behind = [(i + 1, i) for i in range(seqs - 1)]
    low_edge = lax.ppermute(grad_kv[:HALF].astype(BF16), "seq", behind)
    high_edge = lax.ppermute(grad_kv[HALF + rows :].astype(BF16), "seq", ahead)
    attn_g = trade(attn_g, "fy", 0).reshape(seqs, shard, D)
    middle_kv = grad_kv[HALF : HALF + rows]
    gap = jnp.zeros((rows - 2 * HALF, 2 * OWN), F32)
    edges = jnp.concatenate([high_edge.astype(F32), gap, low_edge.astype(F32)], axis=0)
    grad_packed = jnp.concatenate([grad_q, (middle_kv + edges).astype(BF16)], axis=1)
    qkv_kept, qkv_sent = split(rows_dot(grad_packed, hidden).astype(BF16))
    (attn_g, qkv_sent, grad_packed), up_got = close((attn_g, qkv_sent, grad_packed), up_got)
    qkv_x = send_seq(qkv_sent, 1)
    rest_g = turn_back([mlp_got, gate_got, up_got], WIDE).reshape(2, 2, shard, -1)
    rest_g = trade(rest_g, "fy", 0)
    attn_kept, attn_sent = split_rows(attn_g)
    part_hidden = jnp.dot(grad_packed, qkv_full, preferred_element_type=F32)
    parts = jnp.stack([part_hidden, part_out]).reshape(2, 2, 2, share, D)
    qkv_x, rest_g, parts, attn_sent = tie((qkv_x, rest_g, parts, attn_sent))
    qkv_got = z_spread(x_sum(qkv_kept, qkv_x))
    attn_x = send_seq(attn_sent, 1)

    rest_g = trade(rest_g, "core", 1)
    grad_mlp_out, grad_w_in, grad_gain_mlp = back_ff(rest_g, w_in, gain_m)
    grad_hidden, sum_out = reduce_pair(reduce_pair(parts, "core", 2), "fy", 1)
    output = (middle + sum_out).astype(BF16)
    input_grad = grad_middle + norm_back(grad_hidden, normed, inverse)
    attn_x, qkv_got, output, input_grad, grad_mlp_out, grad_w_in, grad_gain_mlp = tie(
        (attn_x, qkv_got, output, input_grad, grad_mlp_out, grad_w_in, grad_gain_mlp)
    )
    attn_got = z_spread(x_sum(attn_kept, attn_x))
    qkv_g = turn_back([qkv_got], 3 * OWN).reshape(2, 2, shard, -1)
    qkv_g = trade(trade(qkv_g, "fy", 0), "core", 1)
    grad_w_qkv, grad_gain_attn = back_qkv(qkv_g, w_qkv, gain_a)
    grad_attn_out = total_of(attn_got)
    return (
        output,
        input_grad,
        grad_w_qkv,
        grad_attn_out,
        grad_w_in,
        grad_mlp_out,
        grad_gain_attn[:, 0],
        grad_gain_mlp[:, 0],
    )


def solution(mesh):
    split = Mesh(mesh.devices.reshape(mesh.shape["seq"], -1, 2), ALL)
    two, one = P(ALL, None), P(ALL)
    return jax.shard_map(
        on_device,
        mesh=split,
        in_specs=(two, two, P(), two, two, two, two, one, one),
        out_specs=(two, two, two, two, two, two, one, one),
        check_vma=False,
    )
```

```python
import jax
import jax.numpy as jnp
from jax import lax
from jax.experimental import pallas as pl
from jax.experimental.pallas import tpu as pltpu
from jax.sharding import Mesh, PartitionSpec as P

D = 1024
HEADS = 16
HDIM = 64
FF = 2624
HALF = 64
GROUP = 4
OWN_HEADS = HEADS // GROUP
OWN = OWN_HEADS * HDIM
OWN_FF = FF // GROUP
WIDE = 2048
VMEM_LIMIT = 48 * 1024 * 1024

EPSILON = 1e-05
MASKED = -1e30
ALL = ("seq", "fy", "core")
BF16 = jnp.bfloat16
F32 = jnp.float32


def flat_pairs(change):
    count = lax.axis_size(ALL)
    return [(i, change(i)) for i in range(count)]


def send_seq(cells, flip):
    return lax.ppermute(cells, ALL, flat_pairs(lambda i: i ^ (flip * GROUP)))


def trade(cells, axis, dim):
    me = lax.axis_index(axis)
    kept = lax.dynamic_slice_in_dim(cells, me, 1, axis=dim)
    sent = lax.dynamic_slice_in_dim(cells, 1 - me, 1, axis=dim)
    got = lax.ppermute(sent, axis, [(0, 1), (1, 0)])
    low = me == 0
    return jnp.concatenate([jnp.where(low, kept, got), jnp.where(low, got, kept)], axis=dim)


def join(cells, axis, dim):
    me = lax.axis_index(axis)
    got = lax.ppermute(cells, axis, [(0, 1), (1, 0)])
    low = me == 0
    return jnp.stack([jnp.where(low, cells, got), jnp.where(low, got, cells)], axis=dim)


def reduce_pair(cells, axis, dim):
    me = lax.axis_index(axis)
    kept = lax.dynamic_index_in_dim(cells, me, dim, keepdims=False)
    sent = lax.dynamic_index_in_dim(cells, 1 - me, dim, keepdims=False).astype(BF16)
    got = lax.ppermute(sent, axis, [(0, 1), (1, 0)])
    return kept.astype(F32) + got.astype(F32)


def core_rows(cells):
    return join(cells, "core", 1).reshape((-1,) + cells.shape[2:])


def group_rows(cells):
    return core_rows(join(cells, "fy", 0))


def group_sum(part, rows):
    cells = part.reshape(2, 2, rows, part.shape[-1])
    return reduce_pair(reduce_pair(cells, "core", 1), "fy", 0)


def depth_of():
    return lax.axis_size("seq") // 2


def direct():
    return lax.axis_size("seq") == 8


def place_of_device():
    seq = lax.axis_index("seq")
    return jnp.stack([seq >> 1, seq & 1]).astype(jnp.int32)


def z_gather(cells):
    if direct():
        return jnp.stack([cells] + [send_seq(cells, 2 * d) for d in range(1, 4)])
    cells, me = cells[None], lax.axis_index("seq") >> 1
    flip = 1
    while flip < depth_of():
        other = send_seq(cells, 2 * flip)
        high = (me & flip) != 0
        cells = jnp.concatenate([jnp.where(high, other, cells), jnp.where(high, cells, other)])
        flip *= 2
    return cells


def x_sum(kept, got):
    return (kept.astype(F32) + got.astype(F32)).astype(BF16)


def z_spread(cells):
    if direct():
        return [cells[0]] + [send_seq(cells[d], 2 * d) for d in range(1, 4)]
    flip, me = depth_of() // 2, lax.axis_index("seq") >> 1
    while flip:
        high = ((me & flip) != 0).astype(jnp.int32)
        kept = lax.dynamic_slice_in_dim(cells, high * flip, flip, 0)
        sent = lax.dynamic_slice_in_dim(cells, (1 - high) * flip, flip, 0)
        cells = kept.astype(F32) + send_seq(sent.astype(BF16), 2 * flip).astype(F32)
        flip //= 2
    return [cells[0]]


def total_of(got):
    return sum(cells.astype(F32) for cells in got)


def local_kernel(kernel, outs, args, scratch=()):
    spaces = [
        pltpu.SMEM if a.dtype == jnp.int32 and a.size == 2 else pltpu.VMEM for a in args
    ]
    moved = sum(a.size * a.dtype.itemsize for a in args)
    return pl.pallas_call(
        kernel,
        out_shape=outs,
        in_specs=[pl.BlockSpec(memory_space=s) for s in spaces],
        out_specs=[pl.BlockSpec(memory_space=pltpu.VMEM)] * len(outs),
        scratch_shapes=list(scratch),
        compiler_params=pltpu.CompilerParams(vmem_limit_bytes=VMEM_LIMIT),
        cost_estimate=pl.CostEstimate(flops=0, bytes_accessed=moved, transcendentals=0),
    )(*args)


def lane_assemble_kernel(cells, got, where, full):
    for d in range(4):
        z = where[0] ^ d
        mine = pl.multiple_of((2 * z + where[1]) * 128, 128)
        theirs = pl.multiple_of((2 * z + 1 - where[1]) * 128, 128)
        full[:, pl.ds(mine, 128)] = cells[d]
        full[:, pl.ds(theirs, 128)] = got[d]


def lane_split_kernel(full, where, kept, sent):
    for d in range(4):
        z = where[0] ^ d
        mine = pl.multiple_of((2 * z + where[1]) * 128, 128)
        theirs = pl.multiple_of((2 * z + 1 - where[1]) * 128, 128)
        kept[d] = full[:, pl.ds(mine, 128)]
        sent[d] = full[:, pl.ds(theirs, 128)]


def row_assemble_kernel(cells, got, where, full):
    for d in range(4):
        z = where[0] ^ d
        full[2 * z + where[1]] = cells[d]
        full[2 * z + 1 - where[1]] = got[d]


def row_split_kernel(full, where, kept, sent):
    for d in range(4):
        z = where[0] ^ d
        kept[d] = full[2 * z + where[1]]
        sent[d] = full[2 * z + 1 - where[1]]


def turn_kernel(cells, *outs):
    turned = cells[...].astype(F32).T.astype(BF16)
    at = 0
    for out in outs:
        out[...] = turned[at : at + out.shape[0]]
        at += out.shape[0]


def turn_back_kernel(*refs):
    *parts, out, full = refs
    at = 0
    full[...] = jnp.zeros_like(full)
    for i in range(0, len(parts), 4):
        total = parts[i][...].astype(F32)
        for j in range(1, 4):
            total = total + parts[i + j][...].astype(F32)
        full[at : at + total.shape[0], :] = total
        at += total.shape[0]
    out[...] = full[...].T.astype(out.dtype)


def columns_kernel(qkv, mlp, both, gain_a, gain_m, out):
    for g in range(GROUP):
        parts = [
            (qkv[:, p * D + g * OWN : p * D + (g + 1) * OWN].astype(F32) * gain_a[...]).astype(BF16)
            for p in range(3)
        ]
        parts.append(mlp[:, g * OWN_FF : (g + 1) * OWN_FF])
        parts += [
            (both[:, p * FF + g * OWN_FF : p * FF + (g + 1) * OWN_FF].astype(F32) * gain_m[...]).astype(
                BF16
            )
            for p in range(2)
        ]
        parts.append(jnp.zeros((qkv.shape[0], WIDE - 3 * OWN_FF), BF16))
        out[g] = jnp.concatenate(parts, axis=1)


def back_ff_kernel(cells, weight, gain, grad_mlp, grad_in, grad_gain):
    total = jnp.zeros(grad_gain.shape, F32)
    for g in range(GROUP):
        block = cells[g].astype(F32)
        grad_mlp[:, g * OWN_FF : (g + 1) * OWN_FF] = block[:, :OWN_FF]
        for p in range(2):
            raw = block[:, (p + 1) * OWN_FF : (p + 2) * OWN_FF]
            at = slice(p * FF + g * OWN_FF, p * FF + (g + 1) * OWN_FF)
            total = total + jnp.sum(raw * weight[:, at].astype(F32), axis=1, keepdims=True)
            grad_in[:, at] = raw * gain[...]
    grad_gain[...] = total


def back_qkv_kernel(cells, weight, gain, grad, grad_gain):
    total = jnp.zeros(grad_gain.shape, F32)
    for g in range(GROUP):
        block = cells[g].astype(F32)
        for p in range(3):
            raw = block[:, p * OWN : (p + 1) * OWN]
            at = slice(p * D + g * OWN, p * D + (g + 1) * OWN)
            total = total + jnp.sum(raw * weight[:, at].astype(F32), axis=1, keepdims=True)
            grad[:, at] = raw * gain[...]
    grad_gain[...] = total


def columns_of(qkv, mlp, both, gain_a, gain_m):
    rows = qkv.shape[0]
    if direct():
        shape = like((GROUP, rows, 3 * OWN + WIDE), BF16)
        cells = local_kernel(columns_kernel, [shape], (qkv, mlp, both, gain_a, gain_m))[0]
        return cells.reshape(2, 2, rows, -1)

    def columns(w, parts, width):
        cells = w.reshape(rows, parts, 2, 2, width).transpose(2, 3, 0, 1, 4)
        return cells.reshape(2, 2, rows, parts * width)

    return jnp.concatenate(
        [
            columns((qkv.astype(F32) * gain_a).astype(BF16), 3, OWN),
            columns(mlp, 1, OWN_FF),
            columns((both.astype(F32) * gain_m).astype(BF16), 2, OWN_FF),
            jnp.zeros((2, 2, rows, WIDE - 3 * OWN_FF), BF16),
        ],
        axis=-1,
    )


def back_columns(cells, parts, width):
    rows = cells.shape[2]
    cells = cells.reshape(2, 2, rows, parts, width).transpose(2, 3, 0, 1, 4)
    return cells.reshape(rows, parts * GROUP * width).astype(F32)


def back_ff(cells, weight, gain):
    rows = weight.shape[0]
    if direct():
        outs = [like((rows, FF), F32), like((rows, 2 * FF), F32), like((rows, 1), F32)]
        return local_kernel(back_ff_kernel, outs, (cells.reshape(GROUP, rows, WIDE), weight, gain))
    raw = back_columns(cells[..., OWN_FF : 3 * OWN_FF], 2, OWN_FF)
    grad_gain = jnp.sum(raw * weight.astype(F32), axis=1, keepdims=True)
    return back_columns(cells[..., :OWN_FF], 1, OWN_FF), raw * gain, grad_gain


def back_qkv(cells, weight, gain):
    rows = weight.shape[0]
    if direct():
        outs = [like((rows, 3 * D), F32), like((rows, 1), F32)]
        return local_kernel(back_qkv_kernel, outs, (cells.reshape(GROUP, rows, -1), weight, gain))
    raw = back_columns(cells, 3, OWN)
    return raw * gain, jnp.sum(raw * weight.astype(F32), axis=1, keepdims=True)


def x_blocks(cells, got):
    high = (lax.axis_index("seq") & 1) == 1
    blocks = []
    for i in range(cells.shape[0]):
        blocks += [jnp.where(high, got[i], cells[i]), jnp.where(high, cells[i], got[i])]
    return blocks


def x_parts(blocks):
    high = (lax.axis_index("seq") & 1) == 1
    pairs = list(zip(blocks[::2], blocks[1::2]))
    kept = jnp.stack([jnp.where(high, b, a) for a, b in pairs])
    sent = jnp.stack([jnp.where(high, a, b) for a, b in pairs])
    return kept, sent


def assemble(cells, got):
    if direct():
        shape = like((cells.shape[1], D), BF16)
        return local_kernel(lane_assemble_kernel, [shape], (cells, got, place_of_device()))[0]
    return jnp.concatenate(x_blocks(cells, got), axis=-1)


def split(grad):
    count = lax.axis_size("seq")
    size = D // count
    if direct():
        shape = like((4, grad.shape[0], size), BF16)
        return local_kernel(lane_split_kernel, [shape, shape], (grad, place_of_device()))
    return x_parts([grad[:, i * size : (i + 1) * size] for i in range(count)])


def assemble_rows(cells, got):
    if direct():
        shape = like((8,) + cells.shape[1:], BF16)
        return local_kernel(row_assemble_kernel, [shape], (cells, got, place_of_device()))[0]
    return jnp.stack(x_blocks(cells, got))


def split_rows(cells):
    if direct():
        shape = like((4,) + cells.shape[1:], BF16)
        return local_kernel(row_split_kernel, [shape, shape], (cells, place_of_device()))
    return x_parts([cells[i] for i in range(cells.shape[0])])


def turn(cells, sizes):
    if direct():
        return local_kernel(turn_kernel, [like((n, cells.shape[0]), BF16) for n in sizes], (cells,))
    turned, outs, at = cells.T, [], 0
    for n in sizes:
        outs.append(turned[at : at + n])
        at += n
    return outs


def turn_back(chunks, width):
    if direct():
        lanes = chunks[0][0].shape[1]
        return local_kernel(
            turn_back_kernel,
            [like((lanes, width), BF16)],
            tuple(c for chunk in chunks for c in chunk),
            [pltpu.VMEM((width, lanes), F32)],
        )[0]
    turned = jnp.concatenate([total_of(c) for c in chunks], axis=0).T.astype(BF16)
    return jnp.pad(turned, ((0, 0), (0, width - turned.shape[1])))


def place(index, seq_lengths):
    count = seq_lengths.shape[0]
    ids = jnp.arange(count, dtype=jnp.int32)
    ends = jnp.sum(jnp.where(ids[None, :] <= ids[:, None], seq_lengths[None, :], 0), axis=1)
    starts = ends - seq_lengths
    segment = jnp.sum((index[:, None] >= ends[None, :]).astype(jnp.int32), axis=1)
    begins = jnp.sum(jnp.where(segment[:, None] == ids[None, :], starts[None, :], 0), axis=1)
    return segment, index - begins


def angles(position):
    freqs = 10000.0 ** (-(jnp.arange(HDIM // 2, dtype=F32) * 2.0) / HDIM)
    freqs = jnp.concatenate([freqs] * 4)
    turns = position.astype(F32)[:, None] * freqs[None, :]
    sign = jnp.where(jnp.arange(128) % HDIM < HDIM // 2, -1.0, 1.0)
    return jnp.cos(turns), jnp.sin(turns) * sign[None, :]


def normalize(values):
    average = jnp.mean(values, axis=-1, keepdims=True)
    centered = values - average
    variance = jnp.mean(centered * centered, axis=-1, keepdims=True)
    inverse = lax.rsqrt(variance + EPSILON)
    return centered * inverse, inverse


def norm_back(grad_hat, normed, inverse):
    return inverse * (
        grad_hat
        - jnp.mean(grad_hat, axis=-1, keepdims=True)
        - normed * jnp.mean(grad_hat * normed, axis=-1, keepdims=True)
    )


def geglu(gate_in, up_in):
    return jax.nn.gelu(gate_in, approximate=False) * up_in


def contract(left, right, dims, out=F32):
    return lax.dot_general(left, right, ((dims[0], dims[1]), ((), ())), preferred_element_type=out)


def rows_dot(left, right):
    return contract(left, right, ((0,), (0,)))


def cols_dot(left, right):
    return contract(left, right, ((1,), (1,)))


def half_swap(values):
    lane = lax.broadcasted_iota(jnp.int32, values.shape, 1)
    left = pltpu.roll(values, 128 - HDIM // 2, 1)
    right = pltpu.roll(values, HDIM // 2, 1)
    return jnp.where(lane % HDIM < HDIM // 2, left, right)


def bias_of(q_seg, k_seg, block):
    row = lax.broadcasted_iota(jnp.int32, (128, 256), 0)
    col = lax.broadcasted_iota(jnp.int32, (128, 256), 1)
    near = jnp.abs(row + HALF - col) <= HALF
    same = q_seg[pl.ds(block * 128, 128), :] == k_seg[:, pl.ds(block * 128, 256)]
    return jnp.where(near & same, 0.0, MASKED)


def softmax_of(scores):
    exponent = jnp.exp(scores - jnp.max(scores, axis=-1, keepdims=True))
    return exponent * (1.0 / jnp.sum(exponent, axis=-1, keepdims=True))


def attend_kernel(packed, cosine, sine, q_seg, k_seg, query, keys, values, attended, bias):
    rows = query.shape[0]
    blocks = rows // 128
    for b in range(blocks):
        bias[b] = bias_of(q_seg, k_seg, b)
    first = lax.broadcasted_iota(jnp.int32, (1, 128), 1) < HDIM
    for p in range(OWN_HEADS // 2):
        at = slice(p * 128, (p + 1) * 128)
        u = packed[HALF : HALF + rows, at]
        q_cos, q_sin = cosine[HALF : HALF + rows, :], sine[HALF : HALF + rows, :]
        query[:, at] = (u * q_cos + half_swap(u) * q_sin).astype(BF16)
        u = packed[:, OWN + p * 128 : OWN + (p + 1) * 128]
        keys[:, at] = (u * cosine[...] + half_swap(u) * sine[...]).astype(BF16)
        values[:, at] = packed[:, 2 * OWN + p * 128 : 2 * OWN + (p + 1) * 128].astype(BF16)
        for b in range(blocks):
            q = query[b * 128 : (b + 1) * 128, at]
            k = keys[b * 128 : b * 128 + 256, at]
            v = values[b * 128 : b * 128 + 256, at]
            outs = []
            for side in (first, ~first):
                q_one = jnp.where(side, q, jnp.zeros_like(q))
                scores = contract(q_one, k, ((1,), (1,))) * (HDIM**-0.5) + bias[b]
                prob = softmax_of(scores).astype(BF16)
                outs.append(contract(prob, v, ((1,), (0,))))
            attended[b * 128 : (b + 1) * 128, at] = jnp.where(first, outs[0], outs[1]).astype(BF16)


def attend_back_kernel(
    query, keys, values, grad, cosine, sine, q_seg, k_seg, grad_q, grad_k, grad_v, bias
):
    rows = query.shape[0]
    blocks = rows // 128
    scale = HDIM**-0.5
    for b in range(blocks):
        bias[b] = bias_of(q_seg, k_seg, b)
    first = lax.broadcasted_iota(jnp.int32, (1, 128), 1) < HDIM
    grad_k[...] = jnp.zeros_like(grad_k)
    grad_v[...] = jnp.zeros_like(grad_v)
    for p in range(OWN_HEADS // 2):
        at = slice(p * 128, (p + 1) * 128)
        for b in range(blocks):
            here, span = slice(b * 128, (b + 1) * 128), slice(b * 128, b * 128 + 256)
            q, go = query[here, at], grad[here, at]
            k, v = keys[span, at], values[span, at]
            d_q = jnp.zeros((128, 128), F32)
            d_k = jnp.zeros((256, 128), F32)
            d_v = jnp.zeros((256, 128), F32)
            for side in (first, ~first):
                q_one = jnp.where(side, q, jnp.zeros_like(q))
                k_one = jnp.where(side, k, jnp.zeros_like(k))
                go_one = jnp.where(side, go, jnp.zeros_like(go))
                scores = contract(q_one, k, ((1,), (1,))) * scale + bias[b]
                prob = softmax_of(scores)
                grad_prob = contract(go_one, v, ((1,), (1,)))
                inner = jnp.sum(grad_prob * prob, axis=-1, keepdims=True)
                grad_scores = (prob * (grad_prob - inner)).astype(BF16)
                d_q = d_q + contract(grad_scores, k_one, ((1,), (0,)))
                d_k = d_k + contract(grad_scores, q_one, ((0,), (0,)))
                d_v = d_v + contract(prob.astype(BF16), go_one, ((0,), (0,)))
            d_q = d_q * scale
            at_q = slice(HALF + b * 128, HALF + (b + 1) * 128)
            turned = d_q * cosine[at_q, :] - half_swap(d_q) * sine[at_q, :]
            grad_q[here, at] = turned.astype(BF16)
            grad_k[span, at] += d_k * scale
            grad_v[span, at] += d_v
        d_k = grad_k[:, at]
        grad_k[:, at] = d_k * cosine[...] - half_swap(d_k) * sine[...]


def call_kernel(kernel, outs, blocks, flops, args):
    moved = sum(a.size * a.dtype.itemsize for a in args) + sum(
        o.size * o.dtype.itemsize for o in outs
    )
    return pl.pallas_call(
        kernel,
        out_shape=outs,
        in_specs=[pl.BlockSpec(memory_space=pltpu.VMEM)] * len(args),
        out_specs=[pl.BlockSpec(memory_space=pltpu.VMEM)] * len(outs),
        scratch_shapes=[pltpu.VMEM((blocks, 128, 256), F32)],
        compiler_params=pltpu.CompilerParams(vmem_limit_bytes=VMEM_LIMIT),
        cost_estimate=pl.CostEstimate(flops=flops, bytes_accessed=moved, transcendentals=0),
    )(*args)


def like(shape, dtype):
    return jax.ShapeDtypeStruct(shape, dtype)


def on_device(
    tokens, cotangent, seq_lengths, w_qkv, w_attn_out, w_in, w_mlp_out, gain_attn, gain_mlp
):
    share = tokens.shape[0]
    rows = GROUP * share
    seq, seqs = lax.axis_index("seq"), lax.axis_size("seq")
    total = seqs * rows
    shard = w_qkv.shape[0]
    tie = lax.optimization_barrier

    def close(first, last):
        first = tie(first)
        return tie((first, last))


    gain_a = gain_attn.astype(F32)[:, None]
    gain_m = gain_mlp.astype(F32)[:, None]

    last = (lax.axis_index("fy") == 1) & (lax.axis_index("core") == 1)
    meetings = range(GROUP - 1, lax.axis_size(ALL) - 1, GROUP)
    swaps = [(i, i + 1) for i in meetings] + [(i + 1, i) for i in meetings]
    edge = lax.ppermute(jnp.where(last, tokens[share - HALF :], tokens[:HALF]), ALL, swaps)
    attn_z = z_gather(w_attn_out)
    cells = columns_of(w_qkv, w_mlp_out, w_in, gain_a, gain_m)
    cells = trade(trade(cells, "fy", 0), "core", 1).reshape(GROUP * shard, -1)
    qkv, mlp, gate, up = turn(cells, (3 * OWN, OWN_FF, OWN_FF, OWN_FF))
    attn_z, qkv, mlp, gate, up, edge, cotangent_in = tie(
        (attn_z, qkv, mlp, gate, up, edge, cotangent)
    )
    qkv_z = z_gather(qkv)
    attn_x = send_seq(attn_z, 1)
    ours = tokens.astype(F32)
    normed, inverse = normalize(ours)
    hidden = jnp.concatenate([normed, normalize(edge.astype(F32))[0]], axis=0).astype(BF16)
    hidden = join(hidden, "fy", 0)
    cot = join(cotangent_in, "fy", 0)
    (attn_x, hidden, cot, mlp, gate, up), qkv_z = close((attn_x, hidden, cot, mlp, gate, up), qkv_z)
    mlp_z = z_gather(mlp)
    qkv_x = send_seq(qkv_z, 1)
    attn = assemble_rows(attn_z, attn_x).reshape(2, 2, seqs // 4, shard, D)
    hidden = core_rows(hidden).reshape(GROUP, share + HALF, D)
    attn = trade(attn, "core", 1)
    (qkv_x, attn, hidden, gate), mlp_z = close((qkv_x, attn, hidden, gate), mlp_z)
    gate_z = z_gather(gate)
    mlp_x = send_seq(mlp_z, 1)
    attn = trade(attn, "fy", 0)
    before, after = hidden[0, share:], hidden[GROUP - 1, share:]
    hidden = hidden[:, :share].reshape(rows, D)
    wide = jnp.concatenate([before, hidden, after], axis=0)
    qkv_full = assemble(qkv_z, qkv_x)
    index = seq * rows - HALF + jnp.arange(rows + 2 * HALF, dtype=jnp.int32)
    segment, position = place(jnp.clip(index, 0, total - 1), seq_lengths)
    segment = jnp.where((index >= 0) & (index < total), segment, -1)
    q_seg = segment[HALF : HALF + rows][:, None]
    k_seg = segment[None, :]
    cosine, sine = angles(position)
    packed = cols_dot(wide, qkv_full)
    blocks = rows // 128
    flops = blocks * OWN_HEADS * 128 * 256 * 128 * 4
    query, keys, values, attended = call_kernel(
        attend_kernel,
        [
            like((rows, OWN), BF16),
            like((rows + 2 * HALF, OWN), BF16),
            like((rows + 2 * HALF, OWN), BF16),
            like((rows, OWN), BF16),
        ],
        blocks,
        flops,
        (packed, cosine, sine, q_seg, k_seg),
    )
    (mlp_x, attended, attn, up), gate_z = close((mlp_x, attended, attn, up), gate_z)
    up_z = z_gather(up)
    gate_x = send_seq(gate_z, 1)
    attn_full = attn.transpose(2, 0, 1, 3, 4).reshape(OWN, D)
    part = jnp.dot(attended, attn_full, preferred_element_type=F32)
    middle = ours + group_sum(part, share)
    mlp_full = assemble(mlp_z, mlp_x)
    (gate_x, middle, mlp_full), up_z = close((gate_x, middle, mlp_full), up_z)
    up_x = send_seq(up_z, 1)
    normed_mid, inverse_mid = normalize(middle)
    lifted = join(normed_mid.astype(BF16), "fy", 0)
    gate_full = assemble(gate_z, gate_x)
    up_x, lifted, gate_full = tie((up_x, lifted, gate_full))
    lifted, cot = tie((core_rows(lifted), core_rows(cot)))
    grad_mixed = cols_dot(cot, mlp_full)
    gate = cols_dot(lifted, gate_full)
    up_full = assemble(up_z, up_x)
    up = cols_dot(lifted, up_full)
    gate, up = tie((gate, up))
    mixed = geglu(gate, up).astype(BF16)

    unused, gelu_back = jax.vjp(geglu, gate, up)
    grad_gate, grad_up = gelu_back(grad_mixed)
    grad_gate, grad_up = grad_gate.astype(BF16), grad_up.astype(BF16)
    mlp_kept, mlp_sent = split(rows_dot(mixed, cot).astype(BF16))
    mlp_kept, mlp_sent, grad_gate, grad_up = tie((mlp_kept, mlp_sent, grad_gate, grad_up))
    mlp_x = send_seq(mlp_sent, 1)
    part_lifted = jnp.dot(grad_gate, gate_full, preferred_element_type=F32) + jnp.dot(
        grad_up, up_full, preferred_element_type=F32
    )
    half_hat = reduce_pair(part_lifted.reshape(2, 2, share, D), "core", 1)
    half_hat, grad_gate, grad_up = tie((half_hat, grad_gate, grad_up))
    grad_hat = reduce_pair(half_hat, "fy", 0)
    gate_kept, gate_sent = split(rows_dot(grad_gate, lifted).astype(BF16))
    up_kept, up_sent = split(rows_dot(grad_up, lifted).astype(BF16))
    mlp_x, gate_sent, up_sent, grad_hat = tie((mlp_x, gate_sent, up_sent, grad_hat))
    mlp_got = z_spread(x_sum(mlp_kept, mlp_x))
    gate_x = send_seq(gate_sent, 1)
    grad_middle = cotangent.astype(F32) + norm_back(grad_hat, normed_mid, inverse_mid)
    grad_attn = join(grad_middle.astype(BF16), "fy", 0)
    (gate_x, grad_attn, attended), mlp_got = close((gate_x, grad_attn, attended), mlp_got)
    gate_got = z_spread(x_sum(gate_kept, gate_x))
    up_x = send_seq(up_sent, 1)
    grad_attn = core_rows(grad_attn)
    grad_attended = cols_dot(grad_attn, attn_full).astype(BF16)
    grad_q, grad_k, grad_v = call_kernel(
        attend_back_kernel,
        [
            like((rows, OWN), BF16),
            like((rows + 2 * HALF, OWN), F32),
            like((rows + 2 * HALF, OWN), F32),
        ],
        blocks,
        flops * 3,
        (query, keys, values, grad_attended, cosine, sine, q_seg, k_seg),
    )
    grad_kv = jnp.concatenate([grad_k, grad_v], axis=1)
    attn_g = rows_dot(attended, grad_attn).astype(BF16)
    attn_g = attn_g.reshape(seqs // 4, 2, 2, shard, D).transpose(1, 2, 0, 3, 4)
    attn_g = trade(attn_g, "core", 1)
    part_out = jnp.dot(mixed, mlp_full, preferred_element_type=F32)
    (up_x, grad_kv, attn_g, part_out), gate_got = close((up_x, grad_kv, attn_g, part_out), gate_got)
    up_got = z_spread(x_sum(up_kept, up_x))
    ahead = [(i, i + 1) for i in range(seqs - 1)]
    behind = [(i + 1, i) for i in range(seqs - 1)]
    low_edge = lax.ppermute(grad_kv[:HALF].astype(BF16), "seq", behind)
    high_edge = lax.ppermute(grad_kv[HALF + rows :].astype(BF16), "seq", ahead)
    attn_g = trade(attn_g, "fy", 0).reshape(seqs, shard, D)
    middle_kv = grad_kv[HALF : HALF + rows]
    gap = jnp.zeros((rows - 2 * HALF, 2 * OWN), F32)
    edges = jnp.concatenate([high_edge.astype(F32), gap, low_edge.astype(F32)], axis=0)
    grad_packed = jnp.concatenate([grad_q, (middle_kv + edges).astype(BF16)], axis=1)
    qkv_kept, qkv_sent = split(rows_dot(grad_packed, hidden).astype(BF16))
    (attn_g, qkv_sent, grad_packed), up_got = close((attn_g, qkv_sent, grad_packed), up_got)
    qkv_x = send_seq(qkv_sent, 1)
    rest_g = turn_back([mlp_got, gate_got, up_got], WIDE).reshape(2, 2, shard, -1)
    rest_g = trade(rest_g, "fy", 0)
    attn_kept, attn_sent = split_rows(attn_g)
    part_hidden = jnp.dot(grad_packed, qkv_full, preferred_element_type=F32)
    parts = jnp.stack([part_hidden, part_out]).reshape(2, 2, 2, share, D)
    qkv_x, rest_g, parts, attn_sent = tie((qkv_x, rest_g, parts, attn_sent))
    qkv_got = z_spread(x_sum(qkv_kept, qkv_x))
    attn_x = send_seq(attn_sent, 1)

    rest_g = trade(rest_g, "core", 1)
    grad_mlp_out, grad_w_in, grad_gain_mlp = back_ff(rest_g, w_in, gain_m)
    grad_hidden, sum_out = reduce_pair(reduce_pair(parts, "core", 2), "fy", 1)
    output = (middle + sum_out).astype(BF16)
    input_grad = grad_middle + norm_back(grad_hidden, normed, inverse)
    attn_x, qkv_got, output, input_grad, grad_mlp_out, grad_w_in, grad_gain_mlp = tie(
        (attn_x, qkv_got, output, input_grad, grad_mlp_out, grad_w_in, grad_gain_mlp)
    )
    attn_got = z_spread(x_sum(attn_kept, attn_x))
    qkv_g = turn_back([qkv_got], 3 * OWN).reshape(2, 2, shard, -1)
    qkv_g = trade(trade(qkv_g, "fy", 0), "core", 1)
    grad_w_qkv, grad_gain_attn = back_qkv(qkv_g, w_qkv, gain_a)
    grad_attn_out = total_of(attn_got)
    return (
        output,
        input_grad,
        grad_w_qkv,
        grad_attn_out,
        grad_w_in,
        grad_mlp_out,
        grad_gain_attn[:, 0],
        grad_gain_mlp[:, 0],
    )


def solution(mesh):
    split = Mesh(mesh.devices.reshape(mesh.shape["seq"], -1, 2), ALL)
    two, one = P(ALL, None), P(ALL)
    return jax.shard_map(
        on_device,
        mesh=split,
        in_specs=(two, two, P(), two, two, two, two, one, one),
        out_specs=(two, two, two, two, two, two, one, one),
        check_vma=False,
    )
```

```python
import jax
import jax.numpy as jnp
from jax import lax
from jax.experimental import pallas as pl
from jax.experimental.pallas import tpu as pltpu
from jax.sharding import Mesh, PartitionSpec as P

D = 1024
HEADS = 16
HDIM = 64
FF = 2624
HALF = 64
GROUP = 4
OWN_HEADS = HEADS // GROUP
OWN = OWN_HEADS * HDIM
OWN_FF = FF // GROUP
WIDE = 2048
VMEM_LIMIT = 48 * 1024 * 1024

EPSILON = 1e-05
MASKED = -1e30
ALL = ("seq", "fy", "core")
BF16 = jnp.bfloat16
F32 = jnp.float32


def flat_pairs(change):
    count = lax.axis_size(ALL)
    return [(i, change(i)) for i in range(count)]


def send_seq(cells, flip):
    return lax.ppermute(cells, ALL, flat_pairs(lambda i: i ^ (flip * GROUP)))


def trade(cells, axis, dim):
    me = lax.axis_index(axis)
    kept = lax.dynamic_slice_in_dim(cells, me, 1, axis=dim)
    sent = lax.dynamic_slice_in_dim(cells, 1 - me, 1, axis=dim)
    got = lax.ppermute(sent, axis, [(0, 1), (1, 0)])
    low = me == 0
    return jnp.concatenate([jnp.where(low, kept, got), jnp.where(low, got, kept)], axis=dim)


def join(cells, axis, dim):
    me = lax.axis_index(axis)
    got = lax.ppermute(cells, axis, [(0, 1), (1, 0)])
    low = me == 0
    return jnp.stack([jnp.where(low, cells, got), jnp.where(low, got, cells)], axis=dim)


def reduce_pair(cells, axis, dim):
    me = lax.axis_index(axis)
    kept = lax.dynamic_index_in_dim(cells, me, dim, keepdims=False)
    sent = lax.dynamic_index_in_dim(cells, 1 - me, dim, keepdims=False).astype(BF16)
    got = lax.ppermute(sent, axis, [(0, 1), (1, 0)])
    return kept.astype(F32) + got.astype(F32)


def core_rows(cells):
    return join(cells, "core", 1).reshape((-1,) + cells.shape[2:])


def group_rows(cells):
    return core_rows(join(cells, "fy", 0))


def group_sum(part, rows):
    cells = part.reshape(2, 2, rows, part.shape[-1])
    return reduce_pair(reduce_pair(cells, "core", 1), "fy", 0)


def depth_of():
    return lax.axis_size("seq") // 2


def direct():
    return lax.axis_size("seq") == 8


def place_of_device():
    seq = lax.axis_index("seq")
    return jnp.stack([seq >> 1, seq & 1]).astype(jnp.int32)


def z_gather(cells):
    if direct():
        return jnp.stack([cells] + [send_seq(cells, 2 * d) for d in range(1, 4)])
    cells, me = cells[None], lax.axis_index("seq") >> 1
    flip = 1
    while flip < depth_of():
        other = send_seq(cells, 2 * flip)
        high = (me & flip) != 0
        cells = jnp.concatenate([jnp.where(high, other, cells), jnp.where(high, cells, other)])
        flip *= 2
    return cells


def x_sum(kept, got):
    return (kept.astype(F32) + got.astype(F32)).astype(BF16)


def z_spread(cells):
    if direct():
        return [cells[0]] + [send_seq(cells[d], 2 * d) for d in range(1, 4)]
    flip, me = depth_of() // 2, lax.axis_index("seq") >> 1
    while flip:
        high = ((me & flip) != 0).astype(jnp.int32)
        kept = lax.dynamic_slice_in_dim(cells, high * flip, flip, 0)
        sent = lax.dynamic_slice_in_dim(cells, (1 - high) * flip, flip, 0)
        cells = kept.astype(F32) + send_seq(sent.astype(BF16), 2 * flip).astype(F32)
        flip //= 2
    return [cells[0]]


def total_of(got):
    return sum(cells.astype(F32) for cells in got)


def feed_kernel(lifted, cot, gate_w, up_w, mlp_w, mixed, grad_gate, grad_up):
    for r in range(0, lifted.shape[0], 128):
        at = slice(r, r + 128)
        gate = cols_dot(lifted[at, :], gate_w[...])
        up = cols_dot(lifted[at, :], up_w[...])
        grad = cols_dot(cot[at, :], mlp_w[...])
        share = 0.5 + 0.5 * lax.erf(gate * (0.5**0.5))
        slope = share + gate * jnp.exp(-0.5 * gate * gate) * ((0.5 / jnp.pi) ** 0.5)
        gelu = gate * share
        mixed[at, :] = (gelu * up).astype(BF16)
        grad_gate[at, :] = (grad * up * slope).astype(BF16)
        grad_up[at, :] = (grad * gelu).astype(BF16)


def local_kernel(kernel, outs, args, scratch=()):
    spaces = [
        pltpu.SMEM if a.dtype == jnp.int32 and a.size == 2 else pltpu.VMEM for a in args
    ]
    moved = sum(a.size * a.dtype.itemsize for a in args)
    return pl.pallas_call(
        kernel,
        out_shape=outs,
        in_specs=[pl.BlockSpec(memory_space=s) for s in spaces],
        out_specs=[pl.BlockSpec(memory_space=pltpu.VMEM)] * len(outs),
        scratch_shapes=list(scratch),
        compiler_params=pltpu.CompilerParams(vmem_limit_bytes=VMEM_LIMIT),
        cost_estimate=pl.CostEstimate(flops=0, bytes_accessed=moved, transcendentals=0),
    )(*args)


def lane_assemble_kernel(cells, got, where, full):
    for d in range(4):
        z = where[0] ^ d
        mine = pl.multiple_of((2 * z + where[1]) * 128, 128)
        theirs = pl.multiple_of((2 * z + 1 - where[1]) * 128, 128)
        full[:, pl.ds(mine, 128)] = cells[d]
        full[:, pl.ds(theirs, 128)] = got[d]


def lane_split_kernel(full, where, kept, sent):
    for d in range(4):
        z = where[0] ^ d
        mine = pl.multiple_of((2 * z + where[1]) * 128, 128)
        theirs = pl.multiple_of((2 * z + 1 - where[1]) * 128, 128)
        kept[d] = full[:, pl.ds(mine, 128)]
        sent[d] = full[:, pl.ds(theirs, 128)]


def row_assemble_kernel(cells, got, where, full):
    for d in range(4):
        z = where[0] ^ d
        full[2 * z + where[1]] = cells[d]
        full[2 * z + 1 - where[1]] = got[d]


def row_split_kernel(full, where, kept, sent):
    for d in range(4):
        z = where[0] ^ d
        kept[d] = full[2 * z + where[1]]
        sent[d] = full[2 * z + 1 - where[1]]


def turn_kernel(cells, *outs):
    turned = cells[...].astype(F32).T.astype(BF16)
    at = 0
    for out in outs:
        out[...] = turned[at : at + out.shape[0]]
        at += out.shape[0]


def turn_back_kernel(*refs):
    *parts, out, full = refs
    at = 0
    full[...] = jnp.zeros_like(full)
    for i in range(0, len(parts), 4):
        total = parts[i][...].astype(F32)
        for j in range(1, 4):
            total = total + parts[i + j][...].astype(F32)
        full[at : at + total.shape[0], :] = total
        at += total.shape[0]
    out[...] = full[...].T.astype(out.dtype)


def columns_kernel(qkv, mlp, both, gain_a, gain_m, out):
    for g in range(GROUP):
        parts = [
            (qkv[:, p * D + g * OWN : p * D + (g + 1) * OWN].astype(F32) * gain_a[...]).astype(BF16)
            for p in range(3)
        ]
        parts.append(mlp[:, g * OWN_FF : (g + 1) * OWN_FF])
        parts += [
            (both[:, p * FF + g * OWN_FF : p * FF + (g + 1) * OWN_FF].astype(F32) * gain_m[...]).astype(
                BF16
            )
            for p in range(2)
        ]
        parts.append(jnp.zeros((qkv.shape[0], WIDE - 3 * OWN_FF), BF16))
        out[g] = jnp.concatenate(parts, axis=1)


def back_ff_kernel(cells, weight, gain, grad_mlp, grad_in, grad_gain):
    total = jnp.zeros(grad_gain.shape, F32)
    for g in range(GROUP):
        block = cells[g].astype(F32)
        grad_mlp[:, g * OWN_FF : (g + 1) * OWN_FF] = block[:, :OWN_FF]
        for p in range(2):
            raw = block[:, (p + 1) * OWN_FF : (p + 2) * OWN_FF]
            at = slice(p * FF + g * OWN_FF, p * FF + (g + 1) * OWN_FF)
            total = total + jnp.sum(raw * weight[:, at].astype(F32), axis=1, keepdims=True)
            grad_in[:, at] = raw * gain[...]
    grad_gain[...] = total


def back_qkv_kernel(cells, weight, gain, grad, grad_gain):
    total = jnp.zeros(grad_gain.shape, F32)
    for g in range(GROUP):
        block = cells[g].astype(F32)
        for p in range(3):
            raw = block[:, p * OWN : (p + 1) * OWN]
            at = slice(p * D + g * OWN, p * D + (g + 1) * OWN)
            total = total + jnp.sum(raw * weight[:, at].astype(F32), axis=1, keepdims=True)
            grad[:, at] = raw * gain[...]
    grad_gain[...] = total


def columns_of(qkv, mlp, both, gain_a, gain_m):
    rows = qkv.shape[0]
    if direct():
        shape = like((GROUP, rows, 3 * OWN + WIDE), BF16)
        cells = local_kernel(columns_kernel, [shape], (qkv, mlp, both, gain_a, gain_m))[0]
        return cells.reshape(2, 2, rows, -1)

    def columns(w, parts, width):
        cells = w.reshape(rows, parts, 2, 2, width).transpose(2, 3, 0, 1, 4)
        return cells.reshape(2, 2, rows, parts * width)

    return jnp.concatenate(
        [
            columns((qkv.astype(F32) * gain_a).astype(BF16), 3, OWN),
            columns(mlp, 1, OWN_FF),
            columns((both.astype(F32) * gain_m).astype(BF16), 2, OWN_FF),
            jnp.zeros((2, 2, rows, WIDE - 3 * OWN_FF), BF16),
        ],
        axis=-1,
    )


def back_columns(cells, parts, width):
    rows = cells.shape[2]
    cells = cells.reshape(2, 2, rows, parts, width).transpose(2, 3, 0, 1, 4)
    return cells.reshape(rows, parts * GROUP * width).astype(F32)


def back_ff(cells, weight, gain):
    rows = weight.shape[0]
    if direct():
        outs = [like((rows, FF), F32), like((rows, 2 * FF), F32), like((rows, 1), F32)]
        return local_kernel(back_ff_kernel, outs, (cells.reshape(GROUP, rows, WIDE), weight, gain))
    raw = back_columns(cells[..., OWN_FF : 3 * OWN_FF], 2, OWN_FF)
    grad_gain = jnp.sum(raw * weight.astype(F32), axis=1, keepdims=True)
    return back_columns(cells[..., :OWN_FF], 1, OWN_FF), raw * gain, grad_gain


def back_qkv(cells, weight, gain):
    rows = weight.shape[0]
    if direct():
        outs = [like((rows, 3 * D), F32), like((rows, 1), F32)]
        return local_kernel(back_qkv_kernel, outs, (cells.reshape(GROUP, rows, -1), weight, gain))
    raw = back_columns(cells, 3, OWN)
    return raw * gain, jnp.sum(raw * weight.astype(F32), axis=1, keepdims=True)


def x_blocks(cells, got):
    high = (lax.axis_index("seq") & 1) == 1
    blocks = []
    for i in range(cells.shape[0]):
        blocks += [jnp.where(high, got[i], cells[i]), jnp.where(high, cells[i], got[i])]
    return blocks


def x_parts(blocks):
    high = (lax.axis_index("seq") & 1) == 1
    pairs = list(zip(blocks[::2], blocks[1::2]))
    kept = jnp.stack([jnp.where(high, b, a) for a, b in pairs])
    sent = jnp.stack([jnp.where(high, a, b) for a, b in pairs])
    return kept, sent


def assemble(cells, got):
    if direct():
        shape = like((cells.shape[1], D), BF16)
        return local_kernel(lane_assemble_kernel, [shape], (cells, got, place_of_device()))[0]
    return jnp.concatenate(x_blocks(cells, got), axis=-1)


def split(grad):
    count = lax.axis_size("seq")
    size = D // count
    if direct():
        shape = like((4, grad.shape[0], size), BF16)
        return local_kernel(lane_split_kernel, [shape, shape], (grad, place_of_device()))
    return x_parts([grad[:, i * size : (i + 1) * size] for i in range(count)])


def assemble_rows(cells, got):
    if direct():
        shape = like((8,) + cells.shape[1:], BF16)
        return local_kernel(row_assemble_kernel, [shape], (cells, got, place_of_device()))[0]
    return jnp.stack(x_blocks(cells, got))


def split_rows(cells):
    if direct():
        shape = like((4,) + cells.shape[1:], BF16)
        return local_kernel(row_split_kernel, [shape, shape], (cells, place_of_device()))
    return x_parts([cells[i] for i in range(cells.shape[0])])


def turn(cells, sizes):
    if direct():
        return local_kernel(turn_kernel, [like((n, cells.shape[0]), BF16) for n in sizes], (cells,))
    turned, outs, at = cells.T, [], 0
    for n in sizes:
        outs.append(turned[at : at + n])
        at += n
    return outs


def turn_back(chunks, width):
    if direct():
        lanes = chunks[0][0].shape[1]
        return local_kernel(
            turn_back_kernel,
            [like((lanes, width), BF16)],
            tuple(c for chunk in chunks for c in chunk),
            [pltpu.VMEM((width, lanes), F32)],
        )[0]
    turned = jnp.concatenate([total_of(c) for c in chunks], axis=0).T.astype(BF16)
    return jnp.pad(turned, ((0, 0), (0, width - turned.shape[1])))


def place(index, seq_lengths):
    count = seq_lengths.shape[0]
    ids = jnp.arange(count, dtype=jnp.int32)
    ends = jnp.sum(jnp.where(ids[None, :] <= ids[:, None], seq_lengths[None, :], 0), axis=1)
    starts = ends - seq_lengths
    segment = jnp.sum((index[:, None] >= ends[None, :]).astype(jnp.int32), axis=1)
    begins = jnp.sum(jnp.where(segment[:, None] == ids[None, :], starts[None, :], 0), axis=1)
    return segment, index - begins


def angles(position):
    freqs = 10000.0 ** (-(jnp.arange(HDIM // 2, dtype=F32) * 2.0) / HDIM)
    freqs = jnp.concatenate([freqs] * 4)
    turns = position.astype(F32)[:, None] * freqs[None, :]
    sign = jnp.where(jnp.arange(128) % HDIM < HDIM // 2, -1.0, 1.0)
    return jnp.cos(turns), jnp.sin(turns) * sign[None, :]


def normalize(values):
    average = jnp.mean(values, axis=-1, keepdims=True)
    centered = values - average
    variance = jnp.mean(centered * centered, axis=-1, keepdims=True)
    inverse = lax.rsqrt(variance + EPSILON)
    return centered * inverse, inverse


def norm_back(grad_hat, normed, inverse):
    return inverse * (
        grad_hat
        - jnp.mean(grad_hat, axis=-1, keepdims=True)
        - normed * jnp.mean(grad_hat * normed, axis=-1, keepdims=True)
    )


def geglu(gate_in, up_in):
    return jax.nn.gelu(gate_in, approximate=False) * up_in


def contract(left, right, dims, out=F32):
    return lax.dot_general(left, right, ((dims[0], dims[1]), ((), ())), preferred_element_type=out)


def rows_dot(left, right):
    return contract(left, right, ((0,), (0,)))


def cols_dot(left, right):
    return contract(left, right, ((1,), (1,)))


def half_swap(values):
    lane = lax.broadcasted_iota(jnp.int32, values.shape, 1)
    left = pltpu.roll(values, 128 - HDIM // 2, 1)
    right = pltpu.roll(values, HDIM // 2, 1)
    return jnp.where(lane % HDIM < HDIM // 2, left, right)


def bias_of(q_seg, k_seg, block):
    row = lax.broadcasted_iota(jnp.int32, (128, 256), 0)
    col = lax.broadcasted_iota(jnp.int32, (128, 256), 1)
    near = jnp.abs(row + HALF - col) <= HALF
    same = q_seg[pl.ds(block * 128, 128), :] == k_seg[:, pl.ds(block * 128, 256)]
    return jnp.where(near & same, 0.0, MASKED)


def softmax_of(scores):
    exponent = jnp.exp(scores - jnp.max(scores, axis=-1, keepdims=True))
    return exponent * (1.0 / jnp.sum(exponent, axis=-1, keepdims=True))


def attend_kernel(packed, cosine, sine, q_seg, k_seg, query, keys, values, attended, bias):
    rows = query.shape[0]
    blocks = rows // 128
    for b in range(blocks):
        bias[b] = bias_of(q_seg, k_seg, b)
    first = lax.broadcasted_iota(jnp.int32, (1, 128), 1) < HDIM
    for p in range(OWN_HEADS // 2):
        at = slice(p * 128, (p + 1) * 128)
        u = packed[HALF : HALF + rows, at]
        q_cos, q_sin = cosine[HALF : HALF + rows, :], sine[HALF : HALF + rows, :]
        query[:, at] = (u * q_cos + half_swap(u) * q_sin).astype(BF16)
        u = packed[:, OWN + p * 128 : OWN + (p + 1) * 128]
        keys[:, at] = (u * cosine[...] + half_swap(u) * sine[...]).astype(BF16)
        values[:, at] = packed[:, 2 * OWN + p * 128 : 2 * OWN + (p + 1) * 128].astype(BF16)
        for b in range(blocks):
            q = query[b * 128 : (b + 1) * 128, at]
            k = keys[b * 128 : b * 128 + 256, at]
            v = values[b * 128 : b * 128 + 256, at]
            outs = []
            for side in (first, ~first):
                q_one = jnp.where(side, q, jnp.zeros_like(q))
                scores = contract(q_one, k, ((1,), (1,))) * (HDIM**-0.5) + bias[b]
                prob = softmax_of(scores).astype(BF16)
                outs.append(contract(prob, v, ((1,), (0,))))
            attended[b * 128 : (b + 1) * 128, at] = jnp.where(first, outs[0], outs[1]).astype(BF16)


def attend_back_kernel(
    query, keys, values, grad, cosine, sine, q_seg, k_seg, grad_q, grad_k, grad_v, bias
):
    rows = query.shape[0]
    blocks = rows // 128
    scale = HDIM**-0.5
    for b in range(blocks):
        bias[b] = bias_of(q_seg, k_seg, b)
    first = lax.broadcasted_iota(jnp.int32, (1, 128), 1) < HDIM
    grad_k[...] = jnp.zeros_like(grad_k)
    grad_v[...] = jnp.zeros_like(grad_v)
    for p in range(OWN_HEADS // 2):
        at = slice(p * 128, (p + 1) * 128)
        for b in range(blocks):
            here, span = slice(b * 128, (b + 1) * 128), slice(b * 128, b * 128 + 256)
            q, go = query[here, at], grad[here, at]
            k, v = keys[span, at], values[span, at]
            d_q = jnp.zeros((128, 128), F32)
            d_k = jnp.zeros((256, 128), F32)
            d_v = jnp.zeros((256, 128), F32)
            for side in (first, ~first):
                q_one = jnp.where(side, q, jnp.zeros_like(q))
                k_one = jnp.where(side, k, jnp.zeros_like(k))
                go_one = jnp.where(side, go, jnp.zeros_like(go))
                scores = contract(q_one, k, ((1,), (1,))) * scale + bias[b]
                prob = softmax_of(scores)
                grad_prob = contract(go_one, v, ((1,), (1,)))
                inner = jnp.sum(grad_prob * prob, axis=-1, keepdims=True)
                grad_scores = (prob * (grad_prob - inner)).astype(BF16)
                d_q = d_q + contract(grad_scores, k_one, ((1,), (0,)))
                d_k = d_k + contract(grad_scores, q_one, ((0,), (0,)))
                d_v = d_v + contract(prob.astype(BF16), go_one, ((0,), (0,)))
            d_q = d_q * scale
            at_q = slice(HALF + b * 128, HALF + (b + 1) * 128)
            turned = d_q * cosine[at_q, :] - half_swap(d_q) * sine[at_q, :]
            grad_q[here, at] = turned.astype(BF16)
            grad_k[span, at] += d_k * scale
            grad_v[span, at] += d_v
        d_k = grad_k[:, at]
        grad_k[:, at] = d_k * cosine[...] - half_swap(d_k) * sine[...]


def call_kernel(kernel, outs, blocks, flops, args):
    moved = sum(a.size * a.dtype.itemsize for a in args) + sum(
        o.size * o.dtype.itemsize for o in outs
    )
    return pl.pallas_call(
        kernel,
        out_shape=outs,
        in_specs=[pl.BlockSpec(memory_space=pltpu.VMEM)] * len(args),
        out_specs=[pl.BlockSpec(memory_space=pltpu.VMEM)] * len(outs),
        scratch_shapes=[pltpu.VMEM((blocks, 128, 256), F32)],
        compiler_params=pltpu.CompilerParams(vmem_limit_bytes=VMEM_LIMIT),
        cost_estimate=pl.CostEstimate(flops=flops, bytes_accessed=moved, transcendentals=0),
    )(*args)


def like(shape, dtype):
    return jax.ShapeDtypeStruct(shape, dtype)


def on_device(
    tokens, cotangent, seq_lengths, w_qkv, w_attn_out, w_in, w_mlp_out, gain_attn, gain_mlp
):
    share = tokens.shape[0]
    rows = GROUP * share
    seq, seqs = lax.axis_index("seq"), lax.axis_size("seq")
    total = seqs * rows
    shard = w_qkv.shape[0]
    tie = lax.optimization_barrier

    def close(first, last):
        first = tie(first)
        return tie((first, last))


    gain_a = gain_attn.astype(F32)[:, None]
    gain_m = gain_mlp.astype(F32)[:, None]

    last = (lax.axis_index("fy") == 1) & (lax.axis_index("core") == 1)
    meetings = range(GROUP - 1, lax.axis_size(ALL) - 1, GROUP)
    swaps = [(i, i + 1) for i in meetings] + [(i + 1, i) for i in meetings]
    edge = lax.ppermute(jnp.where(last, tokens[share - HALF :], tokens[:HALF]), ALL, swaps)
    attn_z = z_gather(w_attn_out)
    cells = columns_of(w_qkv, w_mlp_out, w_in, gain_a, gain_m)
    cells = trade(trade(cells, "fy", 0), "core", 1).reshape(GROUP * shard, -1)
    qkv, mlp, gate, up = turn(cells, (3 * OWN, OWN_FF, OWN_FF, OWN_FF))
    attn_z, qkv, mlp, gate, up, edge, cotangent_in = tie(
        (attn_z, qkv, mlp, gate, up, edge, cotangent)
    )
    qkv_z = z_gather(qkv)
    attn_x = send_seq(attn_z, 1)
    ours = tokens.astype(F32)
    normed, inverse = normalize(ours)
    hidden = jnp.concatenate([normed, normalize(edge.astype(F32))[0]], axis=0).astype(BF16)
    hidden = join(hidden, "fy", 0)
    cot = join(cotangent_in, "fy", 0)
    (attn_x, hidden, cot, mlp, gate, up), qkv_z = close((attn_x, hidden, cot, mlp, gate, up), qkv_z)
    mlp_z = z_gather(mlp)
    qkv_x = send_seq(qkv_z, 1)
    attn = assemble_rows(attn_z, attn_x).reshape(2, 2, seqs // 4, shard, D)
    hidden = core_rows(hidden).reshape(GROUP, share + HALF, D)
    attn = trade(attn, "core", 1)
    (qkv_x, attn, hidden, gate), mlp_z = close((qkv_x, attn, hidden, gate), mlp_z)
    gate_z = z_gather(gate)
    mlp_x = send_seq(mlp_z, 1)
    attn = trade(attn, "fy", 0)
    before, after = hidden[0, share:], hidden[GROUP - 1, share:]
    hidden = hidden[:, :share].reshape(rows, D)
    wide = jnp.concatenate([before, hidden, after], axis=0)
    qkv_full = assemble(qkv_z, qkv_x)
    index = seq * rows - HALF + jnp.arange(rows + 2 * HALF, dtype=jnp.int32)
    segment, position = place(jnp.clip(index, 0, total - 1), seq_lengths)
    segment = jnp.where((index >= 0) & (index < total), segment, -1)
    q_seg = segment[HALF : HALF + rows][:, None]
    k_seg = segment[None, :]
    cosine, sine = angles(position)
    packed = cols_dot(wide, qkv_full)
    blocks = rows // 128
    flops = blocks * OWN_HEADS * 128 * 256 * 128 * 4
    query, keys, values, attended = call_kernel(
        attend_kernel,
        [
            like((rows, OWN), BF16),
            like((rows + 2 * HALF, OWN), BF16),
            like((rows + 2 * HALF, OWN), BF16),
            like((rows, OWN), BF16),
        ],
        blocks,
        flops,
        (packed, cosine, sine, q_seg, k_seg),
    )
    (mlp_x, attended, attn, up), gate_z = close((mlp_x, attended, attn, up), gate_z)
    up_z = z_gather(up)
    gate_x = send_seq(gate_z, 1)
    attn_full = attn.transpose(2, 0, 1, 3, 4).reshape(OWN, D)
    part = jnp.dot(attended, attn_full, preferred_element_type=F32)
    middle = ours + group_sum(part, share)
    mlp_full = assemble(mlp_z, mlp_x)
    (gate_x, middle, mlp_full), up_z = close((gate_x, middle, mlp_full), up_z)
    up_x = send_seq(up_z, 1)
    normed_mid, inverse_mid = normalize(middle)
    lifted = join(normed_mid.astype(BF16), "fy", 0)
    gate_full = assemble(gate_z, gate_x)
    up_x, lifted, gate_full = tie((up_x, lifted, gate_full))
    lifted, cot = tie((core_rows(lifted), core_rows(cot)))
    up_full = assemble(up_z, up_x)
    shape = like((rows, OWN_FF), BF16)
    mixed, grad_gate, grad_up = local_kernel(
        feed_kernel, [shape] * 3, (lifted, cot, gate_full, up_full, mlp_full)
    )

    mlp_kept, mlp_sent = split(rows_dot(mixed, cot).astype(BF16))
    mlp_kept, mlp_sent, grad_gate, grad_up = tie((mlp_kept, mlp_sent, grad_gate, grad_up))
    mlp_x = send_seq(mlp_sent, 1)
    part_lifted = jnp.dot(grad_gate, gate_full, preferred_element_type=F32) + jnp.dot(
        grad_up, up_full, preferred_element_type=F32
    )
    half_hat = reduce_pair(part_lifted.reshape(2, 2, share, D), "core", 1)
    half_hat, grad_gate, grad_up = tie((half_hat, grad_gate, grad_up))
    grad_hat = reduce_pair(half_hat, "fy", 0)
    gate_kept, gate_sent = split(rows_dot(grad_gate, lifted).astype(BF16))
    up_kept, up_sent = split(rows_dot(grad_up, lifted).astype(BF16))
    mlp_x, gate_sent, up_sent, grad_hat = tie((mlp_x, gate_sent, up_sent, grad_hat))
    mlp_got = z_spread(x_sum(mlp_kept, mlp_x))
    gate_x = send_seq(gate_sent, 1)
    grad_middle = cotangent.astype(F32) + norm_back(grad_hat, normed_mid, inverse_mid)
    grad_attn = join(grad_middle.astype(BF16), "fy", 0)
    (gate_x, grad_attn, attended), mlp_got = close((gate_x, grad_attn, attended), mlp_got)
    gate_got = z_spread(x_sum(gate_kept, gate_x))
    up_x = send_seq(up_sent, 1)
    grad_attn = core_rows(grad_attn)
    grad_attended = cols_dot(grad_attn, attn_full).astype(BF16)
    grad_q, grad_k, grad_v = call_kernel(
        attend_back_kernel,
        [
            like((rows, OWN), BF16),
            like((rows + 2 * HALF, OWN), F32),
            like((rows + 2 * HALF, OWN), F32),
        ],
        blocks,
        flops * 3,
        (query, keys, values, grad_attended, cosine, sine, q_seg, k_seg),
    )
    grad_kv = jnp.concatenate([grad_k, grad_v], axis=1)
    attn_g = rows_dot(attended, grad_attn).astype(BF16)
    attn_g = attn_g.reshape(seqs // 4, 2, 2, shard, D).transpose(1, 2, 0, 3, 4)
    attn_g = trade(attn_g, "core", 1)
    part_out = jnp.dot(mixed, mlp_full, preferred_element_type=F32)
    (up_x, grad_kv, attn_g, part_out), gate_got = close((up_x, grad_kv, attn_g, part_out), gate_got)
    up_got = z_spread(x_sum(up_kept, up_x))
    ahead = [(i, i + 1) for i in range(seqs - 1)]
    behind = [(i + 1, i) for i in range(seqs - 1)]
    low_edge = lax.ppermute(grad_kv[:HALF].astype(BF16), "seq", behind)
    high_edge = lax.ppermute(grad_kv[HALF + rows :].astype(BF16), "seq", ahead)
    attn_g = trade(attn_g, "fy", 0).reshape(seqs, shard, D)
    middle_kv = grad_kv[HALF : HALF + rows]
    gap = jnp.zeros((rows - 2 * HALF, 2 * OWN), F32)
    edges = jnp.concatenate([high_edge.astype(F32), gap, low_edge.astype(F32)], axis=0)
    grad_packed = jnp.concatenate([grad_q, (middle_kv + edges).astype(BF16)], axis=1)
    qkv_kept, qkv_sent = split(rows_dot(grad_packed, hidden).astype(BF16))
    (attn_g, qkv_sent, grad_packed), up_got = close((attn_g, qkv_sent, grad_packed), up_got)
    qkv_x = send_seq(qkv_sent, 1)
    rest_g = turn_back([mlp_got, gate_got, up_got], WIDE).reshape(2, 2, shard, -1)
    rest_g = trade(rest_g, "fy", 0)
    attn_kept, attn_sent = split_rows(attn_g)
    part_hidden = jnp.dot(grad_packed, qkv_full, preferred_element_type=F32)
    parts = jnp.stack([part_hidden, part_out]).reshape(2, 2, 2, share, D)
    qkv_x, rest_g, parts, attn_sent = tie((qkv_x, rest_g, parts, attn_sent))
    qkv_got = z_spread(x_sum(qkv_kept, qkv_x))
    attn_x = send_seq(attn_sent, 1)

    rest_g = trade(rest_g, "core", 1)
    grad_mlp_out, grad_w_in, grad_gain_mlp = back_ff(rest_g, w_in, gain_m)
    grad_hidden, sum_out = reduce_pair(reduce_pair(parts, "core", 2), "fy", 1)
    output = (middle + sum_out).astype(BF16)
    input_grad = grad_middle + norm_back(grad_hidden, normed, inverse)
    attn_x, qkv_got, output, input_grad, grad_mlp_out, grad_w_in, grad_gain_mlp = tie(
        (attn_x, qkv_got, output, input_grad, grad_mlp_out, grad_w_in, grad_gain_mlp)
    )
    attn_got = z_spread(x_sum(attn_kept, attn_x))
    qkv_g = turn_back([qkv_got], 3 * OWN).reshape(2, 2, shard, -1)
    qkv_g = trade(trade(qkv_g, "fy", 0), "core", 1)
    grad_w_qkv, grad_gain_attn = back_qkv(qkv_g, w_qkv, gain_a)
    grad_attn_out = total_of(attn_got)
    return (
        output,
        input_grad,
        grad_w_qkv,
        grad_attn_out,
        grad_w_in,
        grad_mlp_out,
        grad_gain_attn[:, 0],
        grad_gain_mlp[:, 0],
    )


def solution(mesh):
    split = Mesh(mesh.devices.reshape(mesh.shape["seq"], -1, 2), ALL)
    two, one = P(ALL, None), P(ALL)
    return jax.shard_map(
        on_device,
        mesh=split,
        in_specs=(two, two, P(), two, two, two, two, one, one),
        out_specs=(two, two, two, two, two, two, one, one),
        check_vma=False,
    )
```

```python
import jax
import jax.numpy as jnp
from jax import lax
from jax.experimental import pallas as pl
from jax.experimental.pallas import tpu as pltpu
from jax.sharding import Mesh, PartitionSpec as P

D = 1024
HEADS = 16
HDIM = 64
FF = 2624
HALF = 64
GROUP = 4
OWN_HEADS = HEADS // GROUP
OWN = OWN_HEADS * HDIM
OWN_FF = FF // GROUP
WIDE = 2048
VMEM_LIMIT = 48 * 1024 * 1024

EPSILON = 1e-05
MASKED = -1e30
ALL = ("seq", "fy", "core")
BF16 = jnp.bfloat16
F32 = jnp.float32


def flat_pairs(change):
    count = lax.axis_size(ALL)
    return [(i, change(i)) for i in range(count)]


def send_seq(cells, flip):
    return lax.ppermute(cells, ALL, flat_pairs(lambda i: i ^ (flip * GROUP)))


def trade(cells, axis, dim):
    me = lax.axis_index(axis)
    kept = lax.dynamic_slice_in_dim(cells, me, 1, axis=dim)
    sent = lax.dynamic_slice_in_dim(cells, 1 - me, 1, axis=dim)
    got = lax.ppermute(sent, axis, [(0, 1), (1, 0)])
    low = me == 0
    return jnp.concatenate([jnp.where(low, kept, got), jnp.where(low, got, kept)], axis=dim)


def join(cells, axis, dim):
    me = lax.axis_index(axis)
    got = lax.ppermute(cells, axis, [(0, 1), (1, 0)])
    low = me == 0
    return jnp.stack([jnp.where(low, cells, got), jnp.where(low, got, cells)], axis=dim)


def reduce_pair(cells, axis, dim):
    me = lax.axis_index(axis)
    kept = lax.dynamic_index_in_dim(cells, me, dim, keepdims=False)
    sent = lax.dynamic_index_in_dim(cells, 1 - me, dim, keepdims=False).astype(BF16)
    got = lax.ppermute(sent, axis, [(0, 1), (1, 0)])
    return kept.astype(F32) + got.astype(F32)


def core_rows(cells):
    return join(cells, "core", 1).reshape((-1,) + cells.shape[2:])


def group_rows(cells):
    return core_rows(join(cells, "fy", 0))


def group_sum(part, rows):
    cells = part.reshape(2, 2, rows, part.shape[-1])
    return reduce_pair(reduce_pair(cells, "core", 1), "fy", 0)


def depth_of():
    return lax.axis_size("seq") // 2


def direct():
    return lax.axis_size("seq") == 8


def place_of_device():
    seq = lax.axis_index("seq")
    return jnp.stack([seq >> 1, seq & 1]).astype(jnp.int32)


def z_gather(cells):
    if direct():
        return jnp.stack([cells] + [send_seq(cells, 2 * d) for d in range(1, 4)])
    cells, me = cells[None], lax.axis_index("seq") >> 1
    flip = 1
    while flip < depth_of():
        other = send_seq(cells, 2 * flip)
        high = (me & flip) != 0
        cells = jnp.concatenate([jnp.where(high, other, cells), jnp.where(high, cells, other)])
        flip *= 2
    return cells


def x_sum(kept, got):
    return (kept.astype(F32) + got.astype(F32)).astype(BF16)


def z_spread(cells):
    if direct():
        return [cells[0]] + [send_seq(cells[d], 2 * d) for d in range(1, 4)]
    flip, me = depth_of() // 2, lax.axis_index("seq") >> 1
    while flip:
        high = ((me & flip) != 0).astype(jnp.int32)
        kept = lax.dynamic_slice_in_dim(cells, high * flip, flip, 0)
        sent = lax.dynamic_slice_in_dim(cells, (1 - high) * flip, flip, 0)
        cells = kept.astype(F32) + send_seq(sent.astype(BF16), 2 * flip).astype(F32)
        flip //= 2
    return [cells[0]]


def total_of(got):
    return sum(cells.astype(F32) for cells in got)


def feed_kernel(lifted, cot, gate_w, up_w, mlp_w, mixed, grad_gate, grad_up):
    for r in range(0, lifted.shape[0], 128):
        at = slice(r, r + 128)
        gate = cols_dot(lifted[at, :], gate_w[...])
        up = cols_dot(lifted[at, :], up_w[...])
        grad = cols_dot(cot[at, :], mlp_w[...])
        share = 0.5 + 0.5 * lax.erf(gate * (0.5**0.5))
        slope = share + gate * jnp.exp(-0.5 * gate * gate) * ((0.5 / jnp.pi) ** 0.5)
        gelu = gate * share
        mixed[at, :] = (gelu * up).astype(BF16)
        grad_gate[at, :] = (grad * up * slope).astype(BF16)
        grad_up[at, :] = (grad * gelu).astype(BF16)


def local_kernel(kernel, outs, args, scratch=()):
    spaces = [
        pltpu.SMEM if a.dtype == jnp.int32 and a.size == 2 else pltpu.VMEM for a in args
    ]
    moved = sum(a.size * a.dtype.itemsize for a in args)
    return pl.pallas_call(
        kernel,
        out_shape=outs,
        in_specs=[pl.BlockSpec(memory_space=s) for s in spaces],
        out_specs=[pl.BlockSpec(memory_space=pltpu.VMEM)] * len(outs),
        scratch_shapes=list(scratch),
        compiler_params=pltpu.CompilerParams(vmem_limit_bytes=VMEM_LIMIT),
        cost_estimate=pl.CostEstimate(flops=0, bytes_accessed=moved, transcendentals=0),
    )(*args)


def lane_assemble_kernel(cells, got, where, full):
    for d in range(4):
        z = where[0] ^ d
        mine = pl.multiple_of((2 * z + where[1]) * 128, 128)
        theirs = pl.multiple_of((2 * z + 1 - where[1]) * 128, 128)
        full[:, pl.ds(mine, 128)] = cells[d]
        full[:, pl.ds(theirs, 128)] = got[d]


def lane_split_kernel(full, where, kept, sent):
    for d in range(4):
        z = where[0] ^ d
        mine = pl.multiple_of((2 * z + where[1]) * 128, 128)
        theirs = pl.multiple_of((2 * z + 1 - where[1]) * 128, 128)
        kept[d] = full[:, pl.ds(mine, 128)]
        sent[d] = full[:, pl.ds(theirs, 128)]


def row_assemble_kernel(cells, got, where, full):
    for d in range(4):
        z = where[0] ^ d
        full[2 * z + where[1]] = cells[d]
        full[2 * z + 1 - where[1]] = got[d]


def row_split_kernel(full, where, kept, sent):
    for d in range(4):
        z = where[0] ^ d
        kept[d] = full[2 * z + where[1]]
        sent[d] = full[2 * z + 1 - where[1]]


def turn_kernel(cells, *outs):
    turned = cells[...].astype(F32).T.astype(BF16)
    at = 0
    for out in outs:
        out[...] = turned[at : at + out.shape[0]]
        at += out.shape[0]


def turn_back_kernel(*refs):
    *parts, out, full = refs
    at = 0
    full[...] = jnp.zeros_like(full)
    for i in range(0, len(parts), 4):
        total = parts[i][...].astype(F32)
        for j in range(1, 4):
            total = total + parts[i + j][...].astype(F32)
        full[at : at + total.shape[0], :] = total
        at += total.shape[0]
    out[...] = full[...].T.astype(out.dtype)


def columns_kernel(qkv, mlp, both, gain_a, gain_m, out):
    for g in range(GROUP):
        parts = [
            (qkv[:, p * D + g * OWN : p * D + (g + 1) * OWN].astype(F32) * gain_a[...]).astype(BF16)
            for p in range(3)
        ]
        parts.append(mlp[:, g * OWN_FF : (g + 1) * OWN_FF])
        parts += [
            (both[:, p * FF + g * OWN_FF : p * FF + (g + 1) * OWN_FF].astype(F32) * gain_m[...]).astype(
                BF16
            )
            for p in range(2)
        ]
        parts.append(jnp.zeros((qkv.shape[0], WIDE - 3 * OWN_FF), BF16))
        out[g] = jnp.concatenate(parts, axis=1)


def back_ff_kernel(cells, weight, gain, grad_mlp, grad_in, grad_gain):
    total = jnp.zeros(grad_gain.shape, F32)
    for g in range(GROUP):
        block = cells[g].astype(F32)
        grad_mlp[:, g * OWN_FF : (g + 1) * OWN_FF] = block[:, :OWN_FF]
        for p in range(2):
            raw = block[:, (p + 1) * OWN_FF : (p + 2) * OWN_FF]
            at = slice(p * FF + g * OWN_FF, p * FF + (g + 1) * OWN_FF)
            total = total + jnp.sum(raw * weight[:, at].astype(F32), axis=1, keepdims=True)
            grad_in[:, at] = raw * gain[...]
    grad_gain[...] = total


def back_qkv_kernel(cells, weight, gain, grad, grad_gain):
    total = jnp.zeros(grad_gain.shape, F32)
    for g in range(GROUP):
        block = cells[g].astype(F32)
        for p in range(3):
            raw = block[:, p * OWN : (p + 1) * OWN]
            at = slice(p * D + g * OWN, p * D + (g + 1) * OWN)
            total = total + jnp.sum(raw * weight[:, at].astype(F32), axis=1, keepdims=True)
            grad[:, at] = raw * gain[...]
    grad_gain[...] = total


def columns_of(qkv, mlp, both, gain_a, gain_m):
    rows = qkv.shape[0]
    if direct():
        shape = like((GROUP, rows, 3 * OWN + WIDE), BF16)
        cells = local_kernel(columns_kernel, [shape], (qkv, mlp, both, gain_a, gain_m))[0]
        return cells.reshape(2, 2, rows, -1)

    def columns(w, parts, width):
        cells = w.reshape(rows, parts, 2, 2, width).transpose(2, 3, 0, 1, 4)
        return cells.reshape(2, 2, rows, parts * width)

    return jnp.concatenate(
        [
            columns((qkv.astype(F32) * gain_a).astype(BF16), 3, OWN),
            columns(mlp, 1, OWN_FF),
            columns((both.astype(F32) * gain_m).astype(BF16), 2, OWN_FF),
            jnp.zeros((2, 2, rows, WIDE - 3 * OWN_FF), BF16),
        ],
        axis=-1,
    )


def back_columns(cells, parts, width):
    rows = cells.shape[2]
    cells = cells.reshape(2, 2, rows, parts, width).transpose(2, 3, 0, 1, 4)
    return cells.reshape(rows, parts * GROUP * width).astype(F32)


def back_ff(cells, weight, gain):
    rows = weight.shape[0]
    if direct():
        outs = [like((rows, FF), F32), like((rows, 2 * FF), F32), like((rows, 1), F32)]
        return local_kernel(back_ff_kernel, outs, (cells.reshape(GROUP, rows, WIDE), weight, gain))
    raw = back_columns(cells[..., OWN_FF : 3 * OWN_FF], 2, OWN_FF)
    grad_gain = jnp.sum(raw * weight.astype(F32), axis=1, keepdims=True)
    return back_columns(cells[..., :OWN_FF], 1, OWN_FF), raw * gain, grad_gain


def back_qkv(cells, weight, gain):
    rows = weight.shape[0]
    if direct():
        outs = [like((rows, 3 * D), F32), like((rows, 1), F32)]
        return local_kernel(back_qkv_kernel, outs, (cells.reshape(GROUP, rows, -1), weight, gain))
    raw = back_columns(cells, 3, OWN)
    return raw * gain, jnp.sum(raw * weight.astype(F32), axis=1, keepdims=True)


def x_blocks(cells, got):
    high = (lax.axis_index("seq") & 1) == 1
    blocks = []
    for i in range(cells.shape[0]):
        blocks += [jnp.where(high, got[i], cells[i]), jnp.where(high, cells[i], got[i])]
    return blocks


def x_parts(blocks):
    high = (lax.axis_index("seq") & 1) == 1
    pairs = list(zip(blocks[::2], blocks[1::2]))
    kept = jnp.stack([jnp.where(high, b, a) for a, b in pairs])
    sent = jnp.stack([jnp.where(high, a, b) for a, b in pairs])
    return kept, sent


def assemble(cells, got):
    if direct():
        shape = like((cells.shape[1], D), BF16)
        return local_kernel(lane_assemble_kernel, [shape], (cells, got, place_of_device()))[0]
    return jnp.concatenate(x_blocks(cells, got), axis=-1)


def split(grad):
    count = lax.axis_size("seq")
    size = D // count
    if direct():
        shape = like((4, grad.shape[0], size), BF16)
        return local_kernel(lane_split_kernel, [shape, shape], (grad, place_of_device()))
    return x_parts([grad[:, i * size : (i + 1) * size] for i in range(count)])


def assemble_rows(cells, got):
    if direct():
        shape = like((8,) + cells.shape[1:], BF16)
        return local_kernel(row_assemble_kernel, [shape], (cells, got, place_of_device()))[0]
    return jnp.stack(x_blocks(cells, got))


def split_rows(cells):
    if direct():
        shape = like((4,) + cells.shape[1:], BF16)
        return local_kernel(row_split_kernel, [shape, shape], (cells, place_of_device()))
    return x_parts([cells[i] for i in range(cells.shape[0])])


def turn(cells, sizes):
    if direct():
        return local_kernel(turn_kernel, [like((n, cells.shape[0]), BF16) for n in sizes], (cells,))
    turned, outs, at = cells.T, [], 0
    for n in sizes:
        outs.append(turned[at : at + n])
        at += n
    return outs


def turn_back(chunks, width):
    if direct():
        lanes = chunks[0][0].shape[1]
        return local_kernel(
            turn_back_kernel,
            [like((lanes, width), BF16)],
            tuple(c for chunk in chunks for c in chunk),
            [pltpu.VMEM((width, lanes), F32)],
        )[0]
    turned = jnp.concatenate([total_of(c) for c in chunks], axis=0).T.astype(BF16)
    return jnp.pad(turned, ((0, 0), (0, width - turned.shape[1])))


def place(index, seq_lengths):
    count = seq_lengths.shape[0]
    ids = jnp.arange(count, dtype=jnp.int32)
    ends = jnp.sum(jnp.where(ids[None, :] <= ids[:, None], seq_lengths[None, :], 0), axis=1)
    starts = ends - seq_lengths
    segment = jnp.sum((index[:, None] >= ends[None, :]).astype(jnp.int32), axis=1)
    begins = jnp.sum(jnp.where(segment[:, None] == ids[None, :], starts[None, :], 0), axis=1)
    return segment, index - begins


def angles(position):
    freqs = 10000.0 ** (-(jnp.arange(HDIM // 2, dtype=F32) * 2.0) / HDIM)
    freqs = jnp.concatenate([freqs] * 4)
    turns = position.astype(F32)[:, None] * freqs[None, :]
    sign = jnp.where(jnp.arange(128) % HDIM < HDIM // 2, -1.0, 1.0)
    return jnp.cos(turns), jnp.sin(turns) * sign[None, :]


def normalize(values):
    average = jnp.mean(values, axis=-1, keepdims=True)
    centered = values - average
    variance = jnp.mean(centered * centered, axis=-1, keepdims=True)
    inverse = lax.rsqrt(variance + EPSILON)
    return centered * inverse, inverse


def norm_back(grad_hat, normed, inverse):
    return inverse * (
        grad_hat
        - jnp.mean(grad_hat, axis=-1, keepdims=True)
        - normed * jnp.mean(grad_hat * normed, axis=-1, keepdims=True)
    )


def geglu(gate_in, up_in):
    return jax.nn.gelu(gate_in, approximate=False) * up_in


def contract(left, right, dims, out=F32):
    return lax.dot_general(left, right, ((dims[0], dims[1]), ((), ())), preferred_element_type=out)


def rows_dot(left, right):
    return contract(left, right, ((0,), (0,)))


def cols_dot(left, right):
    return contract(left, right, ((1,), (1,)))


def half_swap(values):
    lane = lax.broadcasted_iota(jnp.int32, values.shape, 1)
    left = pltpu.roll(values, 128 - HDIM // 2, 1)
    right = pltpu.roll(values, HDIM // 2, 1)
    return jnp.where(lane % HDIM < HDIM // 2, left, right)


def bias_of(q_seg, k_seg, block):
    row = lax.broadcasted_iota(jnp.int32, (128, 256), 0)
    col = lax.broadcasted_iota(jnp.int32, (128, 256), 1)
    near = jnp.abs(row + HALF - col) <= HALF
    same = q_seg[pl.ds(block * 128, 128), :] == k_seg[:, pl.ds(block * 128, 256)]
    return jnp.where(near & same, 0.0, MASKED)


def softmax_of(scores):
    exponent = jnp.exp(scores - jnp.max(scores, axis=-1, keepdims=True))
    return exponent * (1.0 / jnp.sum(exponent, axis=-1, keepdims=True))


def attend_kernel(packed, cosine, sine, q_seg, k_seg, query, keys, values, attended, bias):
    rows = query.shape[0]
    blocks = rows // 128
    for b in range(blocks):
        bias[b] = bias_of(q_seg, k_seg, b)
    first = lax.broadcasted_iota(jnp.int32, (1, 128), 1) < HDIM
    for p in range(OWN_HEADS // 2):
        at = slice(p * 128, (p + 1) * 128)
        u = packed[HALF : HALF + rows, at]
        q_cos, q_sin = cosine[HALF : HALF + rows, :], sine[HALF : HALF + rows, :]
        query[:, at] = (u * q_cos + half_swap(u) * q_sin).astype(BF16)
        u = packed[:, OWN + p * 128 : OWN + (p + 1) * 128]
        keys[:, at] = (u * cosine[...] + half_swap(u) * sine[...]).astype(BF16)
        values[:, at] = packed[:, 2 * OWN + p * 128 : 2 * OWN + (p + 1) * 128].astype(BF16)
        for b in range(blocks):
            q = query[b * 128 : (b + 1) * 128, at]
            k = keys[b * 128 : b * 128 + 256, at]
            v = values[b * 128 : b * 128 + 256, at]
            outs = []
            for side in (first, ~first):
                q_one = jnp.where(side, q, jnp.zeros_like(q))
                scores = contract(q_one, k, ((1,), (1,))) * (HDIM**-0.5) + bias[b]
                prob = softmax_of(scores).astype(BF16)
                outs.append(contract(prob, v, ((1,), (0,))))
            attended[b * 128 : (b + 1) * 128, at] = jnp.where(first, outs[0], outs[1]).astype(BF16)


def attend_back_kernel(
    query, keys, values, grad, cosine, sine, q_seg, k_seg, grad_q, grad_k, grad_v, bias
):
    rows = query.shape[0]
    blocks = rows // 128
    scale = HDIM**-0.5
    for b in range(blocks):
        bias[b] = bias_of(q_seg, k_seg, b)
    first = lax.broadcasted_iota(jnp.int32, (1, 128), 1) < HDIM
    grad_k[...] = jnp.zeros_like(grad_k)
    grad_v[...] = jnp.zeros_like(grad_v)
    for p in range(OWN_HEADS // 2):
        at = slice(p * 128, (p + 1) * 128)
        for b in range(blocks):
            here, span = slice(b * 128, (b + 1) * 128), slice(b * 128, b * 128 + 256)
            q, go = query[here, at], grad[here, at]
            k, v = keys[span, at], values[span, at]
            d_q = jnp.zeros((128, 128), F32)
            d_k = jnp.zeros((256, 128), F32)
            d_v = jnp.zeros((256, 128), F32)
            for side in (first, ~first):
                q_one = jnp.where(side, q, jnp.zeros_like(q))
                k_one = jnp.where(side, k, jnp.zeros_like(k))
                go_one = jnp.where(side, go, jnp.zeros_like(go))
                scores = contract(q_one, k, ((1,), (1,))) * scale + bias[b]
                prob = softmax_of(scores)
                grad_prob = contract(go_one, v, ((1,), (1,)))
                inner = jnp.sum(grad_prob * prob, axis=-1, keepdims=True)
                grad_scores = (prob * (grad_prob - inner)).astype(BF16)
                d_q = d_q + contract(grad_scores, k_one, ((1,), (0,)))
                d_k = d_k + contract(grad_scores, q_one, ((0,), (0,)))
                d_v = d_v + contract(prob.astype(BF16), go_one, ((0,), (0,)))
            d_q = d_q * scale
            at_q = slice(HALF + b * 128, HALF + (b + 1) * 128)
            turned = d_q * cosine[at_q, :] - half_swap(d_q) * sine[at_q, :]
            grad_q[here, at] = turned.astype(BF16)
            grad_k[span, at] += d_k * scale
            grad_v[span, at] += d_v
        d_k = grad_k[:, at]
        grad_k[:, at] = d_k * cosine[...] - half_swap(d_k) * sine[...]


def call_kernel(kernel, outs, blocks, flops, args):
    moved = sum(a.size * a.dtype.itemsize for a in args) + sum(
        o.size * o.dtype.itemsize for o in outs
    )
    return pl.pallas_call(
        kernel,
        out_shape=outs,
        in_specs=[pl.BlockSpec(memory_space=pltpu.VMEM)] * len(args),
        out_specs=[pl.BlockSpec(memory_space=pltpu.VMEM)] * len(outs),
        scratch_shapes=[pltpu.VMEM((blocks, 128, 256), F32)],
        compiler_params=pltpu.CompilerParams(vmem_limit_bytes=VMEM_LIMIT),
        cost_estimate=pl.CostEstimate(flops=flops, bytes_accessed=moved, transcendentals=0),
    )(*args)


def like(shape, dtype):
    return jax.ShapeDtypeStruct(shape, dtype)


def on_device(
    tokens, cotangent, seq_lengths, w_qkv, w_attn_out, w_in, w_mlp_out, gain_attn, gain_mlp
):
    share = tokens.shape[0]
    rows = GROUP * share
    seq, seqs = lax.axis_index("seq"), lax.axis_size("seq")
    total = seqs * rows
    shard = w_qkv.shape[0]
    tie = lax.optimization_barrier

    def close(first, last):
        first = tie(first)
        return tie((first, last))


    gain_a = gain_attn.astype(F32)[:, None]
    gain_m = gain_mlp.astype(F32)[:, None]

    last = (lax.axis_index("fy") == 1) & (lax.axis_index("core") == 1)
    meetings = range(GROUP - 1, lax.axis_size(ALL) - 1, GROUP)
    swaps = [(i, i + 1) for i in meetings] + [(i + 1, i) for i in meetings]
    edge = lax.ppermute(jnp.where(last, tokens[share - HALF :], tokens[:HALF]), ALL, swaps)
    attn_z = z_gather(w_attn_out)
    cells = columns_of(w_qkv, w_mlp_out, w_in, gain_a, gain_m)
    cells = trade(trade(cells, "fy", 0), "core", 1).reshape(GROUP * shard, -1)
    qkv, mlp, gate, up = turn(cells, (3 * OWN, OWN_FF, OWN_FF, OWN_FF))
    attn_z, qkv, mlp, gate, up, edge, cotangent_in = tie(
        (attn_z, qkv, mlp, gate, up, edge, cotangent)
    )
    qkv_z = z_gather(qkv)
    attn_x = send_seq(attn_z, 1)
    ours = tokens.astype(F32)
    normed, inverse = normalize(ours)
    hidden = jnp.concatenate([normed, normalize(edge.astype(F32))[0]], axis=0).astype(BF16)
    hidden = join(hidden, "fy", 0)
    cot = join(cotangent_in, "fy", 0)
    (attn_x, hidden, cot, mlp, gate, up), qkv_z = close((attn_x, hidden, cot, mlp, gate, up), qkv_z)
    mlp_z = z_gather(mlp)
    qkv_x = send_seq(qkv_z, 1)
    attn = assemble_rows(attn_z, attn_x).reshape(2, 2, seqs // 4, shard, D)
    hidden = core_rows(hidden).reshape(GROUP, share + HALF, D)
    attn = trade(attn, "core", 1)
    (qkv_x, attn, hidden, gate), mlp_z = close((qkv_x, attn, hidden, gate), mlp_z)
    gate_z = z_gather(gate)
    mlp_x = send_seq(mlp_z, 1)
    attn = trade(attn, "fy", 0)
    before, after = hidden[0, share:], hidden[GROUP - 1, share:]
    hidden = hidden[:, :share].reshape(rows, D)
    wide = jnp.concatenate([before, hidden, after], axis=0)
    qkv_full = assemble(qkv_z, qkv_x)
    index = seq * rows - HALF + jnp.arange(rows + 2 * HALF, dtype=jnp.int32)
    segment, position = place(jnp.clip(index, 0, total - 1), seq_lengths)
    segment = jnp.where((index >= 0) & (index < total), segment, -1)
    q_seg = segment[HALF : HALF + rows][:, None]
    k_seg = segment[None, :]
    cosine, sine = angles(position)
    packed = cols_dot(wide, qkv_full)
    blocks = rows // 128
    flops = blocks * OWN_HEADS * 128 * 256 * 128 * 4
    query, keys, values, attended = call_kernel(
        attend_kernel,
        [
            like((rows, OWN), BF16),
            like((rows + 2 * HALF, OWN), BF16),
            like((rows + 2 * HALF, OWN), BF16),
            like((rows, OWN), BF16),
        ],
        blocks,
        flops,
        (packed, cosine, sine, q_seg, k_seg),
    )
    (mlp_x, attended, attn, up), gate_z = close((mlp_x, attended, attn, up), gate_z)
    up_z = z_gather(up)
    gate_x = send_seq(gate_z, 1)
    attn_full = attn.transpose(2, 0, 1, 3, 4).reshape(OWN, D)
    part = jnp.dot(attended, attn_full, preferred_element_type=F32)
    middle = ours + group_sum(part, share)
    mlp_full = assemble(mlp_z, mlp_x)
    (gate_x, middle, mlp_full), up_z = close((gate_x, middle, mlp_full), up_z)
    up_x = send_seq(up_z, 1)
    normed_mid, inverse_mid = normalize(middle)
    lifted = join(normed_mid.astype(BF16), "fy", 0)
    gate_full = assemble(gate_z, gate_x)
    up_x, lifted, gate_full = tie((up_x, lifted, gate_full))
    lifted, cot = tie((core_rows(lifted), core_rows(cot)))
    up_full = assemble(up_z, up_x)
    shape = like((rows, OWN_FF), BF16)
    mixed, grad_gate, grad_up = local_kernel(
        feed_kernel, [shape] * 3, (lifted, cot, gate_full, up_full, mlp_full)
    )

    mlp_kept, mlp_sent = split(rows_dot(mixed, cot).astype(BF16))
    mlp_kept, mlp_sent, grad_gate, grad_up = tie((mlp_kept, mlp_sent, grad_gate, grad_up))
    mlp_x = send_seq(mlp_sent, 1)
    part_lifted = jnp.dot(grad_gate, gate_full, preferred_element_type=F32) + jnp.dot(
        grad_up, up_full, preferred_element_type=F32
    )
    half_hat = reduce_pair(part_lifted.reshape(2, 2, share, D), "core", 1)
    half_hat, grad_gate, grad_up = tie((half_hat, grad_gate, grad_up))
    grad_hat = reduce_pair(half_hat, "fy", 0)
    gate_kept, gate_sent = split(rows_dot(grad_gate, lifted).astype(BF16))
    up_kept, up_sent = split(rows_dot(grad_up, lifted).astype(BF16))
    mlp_x, gate_sent, up_sent, grad_hat = tie((mlp_x, gate_sent, up_sent, grad_hat))
    mlp_got = z_spread(x_sum(mlp_kept, mlp_x))
    gate_x = send_seq(gate_sent, 1)
    grad_middle = cotangent.astype(F32) + norm_back(grad_hat, normed_mid, inverse_mid)
    grad_attn = join(grad_middle.astype(BF16), "fy", 0)
    (gate_x, grad_attn, attended), mlp_got = close((gate_x, grad_attn, attended), mlp_got)
    gate_got = z_spread(x_sum(gate_kept, gate_x))
    up_x = send_seq(up_sent, 1)
    grad_attn = core_rows(grad_attn)
    grad_attended = cols_dot(grad_attn, attn_full).astype(BF16)
    grad_q, grad_k, grad_v = call_kernel(
        attend_back_kernel,
        [
            like((rows, OWN), BF16),
            like((rows + 2 * HALF, OWN), F32),
            like((rows + 2 * HALF, OWN), F32),
        ],
        blocks,
        flops * 3,
        (query, keys, values, grad_attended, cosine, sine, q_seg, k_seg),
    )
    grad_kv = jnp.concatenate([grad_k, grad_v], axis=1)
    attn_g = rows_dot(attended, grad_attn).astype(BF16)
    attn_g = attn_g.reshape(seqs // 4, 2, 2, shard, D).transpose(1, 2, 0, 3, 4)
    attn_g = trade(attn_g, "core", 1)
    part_out = jnp.dot(mixed, mlp_full, preferred_element_type=F32)
    (up_x, grad_kv, attn_g, part_out), gate_got = close((up_x, grad_kv, attn_g, part_out), gate_got)
    ahead = [(i, i + 1) for i in range(seqs - 1)]
    behind = [(i + 1, i) for i in range(seqs - 1)]
    low_edge = lax.ppermute(grad_kv[:HALF].astype(BF16), "seq", behind)
    high_edge = lax.ppermute(grad_kv[HALF + rows :].astype(BF16), "seq", ahead)
    attn_g = trade(attn_g, "fy", 0).reshape(seqs, shard, D)
    low_edge, high_edge, up_x = tie((low_edge, high_edge, up_x))
    middle_kv = grad_kv[HALF : HALF + rows]
    gap = jnp.zeros((rows - 2 * HALF, 2 * OWN), F32)
    edges = jnp.concatenate([high_edge.astype(F32), gap, low_edge.astype(F32)], axis=0)
    grad_packed = jnp.concatenate([grad_q, (middle_kv + edges).astype(BF16)], axis=1)
    qkv_kept, qkv_sent = split(rows_dot(grad_packed, hidden).astype(BF16))
    attn_g, qkv_sent, grad_packed, up_x = tie((attn_g, qkv_sent, grad_packed, up_x))
    qkv_x = send_seq(qkv_sent, 1)
    up_got = z_spread(x_sum(up_kept, up_x))
    attn_kept, attn_sent = split_rows(attn_g)
    part_hidden = jnp.dot(grad_packed, qkv_full, preferred_element_type=F32)
    parts = jnp.stack([part_hidden, part_out]).reshape(2, 2, 2, share, D)
    (qkv_x, parts, attn_sent), up_got = close((qkv_x, parts, attn_sent), up_got)
    qkv_got = z_spread(x_sum(qkv_kept, qkv_x))
    attn_x = send_seq(attn_sent, 1)

    rest_g = turn_back([mlp_got, gate_got, up_got], WIDE).reshape(2, 2, shard, -1)
    rest_g = trade(trade(rest_g, "fy", 0), "core", 1)
    grad_mlp_out, grad_w_in, grad_gain_mlp = back_ff(rest_g, w_in, gain_m)
    grad_hidden, sum_out = reduce_pair(reduce_pair(parts, "core", 2), "fy", 1)
    output = (middle + sum_out).astype(BF16)
    input_grad = grad_middle + norm_back(grad_hidden, normed, inverse)
    attn_x, qkv_got, output, input_grad, grad_mlp_out, grad_w_in, grad_gain_mlp = tie(
        (attn_x, qkv_got, output, input_grad, grad_mlp_out, grad_w_in, grad_gain_mlp)
    )
    attn_got = z_spread(x_sum(attn_kept, attn_x))
    qkv_g = turn_back([qkv_got], 3 * OWN).reshape(2, 2, shard, -1)
    qkv_g = trade(trade(qkv_g, "fy", 0), "core", 1)
    grad_w_qkv, grad_gain_attn = back_qkv(qkv_g, w_qkv, gain_a)
    grad_attn_out = total_of(attn_got)
    return (
        output,
        input_grad,
        grad_w_qkv,
        grad_attn_out,
        grad_w_in,
        grad_mlp_out,
        grad_gain_attn[:, 0],
        grad_gain_mlp[:, 0],
    )


def solution(mesh):
    split = Mesh(mesh.devices.reshape(mesh.shape["seq"], -1, 2), ALL)
    two, one = P(ALL, None), P(ALL)
    return jax.shard_map(
        on_device,
        mesh=split,
        in_specs=(two, two, P(), two, two, two, two, one, one),
        out_specs=(two, two, two, two, two, two, one, one),
        check_vma=False,
    )
```

```python
import jax
import jax.numpy as jnp
from jax import lax
from jax.experimental import pallas as pl
from jax.experimental.pallas import tpu as pltpu
from jax.sharding import Mesh, PartitionSpec as P

D = 1024
HEADS = 16
HDIM = 64
FF = 2624
HALF = 64
GROUP = 4
OWN_HEADS = HEADS // GROUP
OWN = OWN_HEADS * HDIM
OWN_FF = FF // GROUP
WIDE = 2048
VMEM_LIMIT = 48 * 1024 * 1024

EPSILON = 1e-05
MASKED = -1e30
ALL = ("seq", "fy", "core")
BF16 = jnp.bfloat16
F32 = jnp.float32


def flat_pairs(change):
    count = lax.axis_size(ALL)
    return [(i, change(i)) for i in range(count)]


def send_seq(cells, flip):
    return lax.ppermute(cells, ALL, flat_pairs(lambda i: i ^ (flip * GROUP)))


def trade(cells, axis, dim):
    me = lax.axis_index(axis)
    kept = lax.dynamic_slice_in_dim(cells, me, 1, axis=dim)
    sent = lax.dynamic_slice_in_dim(cells, 1 - me, 1, axis=dim)
    got = lax.ppermute(sent, axis, [(0, 1), (1, 0)])
    low = me == 0
    return jnp.concatenate([jnp.where(low, kept, got), jnp.where(low, got, kept)], axis=dim)


def join(cells, axis, dim):
    me = lax.axis_index(axis)
    got = lax.ppermute(cells, axis, [(0, 1), (1, 0)])
    low = me == 0
    return jnp.stack([jnp.where(low, cells, got), jnp.where(low, got, cells)], axis=dim)


def reduce_pair(cells, axis, dim):
    me = lax.axis_index(axis)
    kept = lax.dynamic_index_in_dim(cells, me, dim, keepdims=False)
    sent = lax.dynamic_index_in_dim(cells, 1 - me, dim, keepdims=False).astype(BF16)
    got = lax.ppermute(sent, axis, [(0, 1), (1, 0)])
    return kept.astype(F32) + got.astype(F32)


def core_rows(cells):
    return join(cells, "core", 1).reshape((-1,) + cells.shape[2:])


def group_rows(cells):
    return core_rows(join(cells, "fy", 0))


def group_sum(part, rows):
    cells = part.reshape(2, 2, rows, part.shape[-1])
    return reduce_pair(reduce_pair(cells, "core", 1), "fy", 0)


def depth_of():
    return lax.axis_size("seq") // 2


def direct():
    return lax.axis_size("seq") == 8


def place_of_device():
    seq = lax.axis_index("seq")
    return jnp.stack([seq >> 1, seq & 1]).astype(jnp.int32)


def z_gather(cells):
    if direct():
        return jnp.stack([cells] + [send_seq(cells, 2 * d) for d in range(1, 4)])
    cells, me = cells[None], lax.axis_index("seq") >> 1
    flip = 1
    while flip < depth_of():
        other = send_seq(cells, 2 * flip)
        high = (me & flip) != 0
        cells = jnp.concatenate([jnp.where(high, other, cells), jnp.where(high, cells, other)])
        flip *= 2
    return cells


def x_sum(kept, got):
    return (kept.astype(F32) + got.astype(F32)).astype(BF16)


def z_spread(cells):
    if direct():
        return [cells[0]] + [send_seq(cells[d], 2 * d) for d in range(1, 4)]
    flip, me = depth_of() // 2, lax.axis_index("seq") >> 1
    while flip:
        high = ((me & flip) != 0).astype(jnp.int32)
        kept = lax.dynamic_slice_in_dim(cells, high * flip, flip, 0)
        sent = lax.dynamic_slice_in_dim(cells, (1 - high) * flip, flip, 0)
        cells = kept.astype(F32) + send_seq(sent.astype(BF16), 2 * flip).astype(F32)
        flip //= 2
    return [cells[0]]


def total_of(got):
    return sum(cells.astype(F32) for cells in got)


def feed_kernel(lifted, cot, gate_w, up_w, mlp_w, mixed, grad_gate, grad_up):
    for r in range(0, lifted.shape[0], 128):
        at = slice(r, r + 128)
        gate = cols_dot(lifted[at, :], gate_w[...])
        up = cols_dot(lifted[at, :], up_w[...])
        grad = cols_dot(cot[at, :], mlp_w[...])
        share = 0.5 + 0.5 * lax.erf(gate * (0.5**0.5))
        slope = share + gate * jnp.exp(-0.5 * gate * gate) * ((0.5 / jnp.pi) ** 0.5)
        gelu = gate * share
        mixed[at, :] = (gelu * up).astype(BF16)
        grad_gate[at, :] = (grad * up * slope).astype(BF16)
        grad_up[at, :] = (grad * gelu).astype(BF16)


def local_kernel(kernel, outs, args, scratch=()):
    spaces = [
        pltpu.SMEM if a.dtype == jnp.int32 and a.size == 2 else pltpu.VMEM for a in args
    ]
    moved = sum(a.size * a.dtype.itemsize for a in args)
    return pl.pallas_call(
        kernel,
        out_shape=outs,
        in_specs=[pl.BlockSpec(memory_space=s) for s in spaces],
        out_specs=[pl.BlockSpec(memory_space=pltpu.VMEM)] * len(outs),
        scratch_shapes=list(scratch),
        compiler_params=pltpu.CompilerParams(vmem_limit_bytes=VMEM_LIMIT),
        cost_estimate=pl.CostEstimate(flops=0, bytes_accessed=moved, transcendentals=0),
    )(*args)


def lane_assemble_kernel(cells, got, where, full):
    for d in range(4):
        z = where[0] ^ d
        mine = pl.multiple_of((2 * z + where[1]) * 128, 128)
        theirs = pl.multiple_of((2 * z + 1 - where[1]) * 128, 128)
        full[:, pl.ds(mine, 128)] = cells[d]
        full[:, pl.ds(theirs, 128)] = got[d]


def lane_split_kernel(full, where, kept, sent):
    for d in range(4):
        z = where[0] ^ d
        mine = pl.multiple_of((2 * z + where[1]) * 128, 128)
        theirs = pl.multiple_of((2 * z + 1 - where[1]) * 128, 128)
        kept[d] = full[:, pl.ds(mine, 128)]
        sent[d] = full[:, pl.ds(theirs, 128)]


def row_assemble_kernel(cells, got, where, full):
    for d in range(4):
        z = where[0] ^ d
        full[2 * z + where[1]] = cells[d]
        full[2 * z + 1 - where[1]] = got[d]


def row_split_kernel(full, where, kept, sent):
    for d in range(4):
        z = where[0] ^ d
        kept[d] = full[2 * z + where[1]]
        sent[d] = full[2 * z + 1 - where[1]]


def turn_kernel(cells, *outs):
    turned = cells[...].astype(F32).T.astype(BF16)
    at = 0
    for out in outs:
        out[...] = turned[at : at + out.shape[0]]
        at += out.shape[0]


def turn_back_kernel(*refs):
    *parts, out, full = refs
    at = 0
    full[...] = jnp.zeros_like(full)
    for i in range(0, len(parts), 4):
        total = parts[i][...].astype(F32)
        for j in range(1, 4):
            total = total + parts[i + j][...].astype(F32)
        full[at : at + total.shape[0], :] = total
        at += total.shape[0]
    out[...] = full[...].T.astype(out.dtype)


def columns_kernel(qkv, mlp, both, gain_a, gain_m, out):
    for g in range(GROUP):
        parts = [
            (qkv[:, p * D + g * OWN : p * D + (g + 1) * OWN].astype(F32) * gain_a[...]).astype(BF16)
            for p in range(3)
        ]
        parts.append(mlp[:, g * OWN_FF : (g + 1) * OWN_FF])
        parts += [
            (both[:, p * FF + g * OWN_FF : p * FF + (g + 1) * OWN_FF].astype(F32) * gain_m[...]).astype(
                BF16
            )
            for p in range(2)
        ]
        parts.append(jnp.zeros((qkv.shape[0], WIDE - 3 * OWN_FF), BF16))
        out[g] = jnp.concatenate(parts, axis=1)


def back_ff_kernel(cells, weight, gain, grad_mlp, grad_in, grad_gain):
    total = jnp.zeros(grad_gain.shape, F32)
    for g in range(GROUP):
        block = cells[g].astype(F32)
        grad_mlp[:, g * OWN_FF : (g + 1) * OWN_FF] = block[:, :OWN_FF]
        for p in range(2):
            raw = block[:, (p + 1) * OWN_FF : (p + 2) * OWN_FF]
            at = slice(p * FF + g * OWN_FF, p * FF + (g + 1) * OWN_FF)
            total = total + jnp.sum(raw * weight[:, at].astype(F32), axis=1, keepdims=True)
            grad_in[:, at] = raw * gain[...]
    grad_gain[...] = total


def back_qkv_kernel(cells, weight, gain, grad, grad_gain):
    total = jnp.zeros(grad_gain.shape, F32)
    for g in range(GROUP):
        block = cells[g].astype(F32)
        for p in range(3):
            raw = block[:, p * OWN : (p + 1) * OWN]
            at = slice(p * D + g * OWN, p * D + (g + 1) * OWN)
            total = total + jnp.sum(raw * weight[:, at].astype(F32), axis=1, keepdims=True)
            grad[:, at] = raw * gain[...]
    grad_gain[...] = total


def columns_of(qkv, mlp, both, gain_a, gain_m):
    rows = qkv.shape[0]
    if direct():
        shape = like((GROUP, rows, 3 * OWN + WIDE), BF16)
        cells = local_kernel(columns_kernel, [shape], (qkv, mlp, both, gain_a, gain_m))[0]
        return cells.reshape(2, 2, rows, -1)

    def columns(w, parts, width):
        cells = w.reshape(rows, parts, 2, 2, width).transpose(2, 3, 0, 1, 4)
        return cells.reshape(2, 2, rows, parts * width)

    return jnp.concatenate(
        [
            columns((qkv.astype(F32) * gain_a).astype(BF16), 3, OWN),
            columns(mlp, 1, OWN_FF),
            columns((both.astype(F32) * gain_m).astype(BF16), 2, OWN_FF),
            jnp.zeros((2, 2, rows, WIDE - 3 * OWN_FF), BF16),
        ],
        axis=-1,
    )


def back_columns(cells, parts, width):
    rows = cells.shape[2]
    cells = cells.reshape(2, 2, rows, parts, width).transpose(2, 3, 0, 1, 4)
    return cells.reshape(rows, parts * GROUP * width).astype(F32)


def back_ff(cells, weight, gain):
    rows = weight.shape[0]
    if direct():
        outs = [like((rows, FF), F32), like((rows, 2 * FF), F32), like((rows, 1), F32)]
        return local_kernel(back_ff_kernel, outs, (cells.reshape(GROUP, rows, WIDE), weight, gain))
    raw = back_columns(cells[..., OWN_FF : 3 * OWN_FF], 2, OWN_FF)
    grad_gain = jnp.sum(raw * weight.astype(F32), axis=1, keepdims=True)
    return back_columns(cells[..., :OWN_FF], 1, OWN_FF), raw * gain, grad_gain


def back_qkv(cells, weight, gain):
    rows = weight.shape[0]
    if direct():
        outs = [like((rows, 3 * D), F32), like((rows, 1), F32)]
        return local_kernel(back_qkv_kernel, outs, (cells.reshape(GROUP, rows, -1), weight, gain))
    raw = back_columns(cells, 3, OWN)
    return raw * gain, jnp.sum(raw * weight.astype(F32), axis=1, keepdims=True)


def x_blocks(cells, got):
    high = (lax.axis_index("seq") & 1) == 1
    blocks = []
    for i in range(cells.shape[0]):
        blocks += [jnp.where(high, got[i], cells[i]), jnp.where(high, cells[i], got[i])]
    return blocks


def x_parts(blocks):
    high = (lax.axis_index("seq") & 1) == 1
    pairs = list(zip(blocks[::2], blocks[1::2]))
    kept = jnp.stack([jnp.where(high, b, a) for a, b in pairs])
    sent = jnp.stack([jnp.where(high, a, b) for a, b in pairs])
    return kept, sent


def assemble(cells, got):
    if direct():
        shape = like((cells.shape[1], D), BF16)
        return local_kernel(lane_assemble_kernel, [shape], (cells, got, place_of_device()))[0]
    return jnp.concatenate(x_blocks(cells, got), axis=-1)


def split(grad):
    count = lax.axis_size("seq")
    size = D // count
    if direct():
        shape = like((4, grad.shape[0], size), BF16)
        return local_kernel(lane_split_kernel, [shape, shape], (grad, place_of_device()))
    return x_parts([grad[:, i * size : (i + 1) * size] for i in range(count)])


def assemble_rows(cells, got):
    if direct():
        shape = like((8,) + cells.shape[1:], BF16)
        return local_kernel(row_assemble_kernel, [shape], (cells, got, place_of_device()))[0]
    return jnp.stack(x_blocks(cells, got))


def split_rows(cells):
    if direct():
        shape = like((4,) + cells.shape[1:], BF16)
        return local_kernel(row_split_kernel, [shape, shape], (cells, place_of_device()))
    return x_parts([cells[i] for i in range(cells.shape[0])])


def turn(cells, sizes):
    if direct():
        return local_kernel(turn_kernel, [like((n, cells.shape[0]), BF16) for n in sizes], (cells,))
    turned, outs, at = cells.T, [], 0
    for n in sizes:
        outs.append(turned[at : at + n])
        at += n
    return outs


def turn_back(chunks, width):
    if direct():
        lanes = chunks[0][0].shape[1]
        return local_kernel(
            turn_back_kernel,
            [like((lanes, width), BF16)],
            tuple(c for chunk in chunks for c in chunk),
            [pltpu.VMEM((width, lanes), F32)],
        )[0]
    turned = jnp.concatenate([total_of(c) for c in chunks], axis=0).T.astype(BF16)
    return jnp.pad(turned, ((0, 0), (0, width - turned.shape[1])))


def place(index, seq_lengths):
    count = seq_lengths.shape[0]
    ids = jnp.arange(count, dtype=jnp.int32)
    ends = jnp.sum(jnp.where(ids[None, :] <= ids[:, None], seq_lengths[None, :], 0), axis=1)
    starts = ends - seq_lengths
    segment = jnp.sum((index[:, None] >= ends[None, :]).astype(jnp.int32), axis=1)
    begins = jnp.sum(jnp.where(segment[:, None] == ids[None, :], starts[None, :], 0), axis=1)
    return segment, index - begins


def angles(position):
    freqs = 10000.0 ** (-(jnp.arange(HDIM // 2, dtype=F32) * 2.0) / HDIM)
    freqs = jnp.concatenate([freqs] * 4)
    turns = position.astype(F32)[:, None] * freqs[None, :]
    sign = jnp.where(jnp.arange(128) % HDIM < HDIM // 2, -1.0, 1.0)
    return jnp.cos(turns), jnp.sin(turns) * sign[None, :]


def normalize(values):
    average = jnp.mean(values, axis=-1, keepdims=True)
    centered = values - average
    variance = jnp.mean(centered * centered, axis=-1, keepdims=True)
    inverse = lax.rsqrt(variance + EPSILON)
    return centered * inverse, inverse


def norm_back(grad_hat, normed, inverse):
    return inverse * (
        grad_hat
        - jnp.mean(grad_hat, axis=-1, keepdims=True)
        - normed * jnp.mean(grad_hat * normed, axis=-1, keepdims=True)
    )


def geglu(gate_in, up_in):
    return jax.nn.gelu(gate_in, approximate=False) * up_in


def contract(left, right, dims, out=F32):
    return lax.dot_general(left, right, ((dims[0], dims[1]), ((), ())), preferred_element_type=out)


def rows_dot(left, right):
    return contract(left, right, ((0,), (0,)))


def cols_dot(left, right):
    return contract(left, right, ((1,), (1,)))


def half_swap(values):
    lane = lax.broadcasted_iota(jnp.int32, values.shape, 1)
    left = pltpu.roll(values, 128 - HDIM // 2, 1)
    right = pltpu.roll(values, HDIM // 2, 1)
    return jnp.where(lane % HDIM < HDIM // 2, left, right)


def bias_of(q_seg, k_seg, block):
    row = lax.broadcasted_iota(jnp.int32, (128, 256), 0)
    col = lax.broadcasted_iota(jnp.int32, (128, 256), 1)
    near = jnp.abs(row + HALF - col) <= HALF
    same = q_seg[pl.ds(block * 128, 128), :] == k_seg[:, pl.ds(block * 128, 256)]
    return jnp.where(near & same, 0.0, MASKED)


def softmax_of(scores):
    exponent = jnp.exp(scores - jnp.max(scores, axis=-1, keepdims=True))
    return exponent * (1.0 / jnp.sum(exponent, axis=-1, keepdims=True))


def attend_kernel(packed, cosine, sine, q_seg, k_seg, query, keys, values, attended, bias):
    rows = query.shape[0]
    blocks = rows // 128
    for b in range(blocks):
        bias[b] = bias_of(q_seg, k_seg, b)
    first = lax.broadcasted_iota(jnp.int32, (1, 128), 1) < HDIM
    for p in range(OWN_HEADS // 2):
        at = slice(p * 128, (p + 1) * 128)
        u = packed[HALF : HALF + rows, at]
        q_cos, q_sin = cosine[HALF : HALF + rows, :], sine[HALF : HALF + rows, :]
        query[:, at] = (u * q_cos + half_swap(u) * q_sin).astype(BF16)
        u = packed[:, OWN + p * 128 : OWN + (p + 1) * 128]
        keys[:, at] = (u * cosine[...] + half_swap(u) * sine[...]).astype(BF16)
        values[:, at] = packed[:, 2 * OWN + p * 128 : 2 * OWN + (p + 1) * 128].astype(BF16)
        for b in range(blocks):
            q = query[b * 128 : (b + 1) * 128, at]
            k = keys[b * 128 : b * 128 + 256, at]
            v = values[b * 128 : b * 128 + 256, at]
            outs = []
            for side in (first, ~first):
                q_one = jnp.where(side, q, jnp.zeros_like(q))
                scores = contract(q_one, k, ((1,), (1,))) * (HDIM**-0.5) + bias[b]
                prob = softmax_of(scores).astype(BF16)
                outs.append(contract(prob, v, ((1,), (0,))))
            attended[b * 128 : (b + 1) * 128, at] = jnp.where(first, outs[0], outs[1]).astype(BF16)


def attend_back_kernel(
    query, keys, values, grad, cosine, sine, q_seg, k_seg, grad_q, grad_k, grad_v, bias
):
    rows = query.shape[0]
    blocks = rows // 128
    scale = HDIM**-0.5
    for b in range(blocks):
        bias[b] = bias_of(q_seg, k_seg, b)
    first = lax.broadcasted_iota(jnp.int32, (1, 128), 1) < HDIM
    grad_k[...] = jnp.zeros_like(grad_k)
    grad_v[...] = jnp.zeros_like(grad_v)
    for p in range(OWN_HEADS // 2):
        at = slice(p * 128, (p + 1) * 128)
        for b in range(blocks):
            here, span = slice(b * 128, (b + 1) * 128), slice(b * 128, b * 128 + 256)
            q, go = query[here, at], grad[here, at]
            k, v = keys[span, at], values[span, at]
            d_q = jnp.zeros((128, 128), F32)
            d_k = jnp.zeros((256, 128), F32)
            d_v = jnp.zeros((256, 128), F32)
            for side in (first, ~first):
                q_one = jnp.where(side, q, jnp.zeros_like(q))
                k_one = jnp.where(side, k, jnp.zeros_like(k))
                go_one = jnp.where(side, go, jnp.zeros_like(go))
                scores = contract(q_one, k, ((1,), (1,))) * scale + bias[b]
                prob = softmax_of(scores)
                grad_prob = contract(go_one, v, ((1,), (1,)))
                inner = jnp.sum(grad_prob * prob, axis=-1, keepdims=True)
                grad_scores = (prob * (grad_prob - inner)).astype(BF16)
                d_q = d_q + contract(grad_scores, k_one, ((1,), (0,)))
                d_k = d_k + contract(grad_scores, q_one, ((0,), (0,)))
                d_v = d_v + contract(prob.astype(BF16), go_one, ((0,), (0,)))
            d_q = d_q * scale
            at_q = slice(HALF + b * 128, HALF + (b + 1) * 128)
            turned = d_q * cosine[at_q, :] - half_swap(d_q) * sine[at_q, :]
            grad_q[here, at] = turned.astype(BF16)
            grad_k[span, at] += d_k * scale
            grad_v[span, at] += d_v
        d_k = grad_k[:, at]
        grad_k[:, at] = d_k * cosine[...] - half_swap(d_k) * sine[...]


def call_kernel(kernel, outs, blocks, flops, args):
    moved = sum(a.size * a.dtype.itemsize for a in args) + sum(
        o.size * o.dtype.itemsize for o in outs
    )
    return pl.pallas_call(
        kernel,
        out_shape=outs,
        in_specs=[pl.BlockSpec(memory_space=pltpu.VMEM)] * len(args),
        out_specs=[pl.BlockSpec(memory_space=pltpu.VMEM)] * len(outs),
        scratch_shapes=[pltpu.VMEM((blocks, 128, 256), F32)],
        compiler_params=pltpu.CompilerParams(vmem_limit_bytes=VMEM_LIMIT),
        cost_estimate=pl.CostEstimate(flops=flops, bytes_accessed=moved, transcendentals=0),
    )(*args)


def like(shape, dtype):
    return jax.ShapeDtypeStruct(shape, dtype)


def on_device(
    tokens, cotangent, seq_lengths, w_qkv, w_attn_out, w_in, w_mlp_out, gain_attn, gain_mlp
):
    share = tokens.shape[0]
    rows = GROUP * share
    seq, seqs = lax.axis_index("seq"), lax.axis_size("seq")
    total = seqs * rows
    shard = w_qkv.shape[0]
    tie = lax.optimization_barrier

    def close(first, last):
        first = tie(first)
        return tie((first, last))


    gain_a = gain_attn.astype(F32)[:, None]
    gain_m = gain_mlp.astype(F32)[:, None]

    last = (lax.axis_index("fy") == 1) & (lax.axis_index("core") == 1)
    meetings = range(GROUP - 1, lax.axis_size(ALL) - 1, GROUP)
    swaps = [(i, i + 1) for i in meetings] + [(i + 1, i) for i in meetings]
    edge = lax.ppermute(jnp.where(last, tokens[share - HALF :], tokens[:HALF]), ALL, swaps)
    attn_z = z_gather(w_attn_out)
    cells = columns_of(w_qkv, w_mlp_out, w_in, gain_a, gain_m)
    cells = trade(trade(cells, "fy", 0), "core", 1).reshape(GROUP * shard, -1)
    qkv, mlp, gate, up = turn(cells, (3 * OWN, OWN_FF, OWN_FF, OWN_FF))
    attn_z, qkv, mlp, gate, up, edge, cotangent_in = tie(
        (attn_z, qkv, mlp, gate, up, edge, cotangent)
    )
    qkv_z = z_gather(qkv)
    attn_x = send_seq(attn_z, 1)
    ours = tokens.astype(F32)
    normed, inverse = normalize(ours)
    hidden = jnp.concatenate([normed, normalize(edge.astype(F32))[0]], axis=0).astype(BF16)
    hidden = join(hidden, "fy", 0)
    cot = join(cotangent_in, "fy", 0)
    (attn_x, hidden, cot, mlp, gate, up), qkv_z = close((attn_x, hidden, cot, mlp, gate, up), qkv_z)
    mlp_z = z_gather(mlp)
    qkv_x = send_seq(qkv_z, 1)
    attn = assemble_rows(attn_z, attn_x).reshape(2, 2, seqs // 4, shard, D)
    hidden = core_rows(hidden).reshape(GROUP, share + HALF, D)
    attn = trade(attn, "core", 1)
    (qkv_x, attn, hidden, gate), mlp_z = close((qkv_x, attn, hidden, gate), mlp_z)
    gate_z = z_gather(gate)
    mlp_x = send_seq(mlp_z, 1)
    attn = trade(attn, "fy", 0)
    before, after = hidden[0, share:], hidden[GROUP - 1, share:]
    hidden = hidden[:, :share].reshape(rows, D)
    wide = jnp.concatenate([before, hidden, after], axis=0)
    qkv_full = assemble(qkv_z, qkv_x)
    index = seq * rows - HALF + jnp.arange(rows + 2 * HALF, dtype=jnp.int32)
    segment, position = place(jnp.clip(index, 0, total - 1), seq_lengths)
    segment = jnp.where((index >= 0) & (index < total), segment, -1)
    q_seg = segment[HALF : HALF + rows][:, None]
    k_seg = segment[None, :]
    cosine, sine = angles(position)
    packed = cols_dot(wide, qkv_full)
    blocks = rows // 128
    flops = blocks * OWN_HEADS * 128 * 256 * 128 * 4
    query, keys, values, attended = call_kernel(
        attend_kernel,
        [
            like((rows, OWN), BF16),
            like((rows + 2 * HALF, OWN), BF16),
            like((rows + 2 * HALF, OWN), BF16),
            like((rows, OWN), BF16),
        ],
        blocks,
        flops,
        (packed, cosine, sine, q_seg, k_seg),
    )
    (mlp_x, attended, attn, up), gate_z = close((mlp_x, attended, attn, up), gate_z)
    up_z = z_gather(up)
    gate_x = send_seq(gate_z, 1)
    attn_full = attn.transpose(2, 0, 1, 3, 4).reshape(OWN, D)
    part = jnp.dot(attended, attn_full, preferred_element_type=F32)
    middle = ours + group_sum(part, share)
    mlp_full = assemble(mlp_z, mlp_x)
    (gate_x, middle, mlp_full), up_z = close((gate_x, middle, mlp_full), up_z)
    up_x = send_seq(up_z, 1)
    normed_mid, inverse_mid = normalize(middle)
    lifted = join(normed_mid.astype(BF16), "fy", 0)
    gate_full = assemble(gate_z, gate_x)
    up_x, lifted, gate_full = tie((up_x, lifted, gate_full))
    lifted, cot = tie((core_rows(lifted), core_rows(cot)))
    up_full = assemble(up_z, up_x)
    shape = like((rows, OWN_FF), BF16)
    mixed, grad_gate, grad_up = local_kernel(
        feed_kernel, [shape] * 3, (lifted, cot, gate_full, up_full, mlp_full)
    )

    mlp_kept, mlp_sent = split(rows_dot(mixed, cot).astype(BF16))
    mlp_kept, mlp_sent, grad_gate, grad_up = tie((mlp_kept, mlp_sent, grad_gate, grad_up))
    mlp_x = send_seq(mlp_sent, 1)
    part_lifted = jnp.dot(grad_gate, gate_full, preferred_element_type=F32) + jnp.dot(
        grad_up, up_full, preferred_element_type=F32
    )
    half_hat = reduce_pair(part_lifted.reshape(2, 2, share, D), "core", 1)
    half_hat, grad_gate, grad_up = tie((half_hat, grad_gate, grad_up))
    grad_hat = reduce_pair(half_hat, "fy", 0)
    gate_kept, gate_sent = split(rows_dot(grad_gate, lifted).astype(BF16))
    up_kept, up_sent = split(rows_dot(grad_up, lifted).astype(BF16))
    mlp_x, gate_sent, up_sent, grad_hat = tie((mlp_x, gate_sent, up_sent, grad_hat))
    mlp_got = z_spread(x_sum(mlp_kept, mlp_x))
    gate_x = send_seq(gate_sent, 1)
    grad_middle = cotangent.astype(F32) + norm_back(grad_hat, normed_mid, inverse_mid)
    grad_attn = join(grad_middle.astype(BF16), "fy", 0)
    (gate_x, grad_attn, attended), mlp_got = close((gate_x, grad_attn, attended), mlp_got)
    gate_got = z_spread(x_sum(gate_kept, gate_x))
    up_x = send_seq(up_sent, 1)
    grad_attn = core_rows(grad_attn)
    grad_attended = cols_dot(grad_attn, attn_full).astype(BF16)
    grad_q, grad_k, grad_v = call_kernel(
        attend_back_kernel,
        [
            like((rows, OWN), BF16),
            like((rows + 2 * HALF, OWN), F32),
            like((rows + 2 * HALF, OWN), F32),
        ],
        blocks,
        flops * 3,
        (query, keys, values, grad_attended, cosine, sine, q_seg, k_seg),
    )
    grad_kv = jnp.concatenate([grad_k, grad_v], axis=1)
    attn_g = rows_dot(attended, grad_attn).astype(BF16)
    attn_g = attn_g.reshape(seqs // 4, 2, 2, shard, D).transpose(1, 2, 0, 3, 4)
    attn_g = trade(attn_g, "core", 1)
    part_out = jnp.dot(mixed, mlp_full, preferred_element_type=F32)
    (up_x, grad_kv, attn_g, part_out), gate_got = close((up_x, grad_kv, attn_g, part_out), gate_got)
    ahead = [(i, i + 1) for i in range(seqs - 1)]
    behind = [(i + 1, i) for i in range(seqs - 1)]
    low_edge = lax.ppermute(grad_kv[:HALF].astype(BF16), "seq", behind)
    high_edge = lax.ppermute(grad_kv[HALF + rows :].astype(BF16), "seq", ahead)
    attn_g = trade(attn_g, "fy", 0).reshape(seqs, shard, D)
    low_edge, high_edge, up_x = tie((low_edge, high_edge, up_x))
    middle_kv = grad_kv[HALF : HALF + rows]
    gap = jnp.zeros((rows - 2 * HALF, 2 * OWN), F32)
    edges = jnp.concatenate([high_edge.astype(F32), gap, low_edge.astype(F32)], axis=0)
    grad_packed = jnp.concatenate([grad_q, (middle_kv + edges).astype(BF16)], axis=1)
    qkv_kept, qkv_sent = split(rows_dot(grad_packed, hidden).astype(BF16))
    half_out = reduce_pair(part_out.reshape(2, 2, share, D), "core", 1)
    attn_g, qkv_sent, grad_packed, up_x, half_out = tie(
        (attn_g, qkv_sent, grad_packed, up_x, half_out)
    )
    qkv_x = send_seq(qkv_sent, 1)
    up_got = z_spread(x_sum(up_kept, up_x))
    attn_kept, attn_sent = split_rows(attn_g)
    part_hidden = jnp.dot(grad_packed, qkv_full, preferred_element_type=F32)
    sum_out = reduce_pair(half_out, "fy", 0)
    (qkv_x, part_hidden, sum_out, attn_sent), up_got = close(
        (qkv_x, part_hidden, sum_out, attn_sent), up_got
    )
    qkv_got = z_spread(x_sum(qkv_kept, qkv_x))
    attn_x = send_seq(attn_sent, 1)

    rest_g = turn_back([mlp_got, gate_got, up_got], WIDE).reshape(2, 2, shard, -1)
    rest_g = trade(trade(rest_g, "fy", 0), "core", 1)
    grad_mlp_out, grad_w_in, grad_gain_mlp = back_ff(rest_g, w_in, gain_m)
    grad_hidden = group_sum(part_hidden, share)
    output = (middle + sum_out).astype(BF16)
    input_grad = grad_middle + norm_back(grad_hidden, normed, inverse)
    attn_x, qkv_got, output, input_grad, grad_mlp_out, grad_w_in, grad_gain_mlp = tie(
        (attn_x, qkv_got, output, input_grad, grad_mlp_out, grad_w_in, grad_gain_mlp)
    )
    attn_got = z_spread(x_sum(attn_kept, attn_x))
    qkv_g = turn_back([qkv_got], 3 * OWN).reshape(2, 2, shard, -1)
    qkv_g = trade(trade(qkv_g, "fy", 0), "core", 1)
    grad_w_qkv, grad_gain_attn = back_qkv(qkv_g, w_qkv, gain_a)
    grad_attn_out = total_of(attn_got)
    return (
        output,
        input_grad,
        grad_w_qkv,
        grad_attn_out,
        grad_w_in,
        grad_mlp_out,
        grad_gain_attn[:, 0],
        grad_gain_mlp[:, 0],
    )


def solution(mesh):
    split = Mesh(mesh.devices.reshape(mesh.shape["seq"], -1, 2), ALL)
    two, one = P(ALL, None), P(ALL)
    return jax.shard_map(
        on_device,
        mesh=split,
        in_specs=(two, two, P(), two, two, two, two, one, one),
        out_specs=(two, two, two, two, two, two, one, one),
        check_vma=False,
    )
```

```python
import jax
import jax.numpy as jnp
from jax import lax
from jax.experimental import pallas as pl
from jax.experimental.pallas import tpu as pltpu
from jax.sharding import Mesh, PartitionSpec as P

D = 1024
HEADS = 16
HDIM = 64
FF = 2624
HALF = 64
GROUP = 4
OWN_HEADS = HEADS // GROUP
OWN = OWN_HEADS * HDIM
OWN_FF = FF // GROUP
WIDE = 2048
VMEM_LIMIT = 48 * 1024 * 1024

EPSILON = 1e-05
MASKED = -1e30
ALL = ("seq", "fy", "core")
BF16 = jnp.bfloat16
F32 = jnp.float32


def flat_pairs(change):
    count = lax.axis_size(ALL)
    return [(i, change(i)) for i in range(count)]


def send_seq(cells, flip):
    return lax.ppermute(cells, ALL, flat_pairs(lambda i: i ^ (flip * GROUP)))


def trade(cells, axis, dim):
    me = lax.axis_index(axis)
    kept = lax.dynamic_slice_in_dim(cells, me, 1, axis=dim)
    sent = lax.dynamic_slice_in_dim(cells, 1 - me, 1, axis=dim)
    got = lax.ppermute(sent, axis, [(0, 1), (1, 0)])
    low = me == 0
    return jnp.concatenate([jnp.where(low, kept, got), jnp.where(low, got, kept)], axis=dim)


def join(cells, axis, dim):
    me = lax.axis_index(axis)
    got = lax.ppermute(cells, axis, [(0, 1), (1, 0)])
    low = me == 0
    return jnp.stack([jnp.where(low, cells, got), jnp.where(low, got, cells)], axis=dim)


def reduce_pair(cells, axis, dim):
    me = lax.axis_index(axis)
    kept = lax.dynamic_index_in_dim(cells, me, dim, keepdims=False)
    sent = lax.dynamic_index_in_dim(cells, 1 - me, dim, keepdims=False).astype(BF16)
    got = lax.ppermute(sent, axis, [(0, 1), (1, 0)])
    return kept.astype(F32) + got.astype(F32)


def core_rows(cells):
    return join(cells, "core", 1).reshape((-1,) + cells.shape[2:])


def group_rows(cells):
    return core_rows(join(cells, "fy", 0))


def group_sum(part, rows):
    cells = part.reshape(2, 2, rows, part.shape[-1])
    return reduce_pair(reduce_pair(cells, "core", 1), "fy", 0)


def depth_of():
    return lax.axis_size("seq") // 2


def direct():
    return lax.axis_size("seq") == 8


def place_of_device():
    seq = lax.axis_index("seq")
    return jnp.stack([seq >> 1, seq & 1]).astype(jnp.int32)


def z_gather(cells):
    if direct():
        return jnp.stack([cells] + [send_seq(cells, 2 * d) for d in range(1, 4)])
    cells, me = cells[None], lax.axis_index("seq") >> 1
    flip = 1
    while flip < depth_of():
        other = send_seq(cells, 2 * flip)
        high = (me & flip) != 0
        cells = jnp.concatenate([jnp.where(high, other, cells), jnp.where(high, cells, other)])
        flip *= 2
    return cells


def x_sum(kept, got):
    return (kept.astype(F32) + got.astype(F32)).astype(BF16)


def z_spread(cells):
    if direct():
        return [cells[0]] + [send_seq(cells[d], 2 * d) for d in range(1, 4)]
    flip, me = depth_of() // 2, lax.axis_index("seq") >> 1
    while flip:
        high = ((me & flip) != 0).astype(jnp.int32)
        kept = lax.dynamic_slice_in_dim(cells, high * flip, flip, 0)
        sent = lax.dynamic_slice_in_dim(cells, (1 - high) * flip, flip, 0)
        cells = kept.astype(F32) + send_seq(sent.astype(BF16), 2 * flip).astype(F32)
        flip //= 2
    return [cells[0]]


def total_of(got):
    return sum(cells.astype(F32) for cells in got)


def feed_kernel(lifted, cot, gate_w, up_w, mlp_w, mixed, grad_gate, grad_up):
    for r in range(0, lifted.shape[0], 128):
        at = slice(r, r + 128)
        gate = cols_dot(lifted[at, :], gate_w[...])
        up = cols_dot(lifted[at, :], up_w[...])
        grad = cols_dot(cot[at, :], mlp_w[...])
        share = 0.5 + 0.5 * lax.erf(gate * (0.5**0.5))
        slope = share + gate * jnp.exp(-0.5 * gate * gate) * ((0.5 / jnp.pi) ** 0.5)
        gelu = gate * share
        mixed[at, :] = (gelu * up).astype(BF16)
        grad_gate[at, :] = (grad * up * slope).astype(BF16)
        grad_up[at, :] = (grad * gelu).astype(BF16)


def local_kernel(kernel, outs, args, scratch=()):
    spaces = [
        pltpu.SMEM if a.dtype == jnp.int32 and a.size == 2 else pltpu.VMEM for a in args
    ]
    moved = sum(a.size * a.dtype.itemsize for a in args)
    return pl.pallas_call(
        kernel,
        out_shape=outs,
        in_specs=[pl.BlockSpec(memory_space=s) for s in spaces],
        out_specs=[pl.BlockSpec(memory_space=pltpu.VMEM)] * len(outs),
        scratch_shapes=list(scratch),
        compiler_params=pltpu.CompilerParams(vmem_limit_bytes=VMEM_LIMIT),
        cost_estimate=pl.CostEstimate(flops=0, bytes_accessed=moved, transcendentals=0),
    )(*args)


def lane_assemble_kernel(cells, got, where, full):
    for d in range(4):
        z = where[0] ^ d
        mine = pl.multiple_of((2 * z + where[1]) * 128, 128)
        theirs = pl.multiple_of((2 * z + 1 - where[1]) * 128, 128)
        full[:, pl.ds(mine, 128)] = cells[d]
        full[:, pl.ds(theirs, 128)] = got[d]


def lane_split_kernel(full, where, kept, sent):
    for d in range(4):
        z = where[0] ^ d
        mine = pl.multiple_of((2 * z + where[1]) * 128, 128)
        theirs = pl.multiple_of((2 * z + 1 - where[1]) * 128, 128)
        kept[d] = full[:, pl.ds(mine, 128)]
        sent[d] = full[:, pl.ds(theirs, 128)]


def row_assemble_kernel(cells, got, where, full):
    for d in range(4):
        z = where[0] ^ d
        full[2 * z + where[1]] = cells[d]
        full[2 * z + 1 - where[1]] = got[d]


def row_split_kernel(full, where, kept, sent):
    for d in range(4):
        z = where[0] ^ d
        kept[d] = full[2 * z + where[1]]
        sent[d] = full[2 * z + 1 - where[1]]


def turn_kernel(cells, *outs):
    turned = cells[...].astype(F32).T.astype(BF16)
    at = 0
    for out in outs:
        out[...] = turned[at : at + out.shape[0]]
        at += out.shape[0]


def turn_back_kernel(*refs):
    *parts, out, full = refs
    at = 0
    full[...] = jnp.zeros_like(full)
    for i in range(0, len(parts), 4):
        total = parts[i][...].astype(F32)
        for j in range(1, 4):
            total = total + parts[i + j][...].astype(F32)
        full[at : at + total.shape[0], :] = total
        at += total.shape[0]
    out[...] = full[...].T.astype(out.dtype)


def columns_kernel(qkv, mlp, both, gain_a, gain_m, out):
    for g in range(GROUP):
        parts = [
            (qkv[:, p * D + g * OWN : p * D + (g + 1) * OWN].astype(F32) * gain_a[...]).astype(BF16)
            for p in range(3)
        ]
        parts.append(mlp[:, g * OWN_FF : (g + 1) * OWN_FF])
        parts += [
            (both[:, p * FF + g * OWN_FF : p * FF + (g + 1) * OWN_FF].astype(F32) * gain_m[...]).astype(
                BF16
            )
            for p in range(2)
        ]
        parts.append(jnp.zeros((qkv.shape[0], WIDE - 3 * OWN_FF), BF16))
        out[g] = jnp.concatenate(parts, axis=1)


def back_ff_kernel(cells, weight, gain, grad_mlp, grad_in, grad_gain):
    total = jnp.zeros(grad_gain.shape, F32)
    for g in range(GROUP):
        block = cells[g].astype(F32)
        grad_mlp[:, g * OWN_FF : (g + 1) * OWN_FF] = block[:, :OWN_FF]
        for p in range(2):
            raw = block[:, (p + 1) * OWN_FF : (p + 2) * OWN_FF]
            at = slice(p * FF + g * OWN_FF, p * FF + (g + 1) * OWN_FF)
            total = total + jnp.sum(raw * weight[:, at].astype(F32), axis=1, keepdims=True)
            grad_in[:, at] = raw * gain[...]
    grad_gain[...] = total


def back_qkv_kernel(cells, weight, gain, grad, grad_gain):
    total = jnp.zeros(grad_gain.shape, F32)
    for g in range(GROUP):
        block = cells[g].astype(F32)
        for p in range(3):
            raw = block[:, p * OWN : (p + 1) * OWN]
            at = slice(p * D + g * OWN, p * D + (g + 1) * OWN)
            total = total + jnp.sum(raw * weight[:, at].astype(F32), axis=1, keepdims=True)
            grad[:, at] = raw * gain[...]
    grad_gain[...] = total


def columns_of(qkv, mlp, both, gain_a, gain_m):
    rows = qkv.shape[0]
    if direct():
        shape = like((GROUP, rows, 3 * OWN + WIDE), BF16)
        cells = local_kernel(columns_kernel, [shape], (qkv, mlp, both, gain_a, gain_m))[0]
        return cells.reshape(2, 2, rows, -1)

    def columns(w, parts, width):
        cells = w.reshape(rows, parts, 2, 2, width).transpose(2, 3, 0, 1, 4)
        return cells.reshape(2, 2, rows, parts * width)

    return jnp.concatenate(
        [
            columns((qkv.astype(F32) * gain_a).astype(BF16), 3, OWN),
            columns(mlp, 1, OWN_FF),
            columns((both.astype(F32) * gain_m).astype(BF16), 2, OWN_FF),
            jnp.zeros((2, 2, rows, WIDE - 3 * OWN_FF), BF16),
        ],
        axis=-1,
    )


def back_columns(cells, parts, width):
    rows = cells.shape[2]
    cells = cells.reshape(2, 2, rows, parts, width).transpose(2, 3, 0, 1, 4)
    return cells.reshape(rows, parts * GROUP * width).astype(F32)


def back_ff(cells, weight, gain):
    rows = weight.shape[0]
    if direct():
        outs = [like((rows, FF), F32), like((rows, 2 * FF), F32), like((rows, 1), F32)]
        return local_kernel(back_ff_kernel, outs, (cells.reshape(GROUP, rows, WIDE), weight, gain))
    raw = back_columns(cells[..., OWN_FF : 3 * OWN_FF], 2, OWN_FF)
    grad_gain = jnp.sum(raw * weight.astype(F32), axis=1, keepdims=True)
    return back_columns(cells[..., :OWN_FF], 1, OWN_FF), raw * gain, grad_gain


def back_qkv(cells, weight, gain):
    rows = weight.shape[0]
    if direct():
        outs = [like((rows, 3 * D), F32), like((rows, 1), F32)]
        return local_kernel(back_qkv_kernel, outs, (cells.reshape(GROUP, rows, -1), weight, gain))
    raw = back_columns(cells, 3, OWN)
    return raw * gain, jnp.sum(raw * weight.astype(F32), axis=1, keepdims=True)


def x_blocks(cells, got):
    high = (lax.axis_index("seq") & 1) == 1
    blocks = []
    for i in range(cells.shape[0]):
        blocks += [jnp.where(high, got[i], cells[i]), jnp.where(high, cells[i], got[i])]
    return blocks


def x_parts(blocks):
    high = (lax.axis_index("seq") & 1) == 1
    pairs = list(zip(blocks[::2], blocks[1::2]))
    kept = jnp.stack([jnp.where(high, b, a) for a, b in pairs])
    sent = jnp.stack([jnp.where(high, a, b) for a, b in pairs])
    return kept, sent


def assemble(cells, got):
    if direct():
        shape = like((cells.shape[1], D), BF16)
        return local_kernel(lane_assemble_kernel, [shape], (cells, got, place_of_device()))[0]
    return jnp.concatenate(x_blocks(cells, got), axis=-1)


def split(grad):
    count = lax.axis_size("seq")
    size = D // count
    if direct():
        shape = like((4, grad.shape[0], size), BF16)
        return local_kernel(lane_split_kernel, [shape, shape], (grad, place_of_device()))
    return x_parts([grad[:, i * size : (i + 1) * size] for i in range(count)])


def assemble_rows(cells, got):
    if direct():
        shape = like((8,) + cells.shape[1:], BF16)
        return local_kernel(row_assemble_kernel, [shape], (cells, got, place_of_device()))[0]
    return jnp.stack(x_blocks(cells, got))


def split_rows(cells):
    if direct():
        shape = like((4,) + cells.shape[1:], BF16)
        return local_kernel(row_split_kernel, [shape, shape], (cells, place_of_device()))
    return x_parts([cells[i] for i in range(cells.shape[0])])


def turn(cells, sizes):
    if direct():
        return local_kernel(turn_kernel, [like((n, cells.shape[0]), BF16) for n in sizes], (cells,))
    turned, outs, at = cells.T, [], 0
    for n in sizes:
        outs.append(turned[at : at + n])
        at += n
    return outs


def turn_back(chunks, width):
    if direct():
        lanes = chunks[0][0].shape[1]
        return local_kernel(
            turn_back_kernel,
            [like((lanes, width), BF16)],
            tuple(c for chunk in chunks for c in chunk),
            [pltpu.VMEM((width, lanes), F32)],
        )[0]
    turned = jnp.concatenate([total_of(c) for c in chunks], axis=0).T.astype(BF16)
    return jnp.pad(turned, ((0, 0), (0, width - turned.shape[1])))


def place(index, seq_lengths):
    count = seq_lengths.shape[0]
    ids = jnp.arange(count, dtype=jnp.int32)
    ends = jnp.sum(jnp.where(ids[None, :] <= ids[:, None], seq_lengths[None, :], 0), axis=1)
    starts = ends - seq_lengths
    segment = jnp.sum((index[:, None] >= ends[None, :]).astype(jnp.int32), axis=1)
    begins = jnp.sum(jnp.where(segment[:, None] == ids[None, :], starts[None, :], 0), axis=1)
    return segment, index - begins


def angles(position):
    freqs = 10000.0 ** (-(jnp.arange(HDIM // 2, dtype=F32) * 2.0) / HDIM)
    freqs = jnp.concatenate([freqs] * 4)
    turns = position.astype(F32)[:, None] * freqs[None, :]
    sign = jnp.where(jnp.arange(128) % HDIM < HDIM // 2, -1.0, 1.0)
    return jnp.cos(turns), jnp.sin(turns) * sign[None, :]


def normalize(values):
    average = jnp.mean(values, axis=-1, keepdims=True)
    centered = values - average
    variance = jnp.mean(centered * centered, axis=-1, keepdims=True)
    inverse = lax.rsqrt(variance + EPSILON)
    return centered * inverse, inverse


def norm_back(grad_hat, normed, inverse):
    return inverse * (
        grad_hat
        - jnp.mean(grad_hat, axis=-1, keepdims=True)
        - normed * jnp.mean(grad_hat * normed, axis=-1, keepdims=True)
    )


def geglu(gate_in, up_in):
    return jax.nn.gelu(gate_in, approximate=False) * up_in


def contract(left, right, dims, out=F32):
    return lax.dot_general(left, right, ((dims[0], dims[1]), ((), ())), preferred_element_type=out)


def rows_dot(left, right):
    return contract(left, right, ((0,), (0,)))


def cols_dot(left, right):
    return contract(left, right, ((1,), (1,)))


def half_swap(values):
    lane = lax.broadcasted_iota(jnp.int32, values.shape, 1)
    left = pltpu.roll(values, 128 - HDIM // 2, 1)
    right = pltpu.roll(values, HDIM // 2, 1)
    return jnp.where(lane % HDIM < HDIM // 2, left, right)


def bias_of(q_seg, k_seg, block):
    row = lax.broadcasted_iota(jnp.int32, (128, 256), 0)
    col = lax.broadcasted_iota(jnp.int32, (128, 256), 1)
    near = jnp.abs(row + HALF - col) <= HALF
    same = q_seg[pl.ds(block * 128, 128), :] == k_seg[:, pl.ds(block * 128, 256)]
    return jnp.where(near & same, 0.0, MASKED)


def softmax_of(scores):
    exponent = jnp.exp(scores - jnp.max(scores, axis=-1, keepdims=True))
    return exponent * (1.0 / jnp.sum(exponent, axis=-1, keepdims=True))


def attend_kernel(packed, cosine, sine, q_seg, k_seg, query, keys, values, attended, bias):
    rows = query.shape[0]
    blocks = rows // 128
    for b in range(blocks):
        bias[b] = bias_of(q_seg, k_seg, b)
    first = lax.broadcasted_iota(jnp.int32, (1, 128), 1) < HDIM
    for p in range(OWN_HEADS // 2):
        at = slice(p * 128, (p + 1) * 128)
        u = packed[HALF : HALF + rows, at]
        q_cos, q_sin = cosine[HALF : HALF + rows, :], sine[HALF : HALF + rows, :]
        query[:, at] = (u * q_cos + half_swap(u) * q_sin).astype(BF16)
        u = packed[:, OWN + p * 128 : OWN + (p + 1) * 128]
        keys[:, at] = (u * cosine[...] + half_swap(u) * sine[...]).astype(BF16)
        values[:, at] = packed[:, 2 * OWN + p * 128 : 2 * OWN + (p + 1) * 128].astype(BF16)
        for b in range(blocks):
            q = query[b * 128 : (b + 1) * 128, at]
            k = keys[b * 128 : b * 128 + 256, at]
            v = values[b * 128 : b * 128 + 256, at]
            outs = []
            for side in (first, ~first):
                q_one = jnp.where(side, q, jnp.zeros_like(q))
                scores = contract(q_one, k, ((1,), (1,))) * (HDIM**-0.5) + bias[b]
                prob = softmax_of(scores).astype(BF16)
                outs.append(contract(prob, v, ((1,), (0,))))
            attended[b * 128 : (b + 1) * 128, at] = jnp.where(first, outs[0], outs[1]).astype(BF16)


def attend_back_kernel(
    query, keys, values, grad, cosine, sine, q_seg, k_seg, grad_q, grad_k, grad_v, bias
):
    rows = query.shape[0]
    blocks = rows // 128
    scale = HDIM**-0.5
    for b in range(blocks):
        bias[b] = bias_of(q_seg, k_seg, b)
    first = lax.broadcasted_iota(jnp.int32, (1, 128), 1) < HDIM
    grad_k[...] = jnp.zeros_like(grad_k)
    grad_v[...] = jnp.zeros_like(grad_v)
    for p in range(OWN_HEADS // 2):
        at = slice(p * 128, (p + 1) * 128)
        for b in range(blocks):
            here, span = slice(b * 128, (b + 1) * 128), slice(b * 128, b * 128 + 256)
            q, go = query[here, at], grad[here, at]
            k, v = keys[span, at], values[span, at]
            d_q = jnp.zeros((128, 128), F32)
            d_k = jnp.zeros((256, 128), F32)
            d_v = jnp.zeros((256, 128), F32)
            for side in (first, ~first):
                q_one = jnp.where(side, q, jnp.zeros_like(q))
                k_one = jnp.where(side, k, jnp.zeros_like(k))
                go_one = jnp.where(side, go, jnp.zeros_like(go))
                scores = contract(q_one, k, ((1,), (1,))) * scale + bias[b]
                prob = softmax_of(scores)
                grad_prob = contract(go_one, v, ((1,), (1,)))
                inner = jnp.sum(grad_prob * prob, axis=-1, keepdims=True)
                grad_scores = (prob * (grad_prob - inner)).astype(BF16)
                d_q = d_q + contract(grad_scores, k_one, ((1,), (0,)))
                d_k = d_k + contract(grad_scores, q_one, ((0,), (0,)))
                d_v = d_v + contract(prob.astype(BF16), go_one, ((0,), (0,)))
            d_q = d_q * scale
            at_q = slice(HALF + b * 128, HALF + (b + 1) * 128)
            turned = d_q * cosine[at_q, :] - half_swap(d_q) * sine[at_q, :]
            grad_q[here, at] = turned.astype(BF16)
            grad_k[span, at] += d_k * scale
            grad_v[span, at] += d_v
        d_k = grad_k[:, at]
        grad_k[:, at] = d_k * cosine[...] - half_swap(d_k) * sine[...]


def call_kernel(kernel, outs, blocks, flops, args):
    moved = sum(a.size * a.dtype.itemsize for a in args) + sum(
        o.size * o.dtype.itemsize for o in outs
    )
    return pl.pallas_call(
        kernel,
        out_shape=outs,
        in_specs=[pl.BlockSpec(memory_space=pltpu.VMEM)] * len(args),
        out_specs=[pl.BlockSpec(memory_space=pltpu.VMEM)] * len(outs),
        scratch_shapes=[pltpu.VMEM((blocks, 128, 256), F32)],
        compiler_params=pltpu.CompilerParams(vmem_limit_bytes=VMEM_LIMIT),
        cost_estimate=pl.CostEstimate(flops=flops, bytes_accessed=moved, transcendentals=0),
    )(*args)


def like(shape, dtype):
    return jax.ShapeDtypeStruct(shape, dtype)


def on_device(
    tokens, cotangent, seq_lengths, w_qkv, w_attn_out, w_in, w_mlp_out, gain_attn, gain_mlp
):
    share = tokens.shape[0]
    rows = GROUP * share
    seq, seqs = lax.axis_index("seq"), lax.axis_size("seq")
    total = seqs * rows
    shard = w_qkv.shape[0]
    tie = lax.optimization_barrier

    def close(first, last):
        first = tie(first)
        return tie((first, last))


    gain_a = gain_attn.astype(F32)[:, None]
    gain_m = gain_mlp.astype(F32)[:, None]

    last = (lax.axis_index("fy") == 1) & (lax.axis_index("core") == 1)
    meetings = range(GROUP - 1, lax.axis_size(ALL) - 1, GROUP)
    swaps = [(i, i + 1) for i in meetings] + [(i + 1, i) for i in meetings]
    edge = lax.ppermute(jnp.where(last, tokens[share - HALF :], tokens[:HALF]), ALL, swaps)
    attn_z = z_gather(w_attn_out)
    cells = columns_of(w_qkv, w_mlp_out, w_in, gain_a, gain_m)
    cells = trade(trade(cells, "fy", 0), "core", 1).reshape(GROUP * shard, -1)
    qkv, mlp, gate, up = turn(cells, (3 * OWN, OWN_FF, OWN_FF, OWN_FF))
    attn_z, qkv, mlp, gate, up, edge, cotangent_in = tie(
        (attn_z, qkv, mlp, gate, up, edge, cotangent)
    )
    qkv_z = z_gather(qkv)
    attn_x = send_seq(attn_z, 1)
    ours = tokens.astype(F32)
    normed, inverse = normalize(ours)
    hidden = jnp.concatenate([normed, normalize(edge.astype(F32))[0]], axis=0).astype(BF16)
    hidden = join(hidden, "fy", 0)
    cot = join(cotangent_in, "fy", 0)
    (attn_x, hidden, cot, mlp, gate, up), qkv_z = close((attn_x, hidden, cot, mlp, gate, up), qkv_z)
    mlp_z = z_gather(mlp)
    qkv_x = send_seq(qkv_z, 1)
    attn = assemble_rows(attn_z, attn_x).reshape(2, 2, seqs // 4, shard, D)
    hidden = core_rows(hidden).reshape(GROUP, share + HALF, D)
    (qkv_x, attn, hidden, gate), mlp_z = close((qkv_x, attn, hidden, gate), mlp_z)
    gate_z = z_gather(gate)
    mlp_x = send_seq(mlp_z, 1)
    attn = trade(attn, "fy", 0)
    before, after = hidden[0, share:], hidden[GROUP - 1, share:]
    hidden = hidden[:, :share].reshape(rows, D)
    wide = jnp.concatenate([before, hidden, after], axis=0)
    qkv_full = assemble(qkv_z, qkv_x)
    index = seq * rows - HALF + jnp.arange(rows + 2 * HALF, dtype=jnp.int32)
    segment, position = place(jnp.clip(index, 0, total - 1), seq_lengths)
    segment = jnp.where((index >= 0) & (index < total), segment, -1)
    q_seg = segment[HALF : HALF + rows][:, None]
    k_seg = segment[None, :]
    cosine, sine = angles(position)
    packed = cols_dot(wide, qkv_full)
    blocks = rows // 128
    flops = blocks * OWN_HEADS * 128 * 256 * 128 * 4
    query, keys, values, attended = call_kernel(
        attend_kernel,
        [
            like((rows, OWN), BF16),
            like((rows + 2 * HALF, OWN), BF16),
            like((rows + 2 * HALF, OWN), BF16),
            like((rows, OWN), BF16),
        ],
        blocks,
        flops,
        (packed, cosine, sine, q_seg, k_seg),
    )
    (mlp_x, attended, attn, up), gate_z = close((mlp_x, attended, attn, up), gate_z)
    up_z = z_gather(up)
    gate_x = send_seq(gate_z, 1)
    attn_full = trade(attn, "core", 1).transpose(2, 0, 1, 3, 4).reshape(OWN, D)
    part = jnp.dot(attended, attn_full, preferred_element_type=F32)
    middle = ours + group_sum(part, share)
    mlp_full = assemble(mlp_z, mlp_x)
    (gate_x, middle, mlp_full), up_z = close((gate_x, middle, mlp_full), up_z)
    up_x = send_seq(up_z, 1)
    normed_mid, inverse_mid = normalize(middle)
    lifted = join(normed_mid.astype(BF16), "fy", 0)
    gate_full = assemble(gate_z, gate_x)
    up_x, lifted, gate_full = tie((up_x, lifted, gate_full))
    lifted, cot = tie((core_rows(lifted), core_rows(cot)))
    up_full = assemble(up_z, up_x)
    shape = like((rows, OWN_FF), BF16)
    mixed, grad_gate, grad_up = local_kernel(
        feed_kernel, [shape] * 3, (lifted, cot, gate_full, up_full, mlp_full)
    )

    mlp_kept, mlp_sent = split(rows_dot(mixed, cot).astype(BF16))
    mlp_kept, mlp_sent, grad_gate, grad_up = tie((mlp_kept, mlp_sent, grad_gate, grad_up))
    mlp_x = send_seq(mlp_sent, 1)
    part_lifted = jnp.dot(grad_gate, gate_full, preferred_element_type=F32) + jnp.dot(
        grad_up, up_full, preferred_element_type=F32
    )
    half_hat = reduce_pair(part_lifted.reshape(2, 2, share, D), "core", 1)
    half_hat, grad_gate, grad_up = tie((half_hat, grad_gate, grad_up))
    grad_hat = reduce_pair(half_hat, "fy", 0)
    gate_kept, gate_sent = split(rows_dot(grad_gate, lifted).astype(BF16))
    up_kept, up_sent = split(rows_dot(grad_up, lifted).astype(BF16))
    mlp_x, gate_sent, up_sent, grad_hat = tie((mlp_x, gate_sent, up_sent, grad_hat))
    mlp_got = z_spread(x_sum(mlp_kept, mlp_x))
    gate_x = send_seq(gate_sent, 1)
    grad_middle = cotangent.astype(F32) + norm_back(grad_hat, normed_mid, inverse_mid)
    grad_attn = join(grad_middle.astype(BF16), "fy", 0)
    (gate_x, grad_attn, attended), mlp_got = close((gate_x, grad_attn, attended), mlp_got)
    gate_got = z_spread(x_sum(gate_kept, gate_x))
    up_x = send_seq(up_sent, 1)
    grad_attn = core_rows(grad_attn)
    grad_attended = cols_dot(grad_attn, attn_full).astype(BF16)
    grad_q, grad_k, grad_v = call_kernel(
        attend_back_kernel,
        [
            like((rows, OWN), BF16),
            like((rows + 2 * HALF, OWN), F32),
            like((rows + 2 * HALF, OWN), F32),
        ],
        blocks,
        flops * 3,
        (query, keys, values, grad_attended, cosine, sine, q_seg, k_seg),
    )
    grad_kv = jnp.concatenate([grad_k, grad_v], axis=1)
    attn_g = rows_dot(attended, grad_attn).astype(BF16)
    attn_g = attn_g.reshape(seqs // 4, 2, 2, shard, D).transpose(1, 2, 0, 3, 4)
    attn_g = trade(attn_g, "core", 1)
    part_out = jnp.dot(mixed, mlp_full, preferred_element_type=F32)
    (up_x, grad_kv, attn_g, part_out), gate_got = close((up_x, grad_kv, attn_g, part_out), gate_got)
    ahead = [(i, i + 1) for i in range(seqs - 1)]
    behind = [(i + 1, i) for i in range(seqs - 1)]
    low_edge = lax.ppermute(grad_kv[:HALF].astype(BF16), "seq", behind)
    high_edge = lax.ppermute(grad_kv[HALF + rows :].astype(BF16), "seq", ahead)
    attn_g = trade(attn_g, "fy", 0).reshape(seqs, shard, D)
    low_edge, high_edge, up_x = tie((low_edge, high_edge, up_x))
    middle_kv = grad_kv[HALF : HALF + rows]
    gap = jnp.zeros((rows - 2 * HALF, 2 * OWN), F32)
    edges = jnp.concatenate([high_edge.astype(F32), gap, low_edge.astype(F32)], axis=0)
    grad_packed = jnp.concatenate([grad_q, (middle_kv + edges).astype(BF16)], axis=1)
    qkv_kept, qkv_sent = split(rows_dot(grad_packed, hidden).astype(BF16))
    half_out = reduce_pair(part_out.reshape(2, 2, share, D), "core", 1)
    attn_g, qkv_sent, grad_packed, up_x, half_out = tie(
        (attn_g, qkv_sent, grad_packed, up_x, half_out)
    )
    qkv_x = send_seq(qkv_sent, 1)
    up_got = z_spread(x_sum(up_kept, up_x))
    attn_kept, attn_sent = split_rows(attn_g)
    part_hidden = jnp.dot(grad_packed, qkv_full, preferred_element_type=F32)
    sum_out = reduce_pair(half_out, "fy", 0)
    (qkv_x, part_hidden, sum_out, attn_sent), up_got = close(
        (qkv_x, part_hidden, sum_out, attn_sent), up_got
    )
    qkv_got = z_spread(x_sum(qkv_kept, qkv_x))
    attn_x = send_seq(attn_sent, 1)

    rest_g = turn_back([mlp_got, gate_got, up_got], WIDE).reshape(2, 2, shard, -1)
    rest_g = trade(trade(rest_g, "fy", 0), "core", 1)
    grad_mlp_out, grad_w_in, grad_gain_mlp = back_ff(rest_g, w_in, gain_m)
    grad_hidden = group_sum(part_hidden, share)
    output = (middle + sum_out).astype(BF16)
    input_grad = grad_middle + norm_back(grad_hidden, normed, inverse)
    attn_x, qkv_got, output, input_grad, grad_mlp_out, grad_w_in, grad_gain_mlp = tie(
        (attn_x, qkv_got, output, input_grad, grad_mlp_out, grad_w_in, grad_gain_mlp)
    )
    attn_got = z_spread(x_sum(attn_kept, attn_x))
    qkv_g = turn_back([qkv_got], 3 * OWN).reshape(2, 2, shard, -1)
    qkv_g = trade(trade(qkv_g, "fy", 0), "core", 1)
    grad_w_qkv, grad_gain_attn = back_qkv(qkv_g, w_qkv, gain_a)
    grad_attn_out = total_of(attn_got)
    return (
        output,
        input_grad,
        grad_w_qkv,
        grad_attn_out,
        grad_w_in,
        grad_mlp_out,
        grad_gain_attn[:, 0],
        grad_gain_mlp[:, 0],
    )


def solution(mesh):
    split = Mesh(mesh.devices.reshape(mesh.shape["seq"], -1, 2), ALL)
    two, one = P(ALL, None), P(ALL)
    return jax.shard_map(
        on_device,
        mesh=split,
        in_specs=(two, two, P(), two, two, two, two, one, one),
        out_specs=(two, two, two, two, two, two, one, one),
        check_vma=False,
    )
```
